128 devices in a mesh: section: 8 (over z, core), head: 16 (over y, x).
Axes of the slice: x: 4, y: 4, z: 4, core: 2. Of those that a mesh axis runs over, the one named last changes fastest.
Arguments:
- hidden_in: bfloat16 [24576, 2048], P(('section', 'head')), may hold values from -3 to 3
- norm_gain: float32 [2048], replicated, may hold values from 0.1 to 1.9
- w_qkv: bfloat16 [2048, 3, 2048], P(None, None, 'head'), may hold values from -0.5 to 0.5
- w_out: bfloat16 [2048, 2048], P('head'), may hold values from -0.375 to 0.375
- block_lists: int32 [48, 12], P('section'), may hold values from -1 to 47, as said below
Outputs:
- mixed: bfloat16 [24576, 2048], P(('section', 'head'))
The draws below stay inside these ranges and needn't reach their ends.
Inputs may be any that keep to these rules, and one draw needn't show every extreme that they name: `block_lists`: row b starts with b itself, then holds 1 + b * 11 // 47 - 1 further distinct blocks below b, then -1 in every remaining slot.
All inputs are finite; a program needn't handle non-finite values.
Results may differ from the reference program's by a relative error of at most 0.015.
Values may be sent and summed in bfloat16 or wider, within the bound.
A program may use at most 128 MiB of HBM per device.

```python
import math
import jax
import jax.numpy as jnp
from jax import lax

D = 2048
HEADS = 16
HD = 128
BLK = 512
KSEL = 12
NBLK = 48
SEQ = 24576


def draw_hidden_in(key, part):
    base = 0.5 * jax.random.normal(key, (SEQ, D), jnp.float32)
    return jnp.clip(base, -3.0, 3.0).astype(jnp.bfloat16)


def draw_w_qkv(key, part):
    scale = D ** (-0.5)
    base = jax.random.normal(key, (D, 3, HEADS * HD), jnp.float32) * scale
    return jnp.clip(base, -0.5, 0.5).astype(jnp.bfloat16)


def draw_block_lists(key, part):
    blocks = jnp.arange(NBLK, dtype=jnp.int32)
    counts = 1 + blocks * (KSEL - 1) // (NBLK - 1)
    scores = jax.random.randint(key, (NBLK, NBLK), 0, 2 ** 20, dtype=jnp.int32) * NBLK + blocks[None, :]
    scores = jnp.where(blocks[None, :] < blocks[:, None], scores, -1 - blocks[None, :])
    _, picks = lax.top_k(scores, KSEL - 1)
    entries = jnp.concatenate([blocks[:, None], picks.astype(jnp.int32)], axis=1)
    slots = jnp.arange(KSEL, dtype=jnp.int32)
    return jnp.where(slots[None, :] < counts[:, None], entries, -1).astype(jnp.int32)


def level_of(rng, shape, pieces, smallest, top_value):
    def one(position, parts):
        heights = jax.random.uniform(jax.random.fold_in(jax.random.fold_in(rng, 6), position), (parts,), jnp.float32, smallest / len(pieces), top_value / len(pieces))
        return jnp.repeat(jnp.exp(heights), shape[position] // parts).reshape((-1,) + (1,) * (len(shape) - position - 1))

    loudness = one(*pieces[0])
    for cut in pieces[1:]:
        loudness = loudness * one(*cut)
    return loudness


def scatter_about(key, extent, width, most, pieces=(), kind=jnp.bfloat16):
    loudness = level_of(key, extent, pieces, -0.22, 0.18) if pieces else 1.0
    values = jax.random.normal(key, extent, jnp.float32) * width * loudness
    return jnp.minimum(jnp.maximum(values, -most), most).astype(kind)


def setup_inputs(seed: int = 0) -> dict:
    seeds = jax.random.split(jax.random.key(seed), 6)
    hidden_in = draw_hidden_in(jax.random.fold_in(seeds[5], 71), 0)
    norm_gain = jnp.clip(1.0 + 0.18 * jax.random.normal(seeds[1], (D,), jnp.float32), 0.1, 1.9)
    w_qkv = draw_w_qkv(jax.random.fold_in(seeds[5], 71), 0)
    w_out = scatter_about(seeds[3], (HEADS * HD, D), (HEADS * HD // 9) ** -0.5, 0.375, ((0, 16),))
    block_lists = draw_block_lists(jax.random.fold_in(seeds[5], 71), 0)
    return {"hidden_in": hidden_in, "norm_gain": norm_gain, "w_qkv": w_qkv, "w_out": w_out, "block_lists": block_lists}


EPS = 1e-05
THETA = 10000.0

def rope_tables(positions):
    half = HD // 2
    frequency = THETA ** (-(2.0 * jnp.arange(half, dtype=jnp.float32)) / HD)
    angle = positions.astype(jnp.float32)[:, None] * frequency[None, :]
    return (jnp.cos(angle)[:, None, :], jnp.sin(angle)[:, None, :])

def rotate(vectors, cosine, sine):
    half = vectors.shape[-1] // 2
    first = vectors[..., :half]
    second = vectors[..., half:]
    return jnp.concatenate([first * cosine - second * sine, second * cosine + first * sine], axis=-1)

def reference(hidden_in, norm_gain, w_qkv, w_out, block_lists):
    resid = hidden_in.astype(jnp.float32)
    normed = (resid * lax.rsqrt(lax.optimization_barrier(jnp.mean(resid * resid, axis=-1, keepdims=True)) + EPS) * norm_gain).astype(jnp.bfloat16)
    projected = jnp.dot(normed, w_qkv.reshape(D, 3 * HEADS * HD), preferred_element_type=jnp.float32)
    projected = projected.reshape(SEQ, 3, HEADS, HD)
    cosine, sine = rope_tables(jnp.arange(SEQ, dtype=jnp.int32))
    query = rotate(projected[:, 0], cosine, sine).astype(jnp.bfloat16)
    keys = rotate(projected[:, 1], cosine, sine).astype(jnp.bfloat16)
    values = projected[:, 2].astype(jnp.bfloat16)
    scale = 1.0 / math.sqrt(HD)

    def one_block(block):
        query_rows = lax.dynamic_slice_in_dim(query, block * BLK, BLK, 0).astype(jnp.float32)
        block_row = lax.dynamic_index_in_dim(block_lists, block, 0, keepdims=False)
        safe = jnp.maximum(block_row, 0)
        key_positions = (safe[:, None] * BLK + jnp.arange(BLK, dtype=jnp.int32)[None, :]).reshape(-1).astype(jnp.int32)
        key_rows = keys[key_positions].astype(jnp.float32)
        value_rows = values[key_positions].astype(jnp.float32)
        scores = jnp.einsum('qhd,khd->hqk', query_rows, key_rows) * scale
        query_positions = block * BLK + jnp.arange(BLK, dtype=jnp.int32)
        live = jnp.repeat(block_row >= 0, BLK)
        allowed = live[None, :] & (key_positions[None, :] <= query_positions[:, None])
        scores = jnp.where(allowed[None], scores, -jnp.inf)
        highest = lax.optimization_barrier(jnp.max(scores, axis=-1, keepdims=True))
        weights = jnp.exp(scores - highest)
        total = lax.optimization_barrier(jnp.sum(weights, axis=-1, keepdims=True))
        rounded = lax.optimization_barrier(weights.astype(jnp.bfloat16)).astype(jnp.float32)
        summed = jnp.einsum('hqk,khd->hqd', rounded, value_rows) / total
        return jnp.transpose(summed, (1, 0, 2)).reshape(BLK, HEADS * HD).astype(jnp.bfloat16)
    attended = lax.map(one_block, jnp.arange(NBLK, dtype=jnp.int32)).reshape(SEQ, HEADS * HD)
    output = resid + jnp.dot(attended, w_out, preferred_element_type=jnp.float32)
    return output.astype(jnp.bfloat16)
```

```python
import functools
import math

import jax
import jax.numpy as jnp
from jax import lax
from jax.experimental import pallas as pl
from jax.experimental.pallas import tpu as pltpu
from jax.sharding import PartitionSpec as P

D = 2048
HD = 128
BLK = 512
KSEL = 12


EPS = 1e-05
THETA = 10000.0
QSCALE = math.log2(math.e) / math.sqrt(HD)
ROWS = 256


def rotate(vectors, cosine, sine):
    half = vectors.shape[-1] // 2
    first = vectors[..., :half]
    second = vectors[..., half:]
    return jnp.concatenate(
        [first * cosine - second * sine, second * cosine + first * sine], axis=-1
    )


def attention_kernel(lists, q_ref, kv_hbm, o_ref, kv_buf, m_ref, acc_ref, sems):
    blocks = q_ref.shape[0] // BLK

    def live(block):
        count = jnp.int32(0)
        for slot in range(KSEL):
            count += (lists[block, slot] >= 0).astype(jnp.int32)
        return count

    def fetch(block, slot):
        source = jnp.maximum(lists[block, slot], 0)
        start = pl.multiple_of(source * BLK, BLK)
        return pltpu.make_async_copy(
            kv_hbm.at[pl.ds(start, BLK), :],
            kv_buf.at[block % 2, slot],
            sems.at[block % 2, slot],
        )

    def fetch_all(block):
        def one(slot, carry):
            fetch(block, slot).start()
            return carry

        lax.fori_loop(0, live(block), one, 0)

    ones = jnp.ones((BLK, HD), jnp.bfloat16)
    fetch_all(0)

    def one_block(block, carry):
        @pl.when(block + 1 < blocks)
        def _():
            fetch_all(block + 1)

        base = pl.multiple_of(block * BLK, BLK)

        def tile(slot, first):
            keys = kv_buf[block % 2, slot, :, :HD]
            values = jnp.concatenate([kv_buf[block % 2, slot, :, HD:], ones], axis=1)
            for part in range(BLK // ROWS):
                rows = pl.ds(part * ROWS, ROWS)
                query = q_ref[pl.ds(pl.multiple_of(base + part * ROWS, ROWS), ROWS), :]
                scores = lax.dot_general(
                    query, keys, (((1,), (1,)), ((), ())), preferred_element_type=jnp.float32
                )
                if first:
                    row = lax.broadcasted_iota(jnp.int32, (ROWS, BLK), 0) + part * ROWS
                    col = lax.broadcasted_iota(jnp.int32, (ROWS, BLK), 1)
                    scores = jnp.where(col <= row, scores, -jnp.inf)
                peak = jnp.max(scores, axis=1, keepdims=True)
                if not first:
                    old = m_ref[rows, :1]
                    peak = jnp.maximum(peak, old)
                weights = jnp.exp2(scores - peak).astype(jnp.bfloat16)
                update = jnp.dot(weights, values, preferred_element_type=jnp.float32)
                if first:
                    acc_ref[rows, :] = update
                else:
                    acc_ref[rows, :] = acc_ref[rows, :] * jnp.exp2(old - peak) + update
                m_ref[rows, :] = jnp.broadcast_to(peak, (ROWS, HD))

        fetch(block, 0).wait()
        tile(0, True)

        def one_slot(slot, inner):
            fetch(block, slot).wait()
            tile(slot, False)
            return inner

        lax.fori_loop(1, live(block), one_slot, 0)
        for part in range(BLK // ROWS):
            rows = pl.ds(part * ROWS, ROWS)
            o_ref[pl.ds(pl.multiple_of(base + part * ROWS, ROWS), ROWS), :] = (
                acc_ref[rows, :HD] / acc_ref[rows, HD:]
            ).astype(jnp.bfloat16)
        return carry

    lax.fori_loop(0, blocks, one_block, 0)


def attention(lists, query, kv_all):
    return pl.pallas_call(
        attention_kernel,
        out_shape=jax.ShapeDtypeStruct(query.shape, jnp.bfloat16),
        in_specs=[
            pl.BlockSpec(memory_space=pltpu.SMEM),
            pl.BlockSpec(memory_space=pltpu.VMEM),
            pl.BlockSpec(memory_space=pl.ANY),
        ],
        out_specs=pl.BlockSpec(memory_space=pltpu.VMEM),
        scratch_shapes=[
            pltpu.VMEM((2, KSEL, BLK, 2 * HD), jnp.bfloat16),
            pltpu.VMEM((BLK, HD), jnp.float32),
            pltpu.VMEM((BLK, 2 * HD), jnp.float32),
            pltpu.SemaphoreType.DMA((2, KSEL)),
        ],
        compiler_params=pltpu.CompilerParams(vmem_limit_bytes=48 << 20),
        name="block_attention",
    )(lists, query, kv_all)


def local(hidden_in, norm_gain, w_qkv, w_out, block_lists):
    section_id = lax.axis_index("section")
    width = w_qkv.shape[2]
    blocks_here = block_lists.shape[0]
    tok_dev = blocks_here * BLK
    resid = hidden_in.astype(jnp.float32)
    normed = (
        resid * lax.rsqrt(jnp.mean(resid * resid, axis=-1, keepdims=True) + EPS) * norm_gain
    ).astype(jnp.bfloat16)
    flat_weight = w_qkv.reshape(D, 3 * width)
    frequency = THETA ** (-(2.0 * jnp.arange(HD // 2, dtype=jnp.float32)) / HD)
    piece = lax.all_gather(normed, "head", axis=0, tiled=True)
    count = piece.shape[0]
    rows = jnp.dot(piece, flat_weight, preferred_element_type=jnp.float32)
    positions = (section_id * tok_dev + jnp.arange(count, dtype=jnp.int32)).astype(jnp.float32)
    angle = positions[:, None] * frequency[None, :]
    cosine = jnp.cos(angle)
    sine = jnp.sin(angle)
    query = (rotate(rows[:, :HD], cosine, sine) * QSCALE).astype(jnp.bfloat16)
    key_value = jnp.concatenate(
        [rotate(rows[:, HD : 2 * HD], cosine, sine), rows[:, 2 * HD :]], axis=1
    ).astype(jnp.bfloat16)
    kv_all = lax.all_gather(key_value, "section", axis=0, tiled=True)
    attended = attention(block_lists, query, kv_all)
    regrouped = lax.all_to_all(attended, "head", split_axis=0, concat_axis=1, tiled=True)
    summed = jnp.dot(
        regrouped,
        lax.all_gather(w_out, "head", axis=0, tiled=True),
        preferred_element_type=jnp.float32,
    )
    return (resid + summed).astype(jnp.bfloat16)


def solution(mesh):
    placed = (
        P(("section", "head"), None),
        P(),
        P(None, None, "head"),
        P("head", None),
        P("section", None),
    )
    return jax.shard_map(
        local, mesh=mesh, in_specs=placed, out_specs=P(("section", "head"), None), check_vma=False
    )
```

```python
import math

import jax
import jax.numpy as jnp
from jax import lax
from jax.experimental import pallas as pl
from jax.experimental.pallas import tpu as pltpu
from jax.sharding import PartitionSpec as P

D = 2048
HD = 128
BLK = 512
KSEL = 12
NBLK = 48
SECTIONS = 8
HEADS = 16

EPS = 1e-05
THETA = 10000.0
QSCALE = math.log2(math.e) / math.sqrt(HD)
ROWS = 256

PIECE = 192
HALF = PIECE // 2
UNIT = HALF // 2
TOK = PIECE * HEADS
LAST = HEADS // 2
MESH = pl.DeviceIdType.MESH


def layer_kernel(
    lists, xn, w_ref, cos_b, sin_b, cos_r, sin_r, o_ref,
    x_all, kv_all, q_ref, m_ref, acc_ref,
    ring_send, ring_recv, z_send, z_recv, s_send, s_recv,
):
    section = lax.axis_index("section")
    head = lax.axis_index("head")
    ypos, xpos = head // 4, head % 4
    diagonal = (xpos + ypos) % 4
    spot = (4 * ypos + diagonal, 4 * xpos + diagonal)

    def head_of(ring, place):
        place = (place + 2 * HEADS) % HEADS
        slow, fast = place // 4, place % 4
        other = (fast - slow + 4) % 4
        return slow * 4 + other if ring == 0 else other * 4 + slow

    def ring_device(ring, way):
        return {"section": section, "head": head_of(ring, spot[ring] + (1 if way == 0 else -1))}

    ring_to = [[ring_device(ring, way) for way in range(2)] for ring in range(2)]
    z_up = {"section": (section + 2) % SECTIONS, "head": head}
    z_down = {"section": (section + SECTIONS - 2) % SECTIONS, "head": head}
    partner = {"section": section + 1 - 2 * (section % 2), "head": head}

    barrier = pltpu.get_barrier_semaphore()
    for device in (*ring_to[0], *ring_to[1], z_up, z_down, partner):
        pl.semaphore_signal(barrier, inc=1, device_id=device, device_id_type=MESH)
    pl.semaphore_wait(barrier, 7)

    def rows_of(start, size):
        return pl.ds(pl.multiple_of(start, 16), size)

    def send(source, target, send_sem, recv_sem, device):
        pltpu.make_async_remote_copy(
            src_ref=source,
            dst_ref=target,
            send_sem=send_sem,
            recv_sem=recv_sem,
            device_id=device,
            device_id_type=MESH,
        ).start()

    def arrived(ref, rows, sem):
        view = ref.at[pl.ds(0, rows), :]
        pltpu.make_async_copy(view, view, sem).wait()

    def origin(ring, way, step):
        return head_of(ring, spot[ring] + (step if way == 1 else -step))

    def unit_rows(ring, source, unit):
        return rows_of(source * PIECE + ring * HALF + unit * UNIT, UNIT)

    def pass_on(ring, way, unit, step, source):
        rows = unit_rows(ring, source, unit)
        send(
            x_all.at[rows, :],
            x_all.at[rows, :],
            ring_send,
            ring_recv.at[ring, way, unit, step + 1],
            ring_to[ring][way],
        )

    def starts_of(step):
        if isinstance(step, int) and step == 0:
            return [(head, 0), (head, 1)]
        if isinstance(step, int) and step == LAST:
            return [(origin(ring, 0, LAST), ring) for ring in range(2)]
        return [(origin(ring, way, step), ring) for ring in range(2) for way in range(2)]

    def project(tokens, pieces):
        result = jnp.dot(tokens, w_ref[...], preferred_element_type=jnp.float32)
        for index, (source, ring) in enumerate(pieces):
            part = result[index * HALF : (index + 1) * HALF]
            base_cos, base_sin = cos_b[pl.ds(source, 1), :], sin_b[pl.ds(source, 1), :]
            row_cos = cos_r[ring * HALF : (ring + 1) * HALF, :]
            row_sin = sin_r[ring * HALF : (ring + 1) * HALF, :]
            cosine = base_cos * row_cos - base_sin * row_sin
            sine = base_sin * row_cos + base_cos * row_sin
            query, key, value = part[:, :HD], part[:, HD : 2 * HD], part[:, 2 * HD :]
            query = (query * cosine + pltpu.roll(query, HD // 2, 1) * sine) * QSCALE
            key = key * cosine + pltpu.roll(key, HD // 2, 1) * sine
            start = source * PIECE + ring * HALF
            q_ref[rows_of(start, HALF), :] = query.astype(jnp.bfloat16)
            own = rows_of(section * TOK + start, HALF)
            kv_all[own, :HD] = key.astype(jnp.bfloat16)
            kv_all[own, HD:] = value.astype(jnp.bfloat16)

    def kv_copy(region, start, size, send_sem, recv_sem, device):
        rows = rows_of(region * TOK + start, size)
        send(kv_all.at[rows, :], kv_all.at[rows, :], send_sem, recv_sem, device)

    def share(step, pieces):
        for source, ring in pieces:
            start = source * PIECE + ring * HALF
            kv_copy(section, start, HALF, z_send, z_recv.at[0, step], z_up)
            kv_copy(section, start, HALF, z_send, z_recv.at[1, step], z_down)
            kv_copy(section, start, HALF, s_send, s_recv.at[step], partner)

    def relay_near(step, pieces):
        below, above = (section + SECTIONS - 2) % SECTIONS, (section + 2) % SECTIONS
        arrived(kv_all, len(pieces) * HALF, z_recv.at[0, step])
        for source, ring in pieces:
            start = source * PIECE + ring * HALF
            kv_copy(below, start, UNIT, z_send, z_recv.at[2, step], z_up)
            kv_copy(below, start, HALF, s_send, s_recv.at[step], partner)
        arrived(kv_all, len(pieces) * HALF, z_recv.at[1, step])
        for source, ring in pieces:
            start = source * PIECE + ring * HALF
            kv_copy(above, start + UNIT, UNIT, z_send, z_recv.at[3, step], z_down)
            kv_copy(above, start, HALF, s_send, s_recv.at[step], partner)

    def relay_far(step, pieces):
        across = (section + 4) % SECTIONS
        arrived(kv_all, len(pieces) * UNIT, z_recv.at[2, step])
        arrived(kv_all, len(pieces) * UNIT, z_recv.at[3, step])
        for source, ring in pieces:
            start = source * PIECE + ring * HALF
            kv_copy(across, start, HALF, s_send, s_recv.at[step], partner)

    for unit in range(2):
        for ring in range(2):
            for way in range(2):
                send(
                    xn.at[pl.ds(ring * HALF + unit * UNIT, UNIT), :],
                    x_all.at[unit_rows(ring, head, unit), :],
                    ring_send,
                    ring_recv.at[ring, way, unit, 1],
                    ring_to[ring][way],
                )
    project(xn[...], starts_of(0))
    share(0, starts_of(0))
    relay_near(0, starts_of(0))

    def one_step(step, carry):
        for unit in range(2):
            for ring in range(2):
                for way in range(2):
                    arrived(x_all, UNIT, ring_recv.at[ring, way, unit, step])
                    source = origin(ring, way, step)
                    if way == unit:
                        pass_on(ring, way, unit, step, source)
                    else:

                        @pl.when(step < LAST - 1)
                        def _(ring=ring, way=way, unit=unit, source=source):
                            pass_on(ring, way, unit, step, source)

        pieces = starts_of(step)
        tokens = jnp.concatenate(
            [x_all[rows_of(source * PIECE + ring * HALF, HALF), :] for source, ring in pieces],
            axis=0,
        )
        project(tokens, pieces)

        @pl.when(step >= 2)
        def _():
            relay_near(step - 1, starts_of(step - 1))

        @pl.when(step >= 3)
        def _():
            relay_far(step - 2, starts_of(step - 2))

        share(step, pieces)
        return carry

    lax.fori_loop(1, LAST, one_step, 0)
    relay_far(0, starts_of(0))
    for ring in range(2):
        for way in range(2):
            arrived(x_all, UNIT, ring_recv.at[ring, way, way, LAST])
    pieces = starts_of(LAST)
    tokens = jnp.concatenate(
        [x_all[rows_of(source * PIECE + ring * HALF, HALF), :] for source, ring in pieces], axis=0
    )
    project(tokens, pieces)
    relay_near(LAST - 1, starts_of(LAST - 1))
    relay_far(LAST - 2, starts_of(LAST - 2))
    share(LAST, pieces)
    relay_far(LAST - 1, starts_of(LAST - 1))
    relay_near(LAST, pieces)
    relay_far(LAST, pieces)
    for step in range(LAST + 1):
        arrived(kv_all, 4 * HALF * (2 if step in (0, LAST) else 4), s_recv.at[step])

    blocks = TOK // BLK
    ones = jnp.ones((BLK, HD), jnp.bfloat16)

    def one_block(block, carry):
        base = pl.multiple_of(block * BLK, BLK)
        count = 1 + ((section * blocks + block) * (KSEL - 1)) // (NBLK - 1)

        def tile(source, first):
            keys = kv_all[pl.ds(source * BLK, BLK), :HD]
            values = jnp.concatenate([kv_all[pl.ds(source * BLK, BLK), HD:], ones], axis=1)
            for part in range(BLK // ROWS):
                rows = pl.ds(part * ROWS, ROWS)
                query = q_ref[pl.ds(pl.multiple_of(base + part * ROWS, ROWS), ROWS), :]
                scores = lax.dot_general(
                    query, keys, (((1,), (1,)), ((), ())), preferred_element_type=jnp.float32
                )
                if first:
                    row = lax.broadcasted_iota(jnp.int32, (ROWS, BLK), 0) + part * ROWS
                    col = lax.broadcasted_iota(jnp.int32, (ROWS, BLK), 1)
                    scores = jnp.where(col <= row, scores, -jnp.inf)
                peak = jnp.max(scores, axis=1, keepdims=True)
                if not first:
                    old = m_ref[rows, :1]
                    peak = jnp.maximum(peak, old)
                weights = jnp.exp2(scores - peak).astype(jnp.bfloat16)
                update = jnp.dot(weights, values, preferred_element_type=jnp.float32)
                if first:
                    acc_ref[rows, :] = update
                else:
                    acc_ref[rows, :] = acc_ref[rows, :] * jnp.exp2(old - peak) + update
                m_ref[rows, :] = jnp.broadcast_to(peak, (ROWS, HD))

        tile(section * blocks + block, True)

        def one_slot(slot, inner):
            tile(lists[block, slot], False)
            return inner

        lax.fori_loop(1, count, one_slot, 0)
        for part in range(BLK // ROWS):
            rows = pl.ds(part * ROWS, ROWS)
            o_ref[pl.ds(pl.multiple_of(base + part * ROWS, ROWS), ROWS), :] = (
                acc_ref[rows, :HD] / acc_ref[rows, HD:]
            ).astype(jnp.bfloat16)
        return carry

    lax.fori_loop(0, blocks, one_block, 0)

    arrived(x_all, 4 * (2 * LAST - 1) * UNIT, ring_send)
    arrived(kv_all, 3 * TOK, z_send)
    arrived(kv_all, 4 * TOK, s_send)


def attend(lists, normed, weight, tables):
    vmem = pl.BlockSpec(memory_space=pltpu.VMEM)
    return pl.pallas_call(
        layer_kernel,
        out_shape=jax.ShapeDtypeStruct((TOK, HD), jnp.bfloat16),
        in_specs=[pl.BlockSpec(memory_space=pltpu.SMEM)] + [vmem] * 6,
        out_specs=vmem,
        scratch_shapes=[
            pltpu.VMEM((TOK, D), jnp.bfloat16),
            pltpu.VMEM((SECTIONS * TOK, 2 * HD), jnp.bfloat16),
            pltpu.VMEM((TOK, HD), jnp.bfloat16),
            pltpu.VMEM((BLK, HD), jnp.float32),
            pltpu.VMEM((BLK, 2 * HD), jnp.float32),
            pltpu.SemaphoreType.DMA,
            pltpu.SemaphoreType.DMA((2, 2, 2, LAST + 1)),
            pltpu.SemaphoreType.DMA,
            pltpu.SemaphoreType.DMA((4, LAST + 1)),
            pltpu.SemaphoreType.DMA,
            pltpu.SemaphoreType.DMA((LAST + 1,)),
        ],
        compiler_params=pltpu.CompilerParams(
            collective_id=0, has_side_effects=True, vmem_limit_bytes=56 << 20
        ),
        name="layer",
    )(lists, normed, weight, *tables)


def rotary_tables(positions):
    frequency = THETA ** (-(2.0 * jnp.arange(HD // 2, dtype=jnp.float32)) / HD)
    angle = positions.astype(jnp.float32)[:, None] * frequency[None, :]
    cosine, sine = jnp.cos(angle), jnp.sin(angle)
    return jnp.concatenate([cosine, cosine], axis=1), jnp.concatenate([-sine, sine], axis=1)


def local(hidden_in, norm_gain, w_qkv, w_out, block_lists):
    section_id = lax.axis_index("section")
    resid = hidden_in.astype(jnp.float32)
    normed = (
        resid * lax.rsqrt(jnp.mean(resid * resid, axis=-1, keepdims=True) + EPS) * norm_gain
    ).astype(jnp.bfloat16)
    flat_weight = w_qkv.reshape(D, 3 * HD)
    bases = section_id * TOK + PIECE * jnp.arange(HEADS, dtype=jnp.int32)
    cos_b, sin_b = rotary_tables(bases)
    cos_r, sin_r = rotary_tables(jnp.arange(PIECE, dtype=jnp.int32))
    attended = attend(block_lists, normed, flat_weight, (cos_b, sin_b, cos_r, sin_r))
    regrouped = lax.all_to_all(attended, "head", split_axis=0, concat_axis=1, tiled=True)
    summed = jnp.dot(
        regrouped,
        lax.all_gather(w_out, "head", axis=0, tiled=True),
        preferred_element_type=jnp.float32,
    )
    return (resid + summed).astype(jnp.bfloat16)


def solution(mesh):
    placed = (
        P(("section", "head"), None),
        P(),
        P(None, None, "head"),
        P("head", None),
        P("section", None),
    )
    return jax.shard_map(
        local, mesh=mesh, in_specs=placed, out_specs=P(("section", "head"), None), check_vma=False
    )
```

```python
import math

import jax
import jax.numpy as jnp
from jax import lax
from jax.experimental import pallas as pl
from jax.experimental.pallas import tpu as pltpu
from jax.sharding import PartitionSpec as P

D = 2048
HD = 128
BLK = 512
KSEL = 12
NBLK = 48
SECTIONS = 8
HEADS = 16

EPS = 1e-05
THETA = 10000.0
QSCALE = math.log2(math.e) / math.sqrt(HD)
ROWS = 256

PIECE = 192
HALF = PIECE // 2
UNIT = HALF // 2
TOK = PIECE * HEADS
LAST = HEADS // 2
W_HALF = HD // 2
W_PART = W_HALF // 2
W_BLOCK = 3
OUT_TILE = 256
MESH = pl.DeviceIdType.MESH


def layer_kernel(
    lists, hidden, xn, w_ref, shard, cos_b, sin_b, cos_r, sin_r, out_ref,
    x_all, kv_all, q_ref, m_ref, acc_ref, o_ref, w_all, mix,
    ring_send, ring_recv, z_send, z_recv, s_send, s_recv,
    w_send, w_recv, wp_send, wp_recv, w_own, a_send, a_recv, a_own,
):
    section = lax.axis_index("section")
    head = lax.axis_index("head")
    ypos, xpos = head // 4, head % 4
    diagonal = (xpos + ypos) % 4
    spot = (4 * ypos + diagonal, 4 * xpos + diagonal)

    def head_of(ring, place):
        place = (place + 2 * HEADS) % HEADS
        slow, fast = place // 4, place % 4
        other = (fast - slow + 4) % 4
        return slow * 4 + other if ring == 0 else other * 4 + slow

    def ring_device(ring, way):
        return {"section": section, "head": head_of(ring, spot[ring] + (1 if way == 0 else -1))}

    ring_to = [[ring_device(ring, way) for way in range(2)] for ring in range(2)]
    z_up = {"section": (section + 2) % SECTIONS, "head": head}
    z_down = {"section": (section + SECTIONS - 2) % SECTIONS, "head": head}
    partner = {"section": section + 1 - 2 * (section % 2), "head": head}

    barrier = pltpu.get_barrier_semaphore()
    for device in (z_up, z_down, partner):
        pl.semaphore_signal(barrier, inc=1, device_id=device, device_id_type=MESH)

    def greet(step, carry):
        peer = {"section": section, "head": (head + step) % HEADS}
        pl.semaphore_signal(barrier, inc=1, device_id=peer, device_id_type=MESH)
        return carry

    lax.fori_loop(1, HEADS, greet, 0)
    pl.semaphore_wait(barrier, HEADS + 2)

    def rows_of(start, size):
        return pl.ds(pl.multiple_of(start, 16), size)

    def send(source, target, send_sem, recv_sem, device):
        pltpu.make_async_remote_copy(
            src_ref=source,
            dst_ref=target,
            send_sem=send_sem,
            recv_sem=recv_sem,
            device_id=device,
            device_id_type=MESH,
        ).start()

    def arrived(ref, rows, sem):
        view = ref.at[pl.ds(0, rows), :]
        pltpu.make_async_copy(view, view, sem).wait()

    def origin(ring, way, step):
        return head_of(ring, spot[ring] + (step if way == 1 else -step))

    def unit_rows(ring, source, unit):
        return rows_of(source * PIECE + ring * HALF + unit * UNIT, UNIT)

    def pass_on(ring, way, unit, step, source):
        rows = unit_rows(ring, source, unit)
        send(
            x_all.at[rows, :],
            x_all.at[rows, :],
            ring_send,
            ring_recv.at[ring, way, unit, step + 1],
            ring_to[ring][way],
        )

    def starts_of(step):
        if isinstance(step, int) and step == 0:
            return [(head, 0), (head, 1)]
        if isinstance(step, int) and step == LAST:
            return [(origin(ring, 0, LAST), ring) for ring in range(2)]
        return [(origin(ring, way, step), ring) for ring in range(2) for way in range(2)]

    def project(tokens, pieces):
        weight = jnp.concatenate([w_ref[0], w_ref[1], w_ref[2]], axis=1)
        result = jnp.dot(tokens, weight, preferred_element_type=jnp.float32)
        for index, (source, ring) in enumerate(pieces):
            part = result[index * HALF : (index + 1) * HALF]
            base_cos, base_sin = cos_b[pl.ds(source, 1), :], sin_b[pl.ds(source, 1), :]
            row_cos = cos_r[ring * HALF : (ring + 1) * HALF, :]
            row_sin = sin_r[ring * HALF : (ring + 1) * HALF, :]
            cosine = base_cos * row_cos - base_sin * row_sin
            sine = base_sin * row_cos + base_cos * row_sin
            query, key, value = part[:, :HD], part[:, HD : 2 * HD], part[:, 2 * HD :]
            query = (query * cosine + pltpu.roll(query, HD // 2, 1) * sine) * QSCALE
            key = key * cosine + pltpu.roll(key, HD // 2, 1) * sine
            start = source * PIECE + ring * HALF
            q_ref[rows_of(start, HALF), :] = query.astype(jnp.bfloat16)
            own = rows_of(section * TOK + start, HALF)
            kv_all[own, :HD] = key.astype(jnp.bfloat16)
            kv_all[own, HD:] = value.astype(jnp.bfloat16)

    def kv_copy(region, start, size, send_sem, recv_sem, device):
        rows = rows_of(region * TOK + start, size)
        send(kv_all.at[rows, :], kv_all.at[rows, :], send_sem, recv_sem, device)

    def share(step, pieces):
        for source, ring in pieces:
            start = source * PIECE + ring * HALF
            kv_copy(section, start, HALF, z_send, z_recv.at[0, step], z_up)
            kv_copy(section, start, HALF, z_send, z_recv.at[1, step], z_down)
            kv_copy(section, start, HALF, s_send, s_recv.at[step], partner)

    def relay_near(step, pieces):
        below, above = (section + SECTIONS - 2) % SECTIONS, (section + 2) % SECTIONS
        arrived(kv_all, len(pieces) * HALF, z_recv.at[0, step])
        for source, ring in pieces:
            start = source * PIECE + ring * HALF
            kv_copy(below, start, UNIT, z_send, z_recv.at[2, step], z_up)
            kv_copy(below, start, HALF, s_send, s_recv.at[step], partner)
        arrived(kv_all, len(pieces) * HALF, z_recv.at[1, step])
        for source, ring in pieces:
            start = source * PIECE + ring * HALF
            kv_copy(above, start + UNIT, UNIT, z_send, z_recv.at[3, step], z_down)
            kv_copy(above, start, HALF, s_send, s_recv.at[step], partner)

    def relay_far(step, pieces):
        across = (section + 4) % SECTIONS
        arrived(kv_all, len(pieces) * UNIT, z_recv.at[2, step])
        arrived(kv_all, len(pieces) * UNIT, z_recv.at[3, step])
        for source, ring in pieces:
            start = source * PIECE + ring * HALF
            kv_copy(across, start, HALF, s_send, s_recv.at[step], partner)

    for unit in range(2):
        for ring in range(2):
            for way in range(2):
                send(
                    xn.at[pl.ds(ring * HALF + unit * UNIT, UNIT), :],
                    x_all.at[unit_rows(ring, head, unit), :],
                    ring_send,
                    ring_recv.at[ring, way, unit, 1],
                    ring_to[ring][way],
                )
    project(xn[...], starts_of(0))
    share(0, starts_of(0))
    relay_near(0, starts_of(0))

    def one_step(step, carry):
        for unit in range(2):
            for ring in range(2):
                for way in range(2):
                    arrived(x_all, UNIT, ring_recv.at[ring, way, unit, step])
                    source = origin(ring, way, step)
                    if way == unit:
                        pass_on(ring, way, unit, step, source)
                    else:

                        @pl.when(step < LAST - 1)
                        def _(ring=ring, way=way, unit=unit, source=source):
                            pass_on(ring, way, unit, step, source)

        pieces = starts_of(step)
        tokens = jnp.concatenate(
            [x_all[rows_of(source * PIECE + ring * HALF, HALF), :] for source, ring in pieces],
            axis=0,
        )
        project(tokens, pieces)

        @pl.when(step >= 2)
        def _():
            relay_near(step - 1, starts_of(step - 1))

        @pl.when(step >= 3)
        def _():
            relay_far(step - 2, starts_of(step - 2))

        share(step, pieces)
        return carry

    lax.fori_loop(1, LAST, one_step, 0)
    relay_far(0, starts_of(0))
    for ring in range(2):
        for way in range(2):
            arrived(x_all, UNIT, ring_recv.at[ring, way, way, LAST])
    pieces = starts_of(LAST)
    tokens = jnp.concatenate(
        [x_all[rows_of(source * PIECE + ring * HALF, HALF), :] for source, ring in pieces], axis=0
    )
    project(tokens, pieces)

    core = section % 2
    own_rows = pltpu.make_async_copy(
        shard, w_all.at[rows_of(head * HD, HD), :], w_own
    )
    own_rows.start()

    def w_rows(source, part):
        return rows_of(source * HD + core * W_HALF + part * W_PART, W_PART)

    def line(part, step):
        if part == 0:
            return ypos * 4 + (xpos + step) % 4
        return ((ypos + step) % 4) * 4 + xpos

    def w_copy(source, part, stage, target, own):
        if own:
            view = shard.at[rows_of(core * W_HALF + part * W_PART, W_PART), :]
        else:
            view = w_all.at[w_rows(source, part), :]
        send(
            view,
            w_all.at[w_rows(source, part), :],
            w_send,
            w_recv.at[part, stage],
            {"section": section, "head": target},
        )

    for part in range(2):
        for step in range(1, 4):
            w_copy(head, part, 0, line(part, step), True)
    relay_near(LAST - 1, starts_of(LAST - 1))
    relay_far(LAST - 2, starts_of(LAST - 2))
    share(LAST, pieces)
    relay_far(LAST - 1, starts_of(LAST - 1))
    relay_near(LAST, pieces)
    relay_far(LAST, pieces)
    for step in range(LAST + 1):
        arrived(kv_all, 4 * HALF * (2 if step in (0, LAST) else 4), s_recv.at[step])

    for part in range(2):
        arrived(w_all, 3 * W_PART, w_recv.at[part, 0])
        for step in range(1, 4):
            for other in range(4):
                w_copy(line(part, other), part, 1, line(1 - part, step), other == 0)

    def w_to_partner():
        for part in range(2):
            arrived(w_all, 12 * W_PART, w_recv.at[part, 1])

        def one(step, carry):
            rows = rows_of(((head + step) % HEADS) * HD + core * W_HALF, W_HALF)
            send(w_all.at[rows, :], w_all.at[rows, :], wp_send, wp_recv, partner)
            return carry

        lax.fori_loop(1, HEADS, one, 0)

    own_columns = pl.ds(pl.multiple_of(head * HD, HD), HD)

    def deliver(target, carry):
        rows = rows_of(target * PIECE, PIECE)

        @pl.when(target != head)
        def _():
            send(
                o_ref.at[rows, :],
                mix.at[:, own_columns],
                a_send,
                a_recv,
                {"section": section, "head": target},
            )

        return carry

    blocks = TOK // BLK
    ones = jnp.ones((BLK, HD), jnp.bfloat16)

    def one_block(block, carry):
        base = pl.multiple_of(block * BLK, BLK)
        count = 1 + ((section * blocks + block) * (KSEL - 1)) // (NBLK - 1)

        def tile(source, first):
            keys = kv_all[pl.ds(source * BLK, BLK), :HD]
            values = jnp.concatenate([kv_all[pl.ds(source * BLK, BLK), HD:], ones], axis=1)
            for part in range(BLK // ROWS):
                rows = pl.ds(part * ROWS, ROWS)
                query = q_ref[pl.ds(pl.multiple_of(base + part * ROWS, ROWS), ROWS), :]
                scores = lax.dot_general(
                    query, keys, (((1,), (1,)), ((), ())), preferred_element_type=jnp.float32
                )
                if first:
                    row = lax.broadcasted_iota(jnp.int32, (ROWS, BLK), 0) + part * ROWS
                    col = lax.broadcasted_iota(jnp.int32, (ROWS, BLK), 1)
                    scores = jnp.where(col <= row, scores, -jnp.inf)
                peak = jnp.max(scores, axis=1, keepdims=True)
                if not first:
                    old = m_ref[rows, :1]
                    peak = jnp.maximum(peak, old)
                weights = jnp.exp2(scores - peak).astype(jnp.bfloat16)
                update = jnp.dot(weights, values, preferred_element_type=jnp.float32)
                if first:
                    acc_ref[rows, :] = update
                else:
                    acc_ref[rows, :] = acc_ref[rows, :] * jnp.exp2(old - peak) + update
                m_ref[rows, :] = jnp.broadcast_to(peak, (ROWS, HD))

        tile(section * blocks + block, True)

        def one_slot(slot, inner):
            tile(lists[block, slot], False)
            return inner

        lax.fori_loop(1, count, one_slot, 0)
        for part in range(BLK // ROWS):
            rows = pl.ds(part * ROWS, ROWS)
            o_ref[pl.ds(pl.multiple_of(base + part * ROWS, ROWS), ROWS), :] = (
                acc_ref[rows, :HD] / acc_ref[rows, HD:]
            ).astype(jnp.bfloat16)
        lax.fori_loop((block * BLK) // PIECE, ((block + 1) * BLK) // PIECE, deliver, 0)

        @pl.when(block == W_BLOCK)
        def _():
            w_to_partner()

        return carry

    lax.fori_loop(0, blocks, one_block, 0)

    own_piece = pltpu.make_async_copy(
        o_ref.at[rows_of(head * PIECE, PIECE), :], mix.at[:, own_columns], a_own
    )
    own_piece.start()
    own_rows.wait()
    arrived(w_all, (HEADS - 1) * W_HALF, wp_recv)
    own_piece.wait()
    taken = mix.at[:, pl.ds(0, (HEADS - 1) * HD)]
    pltpu.make_async_copy(taken, taken, a_recv).wait()

    def one_tile(tile, carry):
        columns = pl.ds(pl.multiple_of(tile * OUT_TILE, OUT_TILE), OUT_TILE)
        summed = jnp.dot(mix[...], w_all[:, columns], preferred_element_type=jnp.float32)
        out_ref[:, columns] = (hidden[:, columns].astype(jnp.float32) + summed).astype(
            jnp.bfloat16
        )
        return carry

    lax.fori_loop(0, D // OUT_TILE, one_tile, 0)

    arrived(w_all, 30 * W_PART, w_send)
    arrived(w_all, (HEADS - 1) * W_HALF, wp_send)
    pltpu.make_async_copy(taken, taken, a_send).wait()
    arrived(x_all, 4 * (2 * LAST - 1) * UNIT, ring_send)
    arrived(kv_all, 3 * TOK, z_send)
    arrived(kv_all, 4 * TOK, s_send)


def layer(lists, hidden, normed, weight, shard, tables):
    vmem = pl.BlockSpec(memory_space=pltpu.VMEM)
    dma = pltpu.SemaphoreType.DMA
    return pl.pallas_call(
        layer_kernel,
        out_shape=jax.ShapeDtypeStruct((PIECE, D), jnp.bfloat16),
        in_specs=[pl.BlockSpec(memory_space=pltpu.SMEM)] + [vmem] * 8,
        out_specs=vmem,
        scratch_shapes=[
            pltpu.VMEM((TOK, D), jnp.bfloat16),
            pltpu.VMEM((SECTIONS * TOK, 2 * HD), jnp.bfloat16),
            pltpu.VMEM((TOK, HD), jnp.bfloat16),
            pltpu.VMEM((BLK, HD), jnp.float32),
            pltpu.VMEM((BLK, 2 * HD), jnp.float32),
            pltpu.VMEM((TOK, HD), jnp.bfloat16),
            pltpu.VMEM((D, D), jnp.bfloat16),
            pltpu.VMEM((PIECE, D), jnp.bfloat16),
            dma,
            dma((2, 2, 2, LAST + 1)),
            dma,
            dma((4, LAST + 1)),
            dma,
            dma((LAST + 1,)),
            dma,
            dma((2, 2)),
            dma,
            dma,
            dma,
            dma,
            dma,
            dma,
        ],
        compiler_params=pltpu.CompilerParams(
            collective_id=0, has_side_effects=True, vmem_limit_bytes=60 << 20
        ),
        name="layer",
    )(lists, hidden, normed, weight, shard, *tables)


def rotary_tables(positions):
    frequency = THETA ** (-(2.0 * jnp.arange(HD // 2, dtype=jnp.float32)) / HD)
    angle = positions.astype(jnp.float32)[:, None] * frequency[None, :]
    cosine, sine = jnp.cos(angle), jnp.sin(angle)
    return jnp.concatenate([cosine, cosine], axis=1), jnp.concatenate([-sine, sine], axis=1)


def local(hidden_in, norm_gain, w_qkv, w_out, block_lists):
    section_id = lax.axis_index("section")
    resid = hidden_in.astype(jnp.float32)
    normed = (
        resid * lax.rsqrt(jnp.mean(resid * resid, axis=-1, keepdims=True) + EPS) * norm_gain
    ).astype(jnp.bfloat16)
    weight = jnp.transpose(w_qkv, (1, 0, 2))
    bases = section_id * TOK + PIECE * jnp.arange(HEADS, dtype=jnp.int32)
    tables = rotary_tables(bases) + rotary_tables(jnp.arange(PIECE, dtype=jnp.int32))
    return layer(block_lists, hidden_in, normed, weight, w_out, tables)


def solution(mesh):
    placed = (
        P(("section", "head"), None),
        P(),
        P(None, None, "head"),
        P("head", None),
        P("section", None),
    )
    return jax.shard_map(
        local, mesh=mesh, in_specs=placed, out_specs=P(("section", "head"), None), check_vma=False
    )
```

```python
import functools
import math

import jax
import jax.numpy as jnp
from jax import lax
from jax.experimental import pallas as pl
from jax.experimental.pallas import tpu as pltpu
from jax.sharding import PartitionSpec as P

D = 2048
HD = 128
BLK = 512
KSEL = 12
NBLK = 48
SECTIONS = 8
HEADS = 16

EPS = 1e-05
THETA = 10000.0
QSCALE = math.log2(math.e) / math.sqrt(HD)
ROWS = 128
GROUP = 4

PIECE = 192
HALF = PIECE // 2
UNIT = HALF // 2
TOK = PIECE * HEADS
LAST = HEADS // 2
W_HALF = HD // 2
W_PART = W_HALF // 2
W_BLOCK = 3
OUT_TILE = 256
MESH = pl.DeviceIdType.MESH


def layer_kernel(
    lists, hidden, xn, w_ref, shard, cos_b, sin_b, cos_r, sin_r, out_ref,
    x_all, kv_all, q_ref, m_ref, acc_ref, o_ref, w_all, mix,
    ring_send, ring_recv, z_send, z_recv, s_send, s_recv,
    w_send, w_recv, wp_send, wp_recv, w_own, a_send, a_recv, a_own,
):
    section = lax.axis_index("section")
    head = lax.axis_index("head")
    ypos, xpos = head // 4, head % 4
    diagonal = (xpos + ypos) % 4
    spot = (4 * ypos + diagonal, 4 * xpos + diagonal)

    def head_of(ring, place):
        place = (place + 2 * HEADS) % HEADS
        slow, fast = place // 4, place % 4
        other = (fast - slow + 4) % 4
        return slow * 4 + other if ring == 0 else other * 4 + slow

    def ring_device(ring, way):
        return {"section": section, "head": head_of(ring, spot[ring] + (1 if way == 0 else -1))}

    ring_to = [[ring_device(ring, way) for way in range(2)] for ring in range(2)]
    z_up = {"section": (section + 2) % SECTIONS, "head": head}
    z_down = {"section": (section + SECTIONS - 2) % SECTIONS, "head": head}
    partner = {"section": section + 1 - 2 * (section % 2), "head": head}

    barrier = pltpu.get_barrier_semaphore()
    for device in (z_up, z_down, partner):
        pl.semaphore_signal(barrier, inc=1, device_id=device, device_id_type=MESH)

    def greet(step, carry):
        peer = {"section": section, "head": (head + step) % HEADS}
        pl.semaphore_signal(barrier, inc=1, device_id=peer, device_id_type=MESH)
        return carry

    lax.fori_loop(1, HEADS, greet, 0)
    pl.semaphore_wait(barrier, HEADS + 2)

    def rows_of(start, size):
        return pl.ds(pl.multiple_of(start, 16), size)

    def send(source, target, send_sem, recv_sem, device):
        pltpu.make_async_remote_copy(
            src_ref=source,
            dst_ref=target,
            send_sem=send_sem,
            recv_sem=recv_sem,
            device_id=device,
            device_id_type=MESH,
        ).start()

    def arrived(ref, rows, sem):
        view = ref.at[pl.ds(0, rows), :]
        pltpu.make_async_copy(view, view, sem).wait()

    def origin(ring, way, step):
        return head_of(ring, spot[ring] + (step if way == 1 else -step))

    def unit_rows(ring, source, unit):
        return rows_of(source * PIECE + ring * HALF + unit * UNIT, UNIT)

    def pass_on(ring, way, unit, step, source):
        rows = unit_rows(ring, source, unit)
        send(
            x_all.at[rows, :],
            x_all.at[rows, :],
            ring_send,
            ring_recv.at[ring, way, unit, step + 1],
            ring_to[ring][way],
        )

    def starts_of(step):
        if isinstance(step, int) and step == 0:
            return [(head, 0), (head, 1)]
        if isinstance(step, int) and step == LAST:
            return [(origin(ring, 0, LAST), ring) for ring in range(2)]
        return [(origin(ring, way, step), ring) for ring in range(2) for way in range(2)]

    def project(tokens, pieces):
        weight = jnp.concatenate([w_ref[0], w_ref[1], w_ref[2]], axis=1)
        result = jnp.dot(tokens, weight, preferred_element_type=jnp.float32)
        for index, (source, ring) in enumerate(pieces):
            part = result[index * HALF : (index + 1) * HALF]
            base_cos, base_sin = cos_b[pl.ds(source, 1), :], sin_b[pl.ds(source, 1), :]
            row_cos = cos_r[ring * HALF : (ring + 1) * HALF, :]
            row_sin = sin_r[ring * HALF : (ring + 1) * HALF, :]
            cosine = base_cos * row_cos - base_sin * row_sin
            sine = base_sin * row_cos + base_cos * row_sin
            query, key, value = part[:, :HD], part[:, HD : 2 * HD], part[:, 2 * HD :]
            query = (query * cosine + pltpu.roll(query, HD // 2, 1) * sine) * QSCALE
            key = key * cosine + pltpu.roll(key, HD // 2, 1) * sine
            start = source * PIECE + ring * HALF
            q_ref[rows_of(start, HALF), :] = query.astype(jnp.bfloat16)
            own = rows_of(section * TOK + start, HALF)
            kv_all[own, :HD] = key.astype(jnp.bfloat16)
            kv_all[own, HD:] = value.astype(jnp.bfloat16)

    def kv_copy(region, start, size, send_sem, recv_sem, device):
        rows = rows_of(region * TOK + start, size)
        send(kv_all.at[rows, :], kv_all.at[rows, :], send_sem, recv_sem, device)

    def share(step, pieces):
        for source, ring in pieces:
            start = source * PIECE + ring * HALF
            kv_copy(section, start, HALF, z_send, z_recv.at[0, step], z_up)
            kv_copy(section, start, HALF, z_send, z_recv.at[1, step], z_down)
            kv_copy(section, start, HALF, s_send, s_recv.at[step], partner)

    def relay_near(step, pieces):
        below, above = (section + SECTIONS - 2) % SECTIONS, (section + 2) % SECTIONS
        arrived(kv_all, len(pieces) * HALF, z_recv.at[0, step])
        for source, ring in pieces:
            start = source * PIECE + ring * HALF
            kv_copy(below, start, UNIT, z_send, z_recv.at[2, step], z_up)
            kv_copy(below, start, HALF, s_send, s_recv.at[step], partner)
        arrived(kv_all, len(pieces) * HALF, z_recv.at[1, step])
        for source, ring in pieces:
            start = source * PIECE + ring * HALF
            kv_copy(above, start + UNIT, UNIT, z_send, z_recv.at[3, step], z_down)
            kv_copy(above, start, HALF, s_send, s_recv.at[step], partner)

    def relay_far(step, pieces):
        across = (section + 4) % SECTIONS
        arrived(kv_all, len(pieces) * UNIT, z_recv.at[2, step])
        arrived(kv_all, len(pieces) * UNIT, z_recv.at[3, step])
        for source, ring in pieces:
            start = source * PIECE + ring * HALF
            kv_copy(across, start, HALF, s_send, s_recv.at[step], partner)

    for unit in range(2):
        for ring in range(2):
            for way in range(2):
                send(
                    xn.at[pl.ds(ring * HALF + unit * UNIT, UNIT), :],
                    x_all.at[unit_rows(ring, head, unit), :],
                    ring_send,
                    ring_recv.at[ring, way, unit, 1],
                    ring_to[ring][way],
                )
    project(xn[...], starts_of(0))
    share(0, starts_of(0))
    relay_near(0, starts_of(0))

    def one_step(step, carry):
        for unit in range(2):
            for ring in range(2):
                for way in range(2):
                    arrived(x_all, UNIT, ring_recv.at[ring, way, unit, step])
                    source = origin(ring, way, step)
                    if way == unit:
                        pass_on(ring, way, unit, step, source)
                    else:

                        @pl.when(step < LAST - 1)
                        def _(ring=ring, way=way, unit=unit, source=source):
                            pass_on(ring, way, unit, step, source)

        pieces = starts_of(step)
        tokens = jnp.concatenate(
            [x_all[rows_of(source * PIECE + ring * HALF, HALF), :] for source, ring in pieces],
            axis=0,
        )
        project(tokens, pieces)

        @pl.when(step >= 2)
        def _():
            relay_near(step - 1, starts_of(step - 1))

        @pl.when(step >= 3)
        def _():
            relay_far(step - 2, starts_of(step - 2))

        share(step, pieces)
        return carry

    lax.fori_loop(1, LAST, one_step, 0)
    relay_far(0, starts_of(0))
    for ring in range(2):
        for way in range(2):
            arrived(x_all, UNIT, ring_recv.at[ring, way, way, LAST])
    pieces = starts_of(LAST)
    tokens = jnp.concatenate(
        [x_all[rows_of(source * PIECE + ring * HALF, HALF), :] for source, ring in pieces], axis=0
    )
    project(tokens, pieces)

    core = section % 2
    own_rows = pltpu.make_async_copy(
        shard, w_all.at[rows_of(head * HD, HD), :], w_own
    )
    own_rows.start()

    def w_rows(source, part):
        return rows_of(source * HD + core * W_HALF + part * W_PART, W_PART)

    def line(part, step):
        if part == 0:
            return ypos * 4 + (xpos + step) % 4
        return ((ypos + step) % 4) * 4 + xpos

    def w_copy(source, part, stage, target, own):
        if own:
            view = shard.at[rows_of(core * W_HALF + part * W_PART, W_PART), :]
        else:
            view = w_all.at[w_rows(source, part), :]
        send(
            view,
            w_all.at[w_rows(source, part), :],
            w_send,
            w_recv.at[part, stage],
            {"section": section, "head": target},
        )

    for part in range(2):
        for step in range(1, 4):
            w_copy(head, part, 0, line(part, step), True)
    relay_near(LAST - 1, starts_of(LAST - 1))
    relay_far(LAST - 2, starts_of(LAST - 2))
    share(LAST, pieces)
    relay_far(LAST - 1, starts_of(LAST - 1))
    relay_near(LAST, pieces)
    relay_far(LAST, pieces)
    for step in range(LAST + 1):
        arrived(kv_all, 4 * HALF * (2 if step in (0, LAST) else 4), s_recv.at[step])

    for part in range(2):
        arrived(w_all, 3 * W_PART, w_recv.at[part, 0])
        for step in range(1, 4):
            for other in range(4):
                w_copy(line(part, other), part, 1, line(1 - part, step), other == 0)

    def w_to_partner():
        for part in range(2):
            arrived(w_all, 12 * W_PART, w_recv.at[part, 1])

        def one(step, carry):
            rows = rows_of(((head + step) % HEADS) * HD + core * W_HALF, W_HALF)
            send(w_all.at[rows, :], w_all.at[rows, :], wp_send, wp_recv, partner)
            return carry

        lax.fori_loop(1, HEADS, one, 0)

    own_columns = pl.ds(pl.multiple_of(head * HD, HD), HD)

    def deliver(target, carry):
        rows = rows_of(target * PIECE, PIECE)

        @pl.when(target != head)
        def _():
            send(
                o_ref.at[rows, :],
                mix.at[:, own_columns],
                a_send,
                a_recv,
                {"section": section, "head": target},
            )

        return carry

    blocks = TOK // BLK
    ones = jnp.ones((BLK, HD), jnp.bfloat16)

    def one_block(block, carry):
        base = pl.multiple_of(block * BLK, BLK)
        own = section * blocks + block
        others = (own * (KSEL - 1)) // (NBLK - 1)
        spare = others % GROUP

        def tiles(first, slots):
            sources = [lists[block, slot] for slot in slots]
            pairs = [
                (
                    kv_all[pl.ds(source * BLK, BLK), :HD],
                    jnp.concatenate([kv_all[pl.ds(source * BLK, BLK), HD:], ones], axis=1),
                )
                for source in sources
            ]
            for part in range(BLK // ROWS):
                rows = pl.ds(part * ROWS, ROWS)
                query = q_ref[pl.ds(pl.multiple_of(base + part * ROWS, ROWS), ROWS), :]
                keyed = list(pairs)
                if first:
                    seen = (part + 1) * ROWS
                    here = kv_all[pl.ds(own * BLK, seen), :]
                    keyed.append(
                        (here[:, :HD], jnp.concatenate([here[:, HD:], ones[:seen]], axis=1))
                    )
                scores = [
                    lax.dot_general(
                        query, keys, (((1,), (1,)), ((), ())), preferred_element_type=jnp.float32
                    )
                    for keys, _ in keyed
                ]
                if first:
                    row = lax.broadcasted_iota(jnp.int32, (ROWS, seen), 0) + part * ROWS
                    col = lax.broadcasted_iota(jnp.int32, (ROWS, seen), 1)
                    scores[-1] = jnp.where(col <= row, scores[-1], -jnp.inf)
                if len(scores) > 1 and not first:
                    peak = jnp.max(functools.reduce(jnp.maximum, scores), axis=1, keepdims=True)
                else:
                    peak = functools.reduce(
                        jnp.maximum, [jnp.max(one, axis=1, keepdims=True) for one in scores]
                    )
                if not first:
                    old = m_ref[rows, :1]
                    peak = jnp.maximum(peak, old)
                update = None
                for one, (_, values) in zip(scores, keyed):
                    weights = jnp.exp2(one - peak).astype(jnp.bfloat16)
                    term = jnp.dot(weights, values, preferred_element_type=jnp.float32)
                    update = term if update is None else update + term
                if first:
                    acc_ref[rows, :] = update
                else:
                    acc_ref[rows, :] = acc_ref[rows, :] * jnp.exp2(old - peak) + update
                m_ref[rows, :] = jnp.broadcast_to(peak, (ROWS, HD))

        for extra in range(GROUP):

            @pl.when(spare == extra)
            def _(extra=extra):
                tiles(True, [1 + slot for slot in range(extra)])

        def one_group(group, inner):
            first_slot = 1 + spare + group * GROUP
            tiles(False, [first_slot + slot for slot in range(GROUP)])
            return inner

        lax.fori_loop(0, others // GROUP, one_group, 0)
        for part in range(BLK // ROWS):
            rows = pl.ds(part * ROWS, ROWS)
            o_ref[pl.ds(pl.multiple_of(base + part * ROWS, ROWS), ROWS), :] = (
                acc_ref[rows, :HD] / acc_ref[rows, HD:]
            ).astype(jnp.bfloat16)
        lax.fori_loop((block * BLK) // PIECE, ((block + 1) * BLK) // PIECE, deliver, 0)

        @pl.when(block == W_BLOCK)
        def _():
            w_to_partner()

        return carry

    lax.fori_loop(0, blocks, one_block, 0)

    own_piece = pltpu.make_async_copy(
        o_ref.at[rows_of(head * PIECE, PIECE), :], mix.at[:, own_columns], a_own
    )
    own_piece.start()
    own_rows.wait()
    arrived(w_all, (HEADS - 1) * W_HALF, wp_recv)
    own_piece.wait()
    taken = mix.at[:, pl.ds(0, (HEADS - 1) * HD)]
    pltpu.make_async_copy(taken, taken, a_recv).wait()

    def one_tile(tile, carry):
        columns = pl.ds(pl.multiple_of(tile * OUT_TILE, OUT_TILE), OUT_TILE)
        summed = jnp.dot(mix[...], w_all[:, columns], preferred_element_type=jnp.float32)
        out_ref[:, columns] = (hidden[:, columns].astype(jnp.float32) + summed).astype(
            jnp.bfloat16
        )
        return carry

    lax.fori_loop(0, D // OUT_TILE, one_tile, 0)

    arrived(w_all, 30 * W_PART, w_send)
    arrived(w_all, (HEADS - 1) * W_HALF, wp_send)
    pltpu.make_async_copy(taken, taken, a_send).wait()
    arrived(x_all, 4 * (2 * LAST - 1) * UNIT, ring_send)
    arrived(kv_all, 3 * TOK, z_send)
    arrived(kv_all, 4 * TOK, s_send)


def layer(lists, hidden, normed, weight, shard, tables):
    vmem = pl.BlockSpec(memory_space=pltpu.VMEM)
    dma = pltpu.SemaphoreType.DMA
    return pl.pallas_call(
        layer_kernel,
        out_shape=jax.ShapeDtypeStruct((PIECE, D), jnp.bfloat16),
        in_specs=[pl.BlockSpec(memory_space=pltpu.SMEM)] + [vmem] * 8,
        out_specs=vmem,
        scratch_shapes=[
            pltpu.VMEM((TOK, D), jnp.bfloat16),
            pltpu.VMEM((SECTIONS * TOK, 2 * HD), jnp.bfloat16),
            pltpu.VMEM((TOK, HD), jnp.bfloat16),
            pltpu.VMEM((BLK, HD), jnp.float32),
            pltpu.VMEM((BLK, 2 * HD), jnp.float32),
            pltpu.VMEM((TOK, HD), jnp.bfloat16),
            pltpu.VMEM((D, D), jnp.bfloat16),
            pltpu.VMEM((PIECE, D), jnp.bfloat16),
            dma,
            dma((2, 2, 2, LAST + 1)),
            dma,
            dma((4, LAST + 1)),
            dma,
            dma((LAST + 1,)),
            dma,
            dma((2, 2)),
            dma,
            dma,
            dma,
            dma,
            dma,
            dma,
        ],
        compiler_params=pltpu.CompilerParams(
            collective_id=0, has_side_effects=True, vmem_limit_bytes=60 << 20
        ),
        name="layer",
    )(lists, hidden, normed, weight, shard, *tables)


def rotary_tables(positions):
    frequency = THETA ** (-(2.0 * jnp.arange(HD // 2, dtype=jnp.float32)) / HD)
    angle = positions.astype(jnp.float32)[:, None] * frequency[None, :]
    cosine, sine = jnp.cos(angle), jnp.sin(angle)
    return jnp.concatenate([cosine, cosine], axis=1), jnp.concatenate([-sine, sine], axis=1)


def local(hidden_in, norm_gain, w_qkv, w_out, block_lists):
    section_id = lax.axis_index("section")
    resid = hidden_in.astype(jnp.float32)
    normed = (
        resid * lax.rsqrt(jnp.mean(resid * resid, axis=-1, keepdims=True) + EPS) * norm_gain
    ).astype(jnp.bfloat16)
    weight = jnp.transpose(w_qkv, (1, 0, 2))
    bases = section_id * TOK + PIECE * jnp.arange(HEADS, dtype=jnp.int32)
    tables = rotary_tables(bases) + rotary_tables(jnp.arange(PIECE, dtype=jnp.int32))
    return layer(block_lists, hidden_in, normed, weight, w_out, tables)


def solution(mesh):
    placed = (
        P(("section", "head"), None),
        P(),
        P(None, None, "head"),
        P("head", None),
        P("section", None),
    )
    return jax.shard_map(
        local, mesh=mesh, in_specs=placed, out_specs=P(("section", "head"), None), check_vma=False
    )
```

```python
import functools
import math

import jax
import jax.numpy as jnp
from jax import lax
from jax.experimental import pallas as pl
from jax.experimental.pallas import tpu as pltpu
from jax.sharding import PartitionSpec as P

D = 2048
HD = 128
BLK = 512
KSEL = 12
NBLK = 48
SECTIONS = 8
HEADS = 16

EPS = 1e-05
THETA = 10000.0
QSCALE = math.log2(math.e) / math.sqrt(HD)
ROWS = 128
GROUP = 4

PIECE = 192
HALF = PIECE // 2
UNIT = HALF // 2
TOK = PIECE * HEADS
LAST = HEADS // 2
W_HALF = HD // 2
W_PART = W_HALF // 2
BLOCKS = TOK // BLK
MOVED = 3
CHUNK = 64
OUT_TILE = 256
MESH = pl.DeviceIdType.MESH


def layer_kernel(
    lists_here, hidden, xn, w_ref, shard, cos_b, sin_b, cos_r, sin_r, out_ref,
    x_all, kv_all, q_ref, m_ref, acc_ref, o_ref, w_all, mix,
    ring_send, ring_recv, z_send, z_recv, s_send, s_recv,
    w_send, w_recv, wp_send, wp_recv, w_own, a_send, a_recv,
    lists, l_send, l_recv, l_own, m_send, m_recv,
):
    section = lax.axis_index("section")
    head = lax.axis_index("head")
    ypos, xpos = head // 4, head % 4
    diagonal = (xpos + ypos) % 4
    spot = (4 * ypos + diagonal, 4 * xpos + diagonal)

    def head_of(ring, place):
        place = (place + 2 * HEADS) % HEADS
        slow, fast = place // 4, place % 4
        other = (fast - slow + 4) % 4
        return slow * 4 + other if ring == 0 else other * 4 + slow

    def ring_device(ring, way):
        return {"section": section, "head": head_of(ring, spot[ring] + (1 if way == 0 else -1))}

    ring_to = [[ring_device(ring, way) for way in range(2)] for ring in range(2)]
    z_up = {"section": (section + 2) % SECTIONS, "head": head}
    z_down = {"section": (section + SECTIONS - 2) % SECTIONS, "head": head}
    partner = {"section": section + 1 - 2 * (section % 2), "head": head}
    mate_section = SECTIONS - 1 - section
    mate = {"section": mate_section, "head": head}
    heavy = section >= SECTIONS // 2
    moved = (jnp.maximum(section, mate_section) - 1) // 2

    barrier = pltpu.get_barrier_semaphore()
    for device in (z_up, z_down, partner):
        pl.semaphore_signal(barrier, inc=1, device_id=device, device_id_type=MESH)

    def greet(step, carry):
        peer = {"section": section, "head": (head + step) % HEADS}
        pl.semaphore_signal(barrier, inc=1, device_id=peer, device_id_type=MESH)
        return carry

    lax.fori_loop(1, HEADS, greet, 0)

    def greet_mates(step, carry):
        peer = {"section": mate_section, "head": (head + step) % HEADS}
        pl.semaphore_signal(barrier, inc=1, device_id=peer, device_id_type=MESH)
        return carry

    lax.fori_loop(0, HEADS, greet_mates, 0)
    pl.semaphore_wait(barrier, 2 * HEADS + 2)

    def rows_of(start, size):
        return pl.ds(pl.multiple_of(start, 16), size)

    def send(source, target, send_sem, recv_sem, device):
        pltpu.make_async_remote_copy(
            src_ref=source,
            dst_ref=target,
            send_sem=send_sem,
            recv_sem=recv_sem,
            device_id=device,
            device_id_type=MESH,
        ).start()

    def arrived(ref, rows, sem):
        view = ref.at[pl.ds(0, rows), :]
        pltpu.make_async_copy(view, view, sem).wait()

    def origin(ring, way, step):
        return head_of(ring, spot[ring] + (step if way == 1 else -step))

    def unit_rows(ring, source, unit):
        return rows_of(source * PIECE + ring * HALF + unit * UNIT, UNIT)

    def pass_on(ring, way, unit, step, source):
        rows = unit_rows(ring, source, unit)
        send(
            x_all.at[rows, :],
            x_all.at[rows, :],
            ring_send,
            ring_recv.at[ring, way, unit, step + 1],
            ring_to[ring][way],
        )

    def starts_of(step):
        if isinstance(step, int) and step == 0:
            return [(head, 0), (head, 1)]
        if isinstance(step, int) and step == LAST:
            return [(origin(ring, 0, LAST), ring) for ring in range(2)]
        return [(origin(ring, way, step), ring) for ring in range(2) for way in range(2)]

    def project(tokens, pieces):
        weight = jnp.concatenate([w_ref[0], w_ref[1], w_ref[2]], axis=1)
        result = jnp.dot(tokens, weight, preferred_element_type=jnp.float32)
        for index, (source, ring) in enumerate(pieces):
            part = result[index * HALF : (index + 1) * HALF]
            base_cos, base_sin = cos_b[pl.ds(source, 1), :], sin_b[pl.ds(source, 1), :]
            row_cos = cos_r[ring * HALF : (ring + 1) * HALF, :]
            row_sin = sin_r[ring * HALF : (ring + 1) * HALF, :]
            cosine = base_cos * row_cos - base_sin * row_sin
            sine = base_sin * row_cos + base_cos * row_sin
            query, key, value = part[:, :HD], part[:, HD : 2 * HD], part[:, 2 * HD :]
            query = (query * cosine + pltpu.roll(query, HD // 2, 1) * sine) * QSCALE
            key = key * cosine + pltpu.roll(key, HD // 2, 1) * sine
            start = source * PIECE + ring * HALF
            q_ref[rows_of(start, HALF), :] = query.astype(jnp.bfloat16)
            own = rows_of(section * TOK + start, HALF)
            kv_all[own, :HD] = key.astype(jnp.bfloat16)
            kv_all[own, HD:] = value.astype(jnp.bfloat16)

    def kv_copy(region, start, size, send_sem, recv_sem, device):
        rows = rows_of(region * TOK + start, size)
        send(kv_all.at[rows, :], kv_all.at[rows, :], send_sem, recv_sem, device)

    def share(step, pieces):
        for source, ring in pieces:
            start = source * PIECE + ring * HALF
            kv_copy(section, start, HALF, z_send, z_recv.at[0, step], z_up)
            kv_copy(section, start, HALF, z_send, z_recv.at[1, step], z_down)
            kv_copy(section, start, HALF, s_send, s_recv.at[step], partner)

    def relay_near(step, pieces):
        below, above = (section + SECTIONS - 2) % SECTIONS, (section + 2) % SECTIONS
        arrived(kv_all, len(pieces) * HALF, z_recv.at[0, step])
        for source, ring in pieces:
            start = source * PIECE + ring * HALF
            kv_copy(below, start, UNIT, z_send, z_recv.at[2, step], z_up)
            kv_copy(below, start, HALF, s_send, s_recv.at[step], partner)
        arrived(kv_all, len(pieces) * HALF, z_recv.at[1, step])
        for source, ring in pieces:
            start = source * PIECE + ring * HALF
            kv_copy(above, start + UNIT, UNIT, z_send, z_recv.at[3, step], z_down)
            kv_copy(above, start, HALF, s_send, s_recv.at[step], partner)

    def relay_far(step, pieces):
        across = (section + 4) % SECTIONS
        arrived(kv_all, len(pieces) * UNIT, z_recv.at[2, step])
        arrived(kv_all, len(pieces) * UNIT, z_recv.at[3, step])
        for source, ring in pieces:
            start = source * PIECE + ring * HALF
            kv_copy(across, start, HALF, s_send, s_recv.at[step], partner)

    for unit in range(2):
        for ring in range(2):
            for way in range(2):
                send(
                    xn.at[pl.ds(ring * HALF + unit * UNIT, UNIT), :],
                    x_all.at[unit_rows(ring, head, unit), :],
                    ring_send,
                    ring_recv.at[ring, way, unit, 1],
                    ring_to[ring][way],
                )
    send(lists_here, lists.at[1], l_send, l_recv, mate)
    own_lists = pltpu.make_async_copy(lists_here, lists.at[0], l_own)
    own_lists.start()
    project(xn[...], starts_of(0))
    share(0, starts_of(0))
    relay_near(0, starts_of(0))

    def one_step(step, carry):
        for unit in range(2):
            for ring in range(2):
                for way in range(2):
                    arrived(x_all, UNIT, ring_recv.at[ring, way, unit, step])
                    source = origin(ring, way, step)
                    if way == unit:
                        pass_on(ring, way, unit, step, source)
                    else:

                        @pl.when(step < LAST - 1)
                        def _(ring=ring, way=way, unit=unit, source=source):
                            pass_on(ring, way, unit, step, source)

        pieces = starts_of(step)
        tokens = jnp.concatenate(
            [x_all[rows_of(source * PIECE + ring * HALF, HALF), :] for source, ring in pieces],
            axis=0,
        )
        project(tokens, pieces)

        @pl.when(step >= 2)
        def _():
            relay_near(step - 1, starts_of(step - 1))

        @pl.when(step >= 3)
        def _():
            relay_far(step - 2, starts_of(step - 2))

        share(step, pieces)
        return carry

    lax.fori_loop(1, LAST, one_step, 0)
    relay_far(0, starts_of(0))
    for ring in range(2):
        for way in range(2):
            arrived(x_all, UNIT, ring_recv.at[ring, way, way, LAST])
    pieces = starts_of(LAST)
    tokens = jnp.concatenate(
        [x_all[rows_of(source * PIECE + ring * HALF, HALF), :] for source, ring in pieces], axis=0
    )
    project(tokens, pieces)

    core = section % 2
    own_rows = pltpu.make_async_copy(
        shard, w_all.at[rows_of(head * HD, HD), :], w_own
    )
    own_rows.start()

    def w_rows(source, part):
        return rows_of(source * HD + core * W_HALF + part * W_PART, W_PART)

    def line(part, step):
        if part == 0:
            return ypos * 4 + (xpos + step) % 4
        return ((ypos + step) % 4) * 4 + xpos

    def w_copy(source, part, stage, target, own):
        if own:
            view = shard.at[rows_of(core * W_HALF + part * W_PART, W_PART), :]
        else:
            view = w_all.at[w_rows(source, part), :]
        send(
            view,
            w_all.at[w_rows(source, part), :],
            w_send,
            w_recv.at[part, stage],
            {"section": section, "head": target},
        )

    for part in range(2):
        for step in range(1, 4):
            w_copy(head, part, 0, line(part, step), True)

    for block in range(MOVED):

        @pl.when(heavy & (block < moved))
        def _(block=block):
            send(
                q_ref.at[pl.ds(block * BLK, BLK), :],
                q_ref.at[pl.ds(TOK + block * BLK, BLK), :],
                m_send.at[block],
                m_recv.at[block],
                mate,
            )

    relay_near(LAST - 1, starts_of(LAST - 1))
    relay_far(LAST - 2, starts_of(LAST - 2))
    share(LAST, pieces)
    for part in range(2):
        arrived(w_all, 3 * W_PART, w_recv.at[part, 0])
        for step in range(1, 4):
            for other in range(4):
                w_copy(line(part, other), part, 1, line(1 - part, step), other == 0)
    relay_far(LAST - 1, starts_of(LAST - 1))
    relay_near(LAST, pieces)
    relay_far(LAST, pieces)
    for step in range(LAST + 1):
        arrived(kv_all, 4 * HALF * (2 if step in (0, LAST) else 4), s_recv.at[step])

    def w_to_partner():
        for part in range(2):
            arrived(w_all, 12 * W_PART, w_recv.at[part, 1])

        def one(step, carry):
            rows = rows_of(((head + step) % HEADS) * HD + core * W_HALF, W_HALF)
            send(w_all.at[rows, :], w_all.at[rows, :], wp_send, wp_recv, partner)
            return carry

        lax.fori_loop(1, HEADS, one, 0)

    own_columns = pl.ds(pl.multiple_of(head * HD, HD), HD)

    def chunk_of(turn, own, chunk):
        where = own % BLOCKS * BLK + chunk * CHUNK
        target = where // PIECE
        into = mix.at[rows_of(where - target * PIECE, CHUNK), own_columns]
        source = o_ref.at[rows_of(turn * BLK + chunk * CHUNK, CHUNK), :]
        here = (own // BLOCKS == section) & (target == head)
        device = {"section": own // BLOCKS, "head": target}
        copy = pltpu.make_async_remote_copy(
            src_ref=source,
            dst_ref=into,
            send_sem=a_send.at[turn, chunk],
            recv_sem=a_recv,
            device_id=device,
            device_id_type=MESH,
        )
        return source, into, here, copy

    def deliver(turn, own):
        for chunk in range(BLK // CHUNK):
            source, into, here, copy = chunk_of(turn, own, chunk)

            @pl.when(here)
            def _(source=source, into=into):
                pltpu.make_async_copy(source, into, a_recv).start()

            @pl.when(jnp.logical_not(here))
            def _(copy=copy):
                copy.start()

    def delivered(turn, own):
        for chunk in range(BLK // CHUNK):
            _, _, here, copy = chunk_of(turn, own, chunk)

            @pl.when(jnp.logical_not(here))
            def _(copy=copy):
                copy.wait_send()

    own_lists.wait()
    arrived_lists = pltpu.make_async_copy(lists.at[1], lists.at[1], l_recv)
    arrived_lists.wait()
    taken = jnp.where(heavy, 0, moved)
    given = moved - taken
    turns = BLOCKS + taken - given

    for block in range(MOVED):

        @pl.when(block < taken)
        def _(block=block):
            arrived(q_ref, BLK, m_recv.at[block])

    def block_of(turn):
        away = turn < taken
        here = turn - taken + given
        row = jnp.where(away, turn, here)
        side = jnp.where(away, 1, 0)
        own = jnp.where(away, mate_section, section) * BLOCKS + row
        return own, side, row, row * BLK + side * TOK

    ones = jnp.ones((BLK, HD), jnp.bfloat16)

    def one_block(turn, carry):
        own, side, block, base = block_of(turn)
        base = pl.multiple_of(base, BLK)
        landing = pl.multiple_of(turn * BLK, BLK)
        others = (own * (KSEL - 1)) // (NBLK - 1)
        spare = others % GROUP

        def tiles(first, slots):
            sources = [lists[side, block, slot] for slot in slots]
            pairs = [
                (
                    kv_all[pl.ds(source * BLK, BLK), :HD],
                    jnp.concatenate([kv_all[pl.ds(source * BLK, BLK), HD:], ones], axis=1),
                )
                for source in sources
            ]
            for part in range(BLK // ROWS):
                rows = pl.ds(part * ROWS, ROWS)
                query = q_ref[pl.ds(pl.multiple_of(base + part * ROWS, ROWS), ROWS), :]
                keyed = list(pairs)
                if first:
                    seen = (part + 1) * ROWS
                    here = kv_all[pl.ds(own * BLK, seen), :]
                    keyed.append(
                        (here[:, :HD], jnp.concatenate([here[:, HD:], ones[:seen]], axis=1))
                    )
                scores = [
                    lax.dot_general(
                        query, keys, (((1,), (1,)), ((), ())), preferred_element_type=jnp.float32
                    )
                    for keys, _ in keyed
                ]
                if first:
                    row = lax.broadcasted_iota(jnp.int32, (ROWS, seen), 0) + part * ROWS
                    col = lax.broadcasted_iota(jnp.int32, (ROWS, seen), 1)
                    scores[-1] = jnp.where(col <= row, scores[-1], -jnp.inf)
                if len(scores) > 1 and not first:
                    peak = jnp.max(functools.reduce(jnp.maximum, scores), axis=1, keepdims=True)
                else:
                    peak = functools.reduce(
                        jnp.maximum, [jnp.max(one, axis=1, keepdims=True) for one in scores]
                    )
                if not first:
                    old = m_ref[rows, :1]
                    peak = jnp.maximum(peak, old)
                update = None
                for one, (_, values) in zip(scores, keyed):
                    weights = jnp.exp2(one - peak).astype(jnp.bfloat16)
                    term = jnp.dot(weights, values, preferred_element_type=jnp.float32)
                    update = term if update is None else update + term
                if first:
                    acc_ref[rows, :] = update
                else:
                    acc_ref[rows, :] = acc_ref[rows, :] * jnp.exp2(old - peak) + update
                m_ref[rows, :] = jnp.broadcast_to(peak, (ROWS, HD))

        for extra in range(GROUP):

            @pl.when(spare == extra)
            def _(extra=extra):
                tiles(True, [1 + slot for slot in range(extra)])

        def one_group(group, inner):
            first_slot = 1 + spare + group * GROUP
            tiles(False, [first_slot + slot for slot in range(GROUP)])
            return inner

        lax.fori_loop(0, others // GROUP, one_group, 0)
        for part in range(BLK // ROWS):
            rows = pl.ds(part * ROWS, ROWS)
            o_ref[pl.ds(pl.multiple_of(landing + part * ROWS, ROWS), ROWS), :] = (
                acc_ref[rows, :HD] / acc_ref[rows, HD:]
            ).astype(jnp.bfloat16)
        deliver(turn, own)
        return carry

    lax.fori_loop(0, turns, one_block, 0)
    w_to_partner()
    own_rows.wait()
    arrived(w_all, (HEADS - 1) * W_HALF, wp_recv)
    pltpu.make_async_copy(mix, mix, a_recv).wait()

    def one_tile(tile, carry):
        columns = pl.ds(pl.multiple_of(tile * OUT_TILE, OUT_TILE), OUT_TILE)
        summed = jnp.dot(mix[...], w_all[:, columns], preferred_element_type=jnp.float32)
        out_ref[:, columns] = (hidden[:, columns].astype(jnp.float32) + summed).astype(
            jnp.bfloat16
        )
        return carry

    lax.fori_loop(0, D // OUT_TILE, one_tile, 0)

    arrived(w_all, 30 * W_PART, w_send)
    arrived(w_all, (HEADS - 1) * W_HALF, wp_send)

    def sent(turn, carry):
        delivered(turn, block_of(turn)[0])
        return carry

    lax.fori_loop(0, turns, sent, 0)
    pltpu.make_async_copy(lists.at[1], lists.at[1], l_send).wait()
    for block in range(MOVED):

        @pl.when(heavy & (block < moved))
        def _(block=block):
            arrived(q_ref, BLK, m_send.at[block])

    arrived(x_all, 4 * (2 * LAST - 1) * UNIT, ring_send)
    arrived(kv_all, 3 * TOK, z_send)
    arrived(kv_all, 4 * TOK, s_send)


def layer(lists, hidden, normed, weight, shard, tables):
    vmem = pl.BlockSpec(memory_space=pltpu.VMEM)
    dma = pltpu.SemaphoreType.DMA
    return pl.pallas_call(
        layer_kernel,
        out_shape=jax.ShapeDtypeStruct((PIECE, D), jnp.bfloat16),
        in_specs=[pl.BlockSpec(memory_space=pltpu.SMEM)] + [vmem] * 8,
        out_specs=vmem,
        scratch_shapes=[
            pltpu.VMEM((TOK, D), jnp.bfloat16),
            pltpu.VMEM((SECTIONS * TOK, 2 * HD), jnp.bfloat16),
            pltpu.VMEM((TOK + MOVED * BLK, HD), jnp.bfloat16),
            pltpu.VMEM((BLK, HD), jnp.float32),
            pltpu.VMEM((BLK, 2 * HD), jnp.float32),
            pltpu.VMEM((TOK + MOVED * BLK, HD), jnp.bfloat16),
            pltpu.VMEM((D, D), jnp.bfloat16),
            pltpu.VMEM((PIECE, D), jnp.bfloat16),
            dma,
            dma((2, 2, 2, LAST + 1)),
            dma,
            dma((4, LAST + 1)),
            dma,
            dma((LAST + 1,)),
            dma,
            dma((2, 2)),
            dma,
            dma,
            dma,
            dma((BLOCKS + MOVED, BLK // CHUNK)),
            dma,
            pltpu.SMEM((2, BLOCKS, KSEL), jnp.int32),
            dma,
            dma,
            dma,
            dma((MOVED,)),
            dma((MOVED,)),
        ],
        compiler_params=pltpu.CompilerParams(
            collective_id=0, has_side_effects=True, vmem_limit_bytes=60 << 20
        ),
        name="layer",
    )(lists, hidden, normed, weight, shard, *tables)


def rotary_tables(positions):
    frequency = THETA ** (-(2.0 * jnp.arange(HD // 2, dtype=jnp.float32)) / HD)
    angle = positions.astype(jnp.float32)[:, None] * frequency[None, :]
    cosine, sine = jnp.cos(angle), jnp.sin(angle)
    return jnp.concatenate([cosine, cosine], axis=1), jnp.concatenate([-sine, sine], axis=1)


def local(hidden_in, norm_gain, w_qkv, w_out, block_lists):
    section_id = lax.axis_index("section")
    resid = hidden_in.astype(jnp.float32)
    normed = (
        resid * lax.rsqrt(jnp.mean(resid * resid, axis=-1, keepdims=True) + EPS) * norm_gain
    ).astype(jnp.bfloat16)
    weight = jnp.transpose(w_qkv, (1, 0, 2))
    bases = section_id * TOK + PIECE * jnp.arange(HEADS, dtype=jnp.int32)
    tables = rotary_tables(bases) + rotary_tables(jnp.arange(PIECE, dtype=jnp.int32))
    return layer(block_lists, hidden_in, normed, weight, w_out, tables)


def solution(mesh):
    placed = (
        P(("section", "head"), None),
        P(),
        P(None, None, "head"),
        P("head", None),
        P("section", None),
    )
    return jax.shard_map(
        local, mesh=mesh, in_specs=placed, out_specs=P(("section", "head"), None), check_vma=False
    )
```

```python
import functools
import math

import jax
import jax.numpy as jnp
from jax import lax
from jax.experimental import pallas as pl
from jax.experimental.pallas import tpu as pltpu
from jax.sharding import PartitionSpec as P

D = 2048
HD = 128
BLK = 512
KSEL = 12
NBLK = 48
SECTIONS = 8
HEADS = 16

EPS = 1e-05
THETA = 10000.0
QSCALE = math.log2(math.e) / math.sqrt(HD)
ROWS = 128
GROUP = 4

PIECE = 192
HALF = PIECE // 2
UNIT = HALF // 2
TOK = PIECE * HEADS
STAGES = 6
W_HALF = HD // 2
W_PART = W_HALF // 2
BLOCKS = TOK // BLK
MOVED = 3
OUT_TILE = 256
MESH = pl.DeviceIdType.MESH


def layer_kernel(
    lists_here, hidden, xn, w_ref, shard, cos_b, sin_b, cos_r, sin_r, out_ref,
    x_all, kv_all, q_ref, m_ref, acc_ref, o_ref, w_all, mix, w_two, q_two, kv_two,
    near_recv, far_recv, side_recv, copy_recv, x_send, v_send, v_recv, vp_send, vp_recv,
    rq_send, rk_send, rq_recv, rk_recv, z_send, z_recv, s_send, s_recv,
    w_send, w_recv, wp_send, wp_recv, w_own, a_send, a_recv,
    lists, l_send, l_recv, l_own, m_send, m_recv,
):
    section = lax.axis_index("section")
    head = lax.axis_index("head")
    ypos, xpos = head // 4, head % 4

    def at(across, along):
        return {"section": section, "head": (ypos + across) % 4 * 4 + along}

    xside = xpos + 1 - 2 * (xpos % 2)
    xtwin = (xpos + 3 + 2 * (xpos % 2)) % 4
    up, down, beside, twin = at(1, xpos), at(3, xpos), at(0, xside), at(0, xtwin)
    z_up = {"section": (section + 2) % SECTIONS, "head": head}
    z_down = {"section": (section + SECTIONS - 2) % SECTIONS, "head": head}
    partner = {"section": section + 1 - 2 * (section % 2), "head": head}
    mate_section = SECTIONS - 1 - section
    mate = {"section": mate_section, "head": head}
    heavy = section >= SECTIONS // 2
    moved = (jnp.maximum(section, mate_section) - 1) // 2

    barrier = pltpu.get_barrier_semaphore()
    for device in (z_up, z_down, partner):
        pl.semaphore_signal(barrier, inc=1, device_id=device, device_id_type=MESH)

    def greet(step, carry):
        peer = {"section": section, "head": (head + step) % HEADS}
        pl.semaphore_signal(barrier, inc=1, device_id=peer, device_id_type=MESH)
        return carry

    lax.fori_loop(1, HEADS, greet, 0)

    def greet_mates(step, carry):
        peer = {"section": mate_section, "head": (head + step) % HEADS}
        pl.semaphore_signal(barrier, inc=1, device_id=peer, device_id_type=MESH)
        return carry

    lax.fori_loop(0, HEADS, greet_mates, 0)
    pl.semaphore_wait(barrier, 2 * HEADS + 2)

    def rows_of(start, size):
        return pl.ds(pl.multiple_of(start, 16), size)

    def send(source, target, send_sem, recv_sem, device):
        pltpu.make_async_remote_copy(
            src_ref=source,
            dst_ref=target,
            send_sem=send_sem,
            recv_sem=recv_sem,
            device_id=device,
            device_id_type=MESH,
        ).start()

    def arrived(ref, rows, sem):
        view = ref.at[pl.ds(0, rows), :]
        pltpu.make_async_copy(view, view, sem).wait()

    def units_of(stage, along):
        beyond = along + 1 - 2 * (along % 2)
        if stage == 0:
            places = ((0, along, 0), (0, along, 1))
        elif stage == 1:
            places = ((3, along, 0), (1, along, 1), (0, beyond, 0))
        elif stage == 2:
            places = ((3, along, 1), (1, along, 0), (0, beyond, 1))
        elif stage == 3:
            places = ((2, along, 0), (2, along, 1))
        else:
            part = stage - 4
            places = ((3, beyond, part), (1, beyond, part), (2, beyond, part))
        return [((ypos + across) % 4, column, part) for across, column, part in places]

    def slot_rows(unit):
        row, column, part = unit
        return rows_of((row * 2 + column % 2) * PIECE + part * HALF, HALF)

    def token_start(unit):
        row, column, part = unit
        return (row * 4 + column) * PIECE + part * HALF

    def tokens_of(stage):
        if stage == 0:
            return [xn[...]]
        return [x_all[slot_rows(unit), :] for unit in units_of(stage, xpos)]

    def forward(unit, recv_sem, device, own=False):
        rows = slot_rows(unit)
        part = unit[2]
        source = xn.at[pl.ds(part * HALF, HALF), :] if own else x_all.at[rows, :]
        send(source, x_all.at[rows, :], x_send, recv_sem, device)

    def project(stages, mine):
        tokens = [piece for stage in stages for piece in tokens_of(stage)]
        tokens = tokens[0] if len(tokens) == 1 else jnp.concatenate(tokens, axis=0)
        source = w_ref if mine else w_two
        weight = jnp.concatenate([source[0], source[1], source[2]], axis=1)
        result = jnp.dot(tokens, weight, preferred_element_type=jnp.float32)
        units = [unit for stage in stages for unit in units_of(stage, xpos)]
        for index, unit in enumerate(units):
            row, column, half = unit
            part = result[index * HALF : (index + 1) * HALF]
            place = row * 4 + column
            base_cos, base_sin = cos_b[pl.ds(place, 1), :], sin_b[pl.ds(place, 1), :]
            row_cos = cos_r[half * HALF : (half + 1) * HALF, :]
            row_sin = sin_r[half * HALF : (half + 1) * HALF, :]
            cosine = base_cos * row_cos - base_sin * row_sin
            sine = base_sin * row_cos + base_cos * row_sin
            query, key, value = part[:, :HD], part[:, HD : 2 * HD], part[:, 2 * HD :]
            query = (query * cosine + pltpu.roll(query, HD // 2, 1) * sine) * QSCALE
            key = key * cosine + pltpu.roll(key, HD // 2, 1) * sine
            start = token_start(unit)
            if mine:
                q_ref[rows_of(start, HALF), :] = query.astype(jnp.bfloat16)
                own = rows_of(section * TOK + start, HALF)
                kv_all[own, :HD] = key.astype(jnp.bfloat16)
                kv_all[own, HD:] = value.astype(jnp.bfloat16)
            else:
                q_two[slot_rows(unit), :] = query.astype(jnp.bfloat16)
                kv_two[slot_rows(unit), :HD] = key.astype(jnp.bfloat16)
                kv_two[slot_rows(unit), HD:] = value.astype(jnp.bfloat16)

    def send_home(stage):
        for unit in units_of(stage, xpos):
            start = token_start(unit)
            send(
                kv_two.at[slot_rows(unit), :],
                kv_all.at[rows_of(section * TOK + start, HALF), :],
                rk_send,
                rk_recv.at[stage],
                twin,
            )
            send(
                q_two.at[slot_rows(unit), :],
                q_ref.at[rows_of(start, HALF), :],
                rq_send,
                rq_recv.at[stage],
                twin,
            )

    def came_home(stage):
        count = len(units_of(stage, xtwin)) * HALF
        arrived(kv_all, count, rk_recv.at[stage])
        arrived(q_ref, count, rq_recv.at[stage])

    def batch(index):
        return units_of(index % STAGES, xpos if index < STAGES else xtwin)

    def kv_copy(region, start, size, send_sem, recv_sem, device):
        rows = rows_of(region * TOK + start, size)
        send(kv_all.at[rows, :], kv_all.at[rows, :], send_sem, recv_sem, device)

    def share(index):
        for unit in batch(index):
            start = token_start(unit)
            kv_copy(section, start, HALF, z_send, z_recv.at[0, index], z_up)
            kv_copy(section, start, HALF, z_send, z_recv.at[1, index], z_down)
            kv_copy(section, start, HALF, s_send, s_recv.at[index], partner)

    def relay_near(index):
        below, above = (section + SECTIONS - 2) % SECTIONS, (section + 2) % SECTIONS
        units = batch(index)
        arrived(kv_all, len(units) * HALF, z_recv.at[0, index])
        for unit in units:
            start = token_start(unit)
            kv_copy(below, start, UNIT, z_send, z_recv.at[2, index], z_up)
            kv_copy(below, start, HALF, s_send, s_recv.at[index], partner)
        arrived(kv_all, len(units) * HALF, z_recv.at[1, index])
        for unit in units:
            start = token_start(unit)
            kv_copy(above, start + UNIT, UNIT, z_send, z_recv.at[3, index], z_down)
            kv_copy(above, start, HALF, s_send, s_recv.at[index], partner)

    def relay_far(index):
        across = (section + 4) % SECTIONS
        units = batch(index)
        arrived(kv_all, len(units) * UNIT, z_recv.at[2, index])
        arrived(kv_all, len(units) * UNIT, z_recv.at[3, index])
        for unit in units:
            kv_copy(across, token_start(unit), HALF, s_send, s_recv.at[index], partner)

    core = section % 2
    depth = D // 2

    def twin_rows(part):
        return w_two.at[part, rows_of(core * depth, depth), :]

    for order in range(2):
        forward((ypos, xpos, order), near_recv.at[0, order], up, True)
        forward((ypos, xpos, 1 - order), near_recv.at[1, 1 - order], down, True)
        forward((ypos, xpos, order), side_recv.at[0, order], beside, True)
    for part in range(3):
        send(
            w_ref.at[part, rows_of(core * depth, depth), :],
            twin_rows(part),
            v_send,
            v_recv.at[part],
            twin,
        )
    send(lists_here, lists.at[1], l_send, l_recv, mate)
    own_lists = pltpu.make_async_copy(lists_here, lists.at[0], l_own)
    own_lists.start()
    project([0], True)
    share(0)

    for stage in (1, 2):
        below, above, across = units_of(stage, xpos)
        arrived(x_all, HALF, near_recv.at[0, below[2]])
        if stage == 1:
            forward(below, far_recv.at[0], up)
        arrived(x_all, HALF, near_recv.at[1, above[2]])
        if stage == 1:
            forward(above, far_recv.at[1], down)
        arrived(x_all, HALF, side_recv.at[0, across[2]])
        forward(across, copy_recv.at[0, across[2]], up)
        forward(across, copy_recv.at[1, across[2]], down)
        project([stage], True)
        share(stage)
        relay_near(stage - 1)

    for part in range(3):
        pltpu.make_async_copy(twin_rows(part), twin_rows(part), v_recv.at[part]).wait()
        send(twin_rows(part), twin_rows(part), vp_send, vp_recv.at[part], partner)
    relay_far(0)
    for part in range(3):
        pltpu.make_async_copy(twin_rows(part), twin_rows(part), vp_recv.at[part]).wait()
    project([0, 1, 2], False)
    for stage in range(3):
        send_home(stage)

    for part, unit in enumerate(units_of(3, xpos)):
        arrived(x_all, HALF, far_recv.at[part])
        forward(unit, side_recv.at[1, part], beside)
    project([3], True)
    project([3], False)
    send_home(3)
    share(3)
    relay_near(2)
    relay_far(1)
    for stage in range(3):
        came_home(stage)
        share(STAGES + stage)
    relay_near(3)
    relay_far(2)

    for stage in (4, 5):
        for way in range(2):
            arrived(x_all, HALF, copy_recv.at[way, stage - 4])
        arrived(x_all, HALF, side_recv.at[1, stage - 4])
        project([stage], True)
        share(stage)
        project([stage], False)
        send_home(stage)
        if stage == 4:
            for index in range(STAGES, STAGES + 3):
                relay_near(index)
            relay_far(3)
            came_home(3)
            share(STAGES + 3)

    own_rows = pltpu.make_async_copy(
        shard, w_all.at[rows_of(head * HD, HD), :], w_own
    )
    own_rows.start()
    def w_rows(source, part):
        return rows_of(source * HD + core * W_HALF + part * W_PART, W_PART)

    def line(part, step):
        if part == 0:
            return ypos * 4 + (xpos + step) % 4
        return ((ypos + step) % 4) * 4 + xpos

    def w_copy(source, part, stage, target, own):
        if own:
            view = shard.at[rows_of(core * W_HALF + part * W_PART, W_PART), :]
        else:
            view = w_all.at[w_rows(source, part), :]
        send(
            view,
            w_all.at[w_rows(source, part), :],
            w_send,
            w_recv.at[part, stage],
            {"section": section, "head": target},
        )

    for part in range(2):
        for step in range(1, 4):
            w_copy(head, part, 0, line(part, step), True)

    relay_near(4)
    for index in range(STAGES, STAGES + 3):
        relay_far(index)
    relay_near(STAGES + 3)
    came_home(4)
    share(STAGES + 4)
    for part in range(2):
        arrived(w_all, 3 * W_PART, w_recv.at[part, 0])
        for step in range(1, 4):
            for other in range(4):
                w_copy(line(part, other), part, 1, line(1 - part, step), other == 0)
    relay_near(5)
    relay_far(4)
    relay_far(STAGES + 3)
    came_home(5)
    share(STAGES + 5)

    for block in range(MOVED):

        @pl.when(heavy & (block < moved))
        def _(block=block):
            send(
                q_ref.at[pl.ds(block * BLK, BLK), :],
                q_ref.at[pl.ds(TOK + block * BLK, BLK), :],
                m_send.at[block],
                m_recv.at[block],
                mate,
            )

    relay_near(STAGES + 4)
    relay_far(5)
    relay_near(STAGES + 5)
    relay_far(STAGES + 4)
    relay_far(STAGES + 5)
    for index in range(2 * STAGES):
        arrived(kv_all, 4 * HALF * len(batch(index)), s_recv.at[index])

    def w_to_partner():
        for part in range(2):
            arrived(w_all, 12 * W_PART, w_recv.at[part, 1])

        def one(step, carry):
            rows = rows_of(((head + step) % HEADS) * HD + core * W_HALF, W_HALF)
            send(w_all.at[rows, :], w_all.at[rows, :], wp_send, wp_recv, partner)
            return carry

        lax.fori_loop(1, HEADS, one, 0)

    def copies_of(turn, own, phase):
        base = own % BLOCKS * BLK
        copies = []
        offset, index = 0, 0
        while offset < BLK:
            inside = (phase * BLK + offset) % PIECE
            size = min(PIECE - inside, BLK - offset)
            target = (base + offset) // PIECE
            source = o_ref.at[rows_of(turn * BLK + offset, size), :]
            into = mix.at[head, pl.ds(inside, size), :]
            here = (own // BLOCKS == section) & (target == head)
            copy = pltpu.make_async_remote_copy(
                src_ref=source,
                dst_ref=into,
                send_sem=a_send.at[turn, index],
                recv_sem=a_recv,
                device_id={"section": own // BLOCKS, "head": target},
                device_id_type=MESH,
            )
            copies.append((source, into, here, copy))
            offset, index = offset + size, index + 1
        return copies

    def deliver(turn, own):
        for phase in range(3):

            @pl.when(own % 3 == phase)
            def _(phase=phase):
                for source, into, here, copy in copies_of(turn, own, phase):

                    @pl.when(here)
                    def _(source=source, into=into):
                        pltpu.make_async_copy(source, into, a_recv).start()

                    @pl.when(jnp.logical_not(here))
                    def _(copy=copy):
                        copy.start()

    def delivered(turn, own):
        for phase in range(3):

            @pl.when(own % 3 == phase)
            def _(phase=phase):
                for _, _, here, copy in copies_of(turn, own, phase):

                    @pl.when(jnp.logical_not(here))
                    def _(copy=copy):
                        copy.wait_send()

    own_lists.wait()
    arrived_lists = pltpu.make_async_copy(lists.at[1], lists.at[1], l_recv)
    arrived_lists.wait()
    taken = jnp.where(heavy, 0, moved)
    given = moved - taken
    turns = BLOCKS + taken - given

    for block in range(MOVED):

        @pl.when(block < taken)
        def _(block=block):
            arrived(q_ref, BLK, m_recv.at[block])

    def block_of(turn):
        away = turn < taken
        here = turn - taken + given
        row = jnp.where(away, turn, here)
        side = jnp.where(away, 1, 0)
        own = jnp.where(away, mate_section, section) * BLOCKS + row
        return own, side, row, row * BLK + side * TOK

    ones = jnp.ones((BLK, HD), jnp.bfloat16)

    def one_block(turn, carry):
        own, side, block, base = block_of(turn)
        base = pl.multiple_of(base, BLK)
        landing = pl.multiple_of(turn * BLK, BLK)
        others = (own * (KSEL - 1)) // (NBLK - 1)
        spare = others % GROUP

        def tiles(first, slots):
            sources = [lists[side, block, slot] for slot in slots]
            pairs = [
                (
                    kv_all[pl.ds(source * BLK, BLK), :HD],
                    jnp.concatenate([kv_all[pl.ds(source * BLK, BLK), HD:], ones], axis=1),
                )
                for source in sources
            ]
            for part in range(BLK // ROWS):
                rows = pl.ds(part * ROWS, ROWS)
                query = q_ref[pl.ds(pl.multiple_of(base + part * ROWS, ROWS), ROWS), :]
                keyed = list(pairs)
                if first:
                    seen = (part + 1) * ROWS
                    here = kv_all[pl.ds(own * BLK, seen), :]
                    keyed.append(
                        (here[:, :HD], jnp.concatenate([here[:, HD:], ones[:seen]], axis=1))
                    )
                scores = [
                    lax.dot_general(
                        query, keys, (((1,), (1,)), ((), ())), preferred_element_type=jnp.float32
                    )
                    for keys, _ in keyed
                ]
                if first:
                    row = lax.broadcasted_iota(jnp.int32, (ROWS, seen), 0) + part * ROWS
                    col = lax.broadcasted_iota(jnp.int32, (ROWS, seen), 1)
                    scores[-1] = jnp.where(col <= row, scores[-1], -jnp.inf)
                lanes = [
                    one[:, start : start + HD]
                    for one in scores
                    for start in range(0, one.shape[1], HD)
                ]
                peak = jnp.max(functools.reduce(jnp.maximum, lanes), axis=1, keepdims=True)
                if not first:
                    old = m_ref[rows, :1]
                    peak = jnp.maximum(peak, old)
                update = None
                for one, (_, values) in zip(scores, keyed):
                    weights = jnp.exp2(one - peak).astype(jnp.bfloat16)
                    term = jnp.dot(weights, values, preferred_element_type=jnp.float32)
                    update = term if update is None else update + term
                if first:
                    acc_ref[rows, :] = update
                else:
                    acc_ref[rows, :] = acc_ref[rows, :] * jnp.exp2(old - peak) + update
                m_ref[rows, :] = jnp.broadcast_to(peak, (ROWS, HD))

        for extra in range(GROUP):

            @pl.when(spare == extra)
            def _(extra=extra):
                tiles(True, [1 + slot for slot in range(extra)])

        def one_group(group, inner):
            first_slot = 1 + spare + group * GROUP
            tiles(False, [first_slot + slot for slot in range(GROUP)])
            return inner

        lax.fori_loop(0, others // GROUP, one_group, 0)
        for part in range(BLK // ROWS):
            rows = pl.ds(part * ROWS, ROWS)
            o_ref[pl.ds(pl.multiple_of(landing + part * ROWS, ROWS), ROWS), :] = (
                acc_ref[rows, :HD] / acc_ref[rows, HD:]
            ).astype(jnp.bfloat16)
        deliver(turn, own)
        return carry

    lax.fori_loop(0, turns, one_block, 0)
    w_to_partner()
    own_rows.wait()
    arrived(w_all, (HEADS - 1) * W_HALF, wp_recv)
    pltpu.make_async_copy(mix, mix, a_recv).wait()

    mixed = jnp.concatenate([mix[source] for source in range(HEADS)], axis=1)

    def one_tile(tile, carry):
        columns = pl.ds(pl.multiple_of(tile * OUT_TILE, OUT_TILE), OUT_TILE)
        summed = jnp.dot(mixed, w_all[:, columns], preferred_element_type=jnp.float32)
        out_ref[:, columns] = (hidden[:, columns].astype(jnp.float32) + summed).astype(
            jnp.bfloat16
        )
        return carry

    lax.fori_loop(0, D // OUT_TILE, one_tile, 0)

    arrived(w_all, 30 * W_PART, w_send)
    arrived(w_all, (HEADS - 1) * W_HALF, wp_send)

    def sent(turn, carry):
        delivered(turn, block_of(turn)[0])
        return carry

    lax.fori_loop(0, turns, sent, 0)
    pltpu.make_async_copy(lists.at[1], lists.at[1], l_send).wait()
    for block in range(MOVED):

        @pl.when(heavy & (block < moved))
        def _(block=block):
            arrived(q_ref, BLK, m_send.at[block])

    arrived(x_all, 7 * PIECE, x_send)
    half_two = w_two.at[:, pl.ds(0, depth), :]
    pltpu.make_async_copy(half_two, half_two, v_send).wait()
    pltpu.make_async_copy(half_two, half_two, vp_send).wait()
    arrived(kv_all, TOK // 2, rk_send)
    arrived(q_ref, TOK // 2, rq_send)
    arrived(kv_all, 3 * TOK, z_send)
    arrived(kv_all, 4 * TOK, s_send)


def layer(lists, hidden, normed, weight, shard, tables):
    vmem = pl.BlockSpec(memory_space=pltpu.VMEM)
    dma = pltpu.SemaphoreType.DMA
    return pl.pallas_call(
        layer_kernel,
        out_shape=jax.ShapeDtypeStruct((PIECE, D), jnp.bfloat16),
        in_specs=[pl.BlockSpec(memory_space=pltpu.SMEM)] + [vmem] * 8,
        out_specs=vmem,
        scratch_shapes=[
            pltpu.VMEM((TOK // 2, D), jnp.bfloat16),
            pltpu.VMEM((SECTIONS * TOK, 2 * HD), jnp.bfloat16),
            pltpu.VMEM((TOK + MOVED * BLK, HD), jnp.bfloat16),
            pltpu.VMEM((BLK, HD), jnp.float32),
            pltpu.VMEM((BLK, 2 * HD), jnp.float32),
            pltpu.VMEM((TOK + MOVED * BLK, HD), jnp.bfloat16),
            pltpu.VMEM((D, D), jnp.bfloat16),
            pltpu.VMEM((HEADS, PIECE, HD), jnp.bfloat16),
            pltpu.VMEM((3, D, HD), jnp.bfloat16),
            pltpu.VMEM((TOK // 2, HD), jnp.bfloat16),
            pltpu.VMEM((TOK // 2, 2 * HD), jnp.bfloat16),
            dma((2, 2)),
            dma((2,)),
            dma((2, 2)),
            dma((2, 2)),
            dma,
            dma,
            dma((3,)),
            dma,
            dma((3,)),
            dma,
            dma,
            dma((STAGES,)),
            dma((STAGES,)),
            dma,
            dma((4, 2 * STAGES)),
            dma,
            dma((2 * STAGES,)),
            dma,
            dma((2, 2)),
            dma,
            dma,
            dma,
            dma((BLOCKS + MOVED, 4)),
            dma,
            pltpu.SMEM((2, BLOCKS, KSEL), jnp.int32),
            dma,
            dma,
            dma,
            dma((MOVED,)),
            dma((MOVED,)),
        ],
        compiler_params=pltpu.CompilerParams(
            collective_id=0, has_side_effects=True, vmem_limit_bytes=60 << 20
        ),
        name="layer",
    )(lists, hidden, normed, weight, shard, *tables)


def rotary_tables(positions):
    frequency = THETA ** (-(2.0 * jnp.arange(HD // 2, dtype=jnp.float32)) / HD)
    angle = positions.astype(jnp.float32)[:, None] * frequency[None, :]
    cosine, sine = jnp.cos(angle), jnp.sin(angle)
    return jnp.concatenate([cosine, cosine], axis=1), jnp.concatenate([-sine, sine], axis=1)


def local(hidden_in, norm_gain, w_qkv, w_out, block_lists):
    section_id = lax.axis_index("section")
    resid = hidden_in.astype(jnp.float32)
    normed = (
        resid * lax.rsqrt(jnp.mean(resid * resid, axis=-1, keepdims=True) + EPS) * norm_gain
    ).astype(jnp.bfloat16)
    weight = jnp.transpose(w_qkv, (1, 0, 2))
    bases = section_id * TOK + PIECE * jnp.arange(HEADS, dtype=jnp.int32)
    tables = rotary_tables(bases) + rotary_tables(jnp.arange(PIECE, dtype=jnp.int32))
    return layer(block_lists, hidden_in, normed, weight, w_out, tables)


def solution(mesh):
    placed = (
        P(("section", "head"), None),
        P(),
        P(None, None, "head"),
        P("head", None),
        P("section", None),
    )
    return jax.shard_map(
        local, mesh=mesh, in_specs=placed, out_specs=P(("section", "head"), None), check_vma=False
    )
```

```python
import functools
import math

import jax
import jax.numpy as jnp
import numpy as np
from jax import lax
from jax.experimental import pallas as pl
from jax.experimental.pallas import tpu as pltpu
from jax.sharding import PartitionSpec as P

D = 2048
HD = 128
BLK = 512
KSEL = 12
NBLK = 48
SECTIONS = 8
HEADS = 16

EPS = 1e-05
THETA = 10000.0
QSCALE = math.log2(math.e) / math.sqrt(HD)
ROWS = 128
GROUP = 4

PIECE = 192
HALF = PIECE // 2
UNIT = HALF // 2
TOK = PIECE * HEADS
STAGES = 6
W_HALF = HD // 2
W_PART = W_HALF // 2
BLOCKS = TOK // BLK
MOVED = 3
OUT_TILE = 256
MESH = pl.DeviceIdType.MESH


def layer_kernel(
    lists_here, hidden_in, gain, w_in, shard, cos_b, sin_b, cos_r, sin_r, out_ref,
    hidden, xn, w_ref, in_sems,
    x_all, kv_all, q_ref, m_ref, acc_ref, o_ref, w_all, mix, w_two, q_two, kv_two,
    near_recv, far_recv, side_recv, copy_recv, x_send, v_send, v_recv, vp_send, vp_recv,
    rq_send, rk_send, rq_recv, rk_recv, z_send, z_recv, s_send, s_recv,
    w_send, w_recv, wp_send, wp_recv, w_own, a_send, a_recv,
    lists, l_send, l_recv, l_own, m_send, m_recv,
):
    section = lax.axis_index("section")
    head = lax.axis_index("head")
    ypos, xpos = head // 4, head % 4

    def at(across, along):
        return {"section": section, "head": (ypos + across) % 4 * 4 + along}

    xside = xpos + 1 - 2 * (xpos % 2)
    xtwin = (xpos + 3 + 2 * (xpos % 2)) % 4
    up, down, beside, twin = at(1, xpos), at(3, xpos), at(0, xside), at(0, xtwin)
    z_up = {"section": (section + 2) % SECTIONS, "head": head}
    z_down = {"section": (section + SECTIONS - 2) % SECTIONS, "head": head}
    partner = {"section": section + 1 - 2 * (section % 2), "head": head}
    mate_section = SECTIONS - 1 - section
    mate = {"section": mate_section, "head": head}
    heavy = section >= SECTIONS // 2
    moved = (jnp.maximum(section, mate_section) - 1) // 2

    barrier = pltpu.get_barrier_semaphore()
    for device in (z_up, z_down, partner):
        pl.semaphore_signal(barrier, inc=1, device_id=device, device_id_type=MESH)

    def greet(step, carry):
        peer = {"section": section, "head": (head + step) % HEADS}
        pl.semaphore_signal(barrier, inc=1, device_id=peer, device_id_type=MESH)
        return carry

    lax.fori_loop(1, HEADS, greet, 0)

    def greet_mates(step, carry):
        peer = {"section": mate_section, "head": (head + step) % HEADS}
        pl.semaphore_signal(barrier, inc=1, device_id=peer, device_id_type=MESH)
        return carry

    lax.fori_loop(0, HEADS, greet_mates, 0)
    own_hidden = pltpu.make_async_copy(hidden_in, hidden, in_sems.at[0])
    own_weight = pltpu.make_async_copy(w_in, w_ref, in_sems.at[1])
    own_hidden.start()
    own_weight.start()
    own_hidden.wait()
    resid = hidden[...].astype(jnp.float32)
    spread = jnp.mean(resid * resid, axis=1, keepdims=True)
    xn[...] = (resid * lax.rsqrt(spread + EPS) * gain[...]).astype(jnp.bfloat16)
    pl.semaphore_wait(barrier, 2 * HEADS + 2)

    def rows_of(start, size):
        return pl.ds(pl.multiple_of(start, 16), size)

    def send(source, target, send_sem, recv_sem, device):
        pltpu.make_async_remote_copy(
            src_ref=source,
            dst_ref=target,
            send_sem=send_sem,
            recv_sem=recv_sem,
            device_id=device,
            device_id_type=MESH,
        ).start()

    def arrived(ref, rows, sem):
        view = ref.at[pl.ds(0, rows), :]
        pltpu.make_async_copy(view, view, sem).wait()

    def units_of(stage, along):
        beyond = along + 1 - 2 * (along % 2)
        if stage == 0:
            places = ((0, along, 0), (0, along, 1))
        elif stage == 1:
            places = ((3, along, 0), (1, along, 1), (0, beyond, 0))
        elif stage == 2:
            places = ((3, along, 1), (1, along, 0), (0, beyond, 1))
        elif stage == 3:
            places = ((2, along, 0), (2, along, 1))
        else:
            part = stage - 4
            places = ((3, beyond, part), (1, beyond, part), (2, beyond, part))
        return [((ypos + across) % 4, column, part) for across, column, part in places]

    def slot_rows(unit):
        row, column, part = unit
        return rows_of((row * 2 + column % 2) * PIECE + part * HALF, HALF)

    def token_start(unit):
        row, column, part = unit
        return (row * 4 + column) * PIECE + part * HALF

    def tokens_of(stage):
        if stage == 0:
            return [xn[...]]
        return [x_all[slot_rows(unit), :] for unit in units_of(stage, xpos)]

    def forward(unit, recv_sem, device, own=False):
        rows = slot_rows(unit)
        part = unit[2]
        source = xn.at[pl.ds(part * HALF, HALF), :] if own else x_all.at[rows, :]
        send(source, x_all.at[rows, :], x_send, recv_sem, device)

    def project(stages, mine, wanted=(0, 1, 2)):
        tokens = [piece for stage in stages for piece in tokens_of(stage)]
        tokens = tokens[0] if len(tokens) == 1 else jnp.concatenate(tokens, axis=0)
        source = w_ref if mine else w_two
        weight = [source[part] for part in wanted]
        weight = weight[0] if len(weight) == 1 else jnp.concatenate(weight, axis=1)
        result = jnp.dot(tokens, weight, preferred_element_type=jnp.float32)
        units = [unit for stage in stages for unit in units_of(stage, xpos)]
        for index, unit in enumerate(units):
            row, column, half = unit
            part = result[index * HALF : (index + 1) * HALF]
            parts = {
                name: part[:, place * HD : (place + 1) * HD] for place, name in enumerate(wanted)
            }
            place = section * HEADS + row * 4 + column
            base_cos, base_sin = cos_b[pl.ds(place, 1), :], sin_b[pl.ds(place, 1), :]
            row_cos = cos_r[half * HALF : (half + 1) * HALF, :]
            row_sin = sin_r[half * HALF : (half + 1) * HALF, :]
            cosine = base_cos * row_cos - base_sin * row_sin
            sine = base_sin * row_cos + base_cos * row_sin
            start = token_start(unit)
            if mine:
                q_to, q_rows = q_ref, rows_of(start, HALF)
                kv_to, kv_rows = kv_all, rows_of(section * TOK + start, HALF)
            else:
                q_to, kv_to = q_two, kv_two
                q_rows = kv_rows = slot_rows(unit)
            if 0 in parts:
                query = parts[0]
                query = (query * cosine + pltpu.roll(query, HD // 2, 1) * sine) * QSCALE
                q_to[q_rows, :] = query.astype(jnp.bfloat16)
            if 1 in parts:
                key = parts[1]
                key = key * cosine + pltpu.roll(key, HD // 2, 1) * sine
                kv_to[kv_rows, :HD] = key.astype(jnp.bfloat16)
                kv_to[kv_rows, HD:] = parts[2].astype(jnp.bfloat16)

    def keys_home(stage):
        for unit in units_of(stage, xpos):
            rows = rows_of(section * TOK + token_start(unit), HALF)
            send(
                kv_two.at[slot_rows(unit), :], kv_all.at[rows, :], rk_send, rk_recv.at[stage], twin
            )

    def queries_home(stage):
        for unit in units_of(stage, xpos):
            rows = rows_of(token_start(unit), HALF)
            send(q_two.at[slot_rows(unit), :], q_ref.at[rows, :], rq_send, rq_recv.at[stage], twin)

    def came_home(stage):
        count = len(units_of(stage, xtwin)) * HALF
        arrived(kv_all, count, rk_recv.at[stage])

    def batch(index):
        return units_of(index % STAGES, xpos if index < STAGES else xtwin)

    def kv_copy(region, start, size, send_sem, recv_sem, device):
        rows = rows_of(region * TOK + start, size)
        send(kv_all.at[rows, :], kv_all.at[rows, :], send_sem, recv_sem, device)

    def share(index):
        for unit in batch(index):
            start = token_start(unit)
            kv_copy(section, start, HALF, z_send, z_recv.at[0, index], z_up)
            kv_copy(section, start, HALF, z_send, z_recv.at[1, index], z_down)
            kv_copy(section, start, HALF, s_send, s_recv.at[index], partner)

    def relay_near(index):
        below, above = (section + SECTIONS - 2) % SECTIONS, (section + 2) % SECTIONS
        units = batch(index)
        arrived(kv_all, len(units) * HALF, z_recv.at[0, index])
        for unit in units:
            start = token_start(unit)
            kv_copy(below, start, UNIT, z_send, z_recv.at[2, index], z_up)
            kv_copy(below, start, HALF, s_send, s_recv.at[index], partner)
        arrived(kv_all, len(units) * HALF, z_recv.at[1, index])
        for unit in units:
            start = token_start(unit)
            kv_copy(above, start + UNIT, UNIT, z_send, z_recv.at[3, index], z_down)
            kv_copy(above, start, HALF, s_send, s_recv.at[index], partner)

    def relay_far(index):
        across = (section + 4) % SECTIONS
        units = batch(index)
        arrived(kv_all, len(units) * UNIT, z_recv.at[2, index])
        arrived(kv_all, len(units) * UNIT, z_recv.at[3, index])
        for unit in units:
            kv_copy(across, token_start(unit), HALF, s_send, s_recv.at[index], partner)

    core = section % 2
    depth = D // 2

    def twin_rows(part):
        return w_two.at[part, rows_of(core * depth, depth), :]

    for order in range(2):
        forward((ypos, xpos, order), near_recv.at[0, order], up, True)
        forward((ypos, xpos, 1 - order), near_recv.at[1, 1 - order], down, True)
        forward((ypos, xpos, order), side_recv.at[0, order], beside, True)
    own_weight.wait()
    for part in (1, 2, 0):
        send(
            w_ref.at[part, rows_of(core * depth, depth), :],
            twin_rows(part),
            v_send,
            v_recv.at[part],
            twin,
        )
    send(lists_here, lists.at[1], l_send, l_recv, mate)
    own_lists = pltpu.make_async_copy(lists_here, lists.at[0], l_own)
    own_lists.start()
    own_rows = pltpu.make_async_copy(
        shard, w_all.at[rows_of(head * HD, HD), :], w_own
    )
    own_rows.start()

    def weight_on(part):
        pltpu.make_async_copy(twin_rows(part), twin_rows(part), v_recv.at[part]).wait()
        send(twin_rows(part), twin_rows(part), vp_send, vp_recv.at[part], partner)

    def weight_in(part):
        pltpu.make_async_copy(twin_rows(part), twin_rows(part), vp_recv.at[part]).wait()

    def first_stage(stage):
        below, above, across = units_of(stage, xpos)
        arrived(x_all, HALF, near_recv.at[0, below[2]])
        if stage == 1:
            forward(below, far_recv.at[0], up)
        arrived(x_all, HALF, near_recv.at[1, above[2]])
        if stage == 1:
            forward(above, far_recv.at[1], down)
        arrived(x_all, HALF, side_recv.at[0, across[2]])
        forward(across, copy_recv.at[0, across[2]], up)
        forward(across, copy_recv.at[1, across[2]], down)
        project([stage], True)
        share(stage)

    def last_stage(stage):
        for way in range(2):
            arrived(x_all, HALF, copy_recv.at[way, stage - 4])
        arrived(x_all, HALF, side_recv.at[1, stage - 4])
        project([stage], True)
        share(stage)
        project([stage], False, (1, 2))
        keys_home(stage)

    def bring(stage):
        came_home(stage)
        share(STAGES + stage)

    project([0], True)
    share(0)
    first_stage(1)
    relay_near(0)
    for part in (1, 2):
        weight_on(part)
    for part in (1, 2):
        weight_in(part)
    project([0, 1], False, (1, 2))
    keys_home(0)
    keys_home(1)
    relay_far(0)
    first_stage(2)
    project([2], False, (1, 2))
    keys_home(2)
    weight_on(0)
    relay_near(1)
    bring(0)
    bring(1)
    for part, unit in enumerate(units_of(3, xpos)):
        arrived(x_all, HALF, far_recv.at[part])
        forward(unit, side_recv.at[1, part], beside)
    project([3], True)
    share(3)
    project([3], False, (1, 2))
    keys_home(3)
    bring(2)
    relay_near(2)
    relay_near(STAGES)
    relay_far(1)
    relay_near(STAGES + 1)
    weight_in(0)
    project([0, 1, 2, 3], False, (0,))
    for stage in range(4):
        queries_home(stage)
    relay_near(3)
    relay_near(STAGES + 2)
    bring(3)
    relay_far(2)
    relay_far(STAGES)
    last_stage(4)
    relay_far(STAGES + 1)
    relay_near(STAGES + 3)
    relay_far(3)
    relay_far(STAGES + 2)
    last_stage(5)
    project([4, 5], False, (0,))
    queries_home(4)
    queries_home(5)
    own_rows.wait()
    def w_rows(source, part):
        return rows_of(source * HD + core * W_HALF + part * W_PART, W_PART)

    def line(part, step):
        if part == 0:
            return ypos * 4 + (xpos + step) % 4
        return ((ypos + step) % 4) * 4 + xpos

    def w_copy(source, part, stage, target):
        view = w_all.at[w_rows(source, part), :]
        send(
            view,
            w_all.at[w_rows(source, part), :],
            w_send,
            w_recv.at[part, stage],
            {"section": section, "head": target},
        )

    for part in range(2):
        for step in range(1, 4):
            w_copy(head, part, 0, line(part, step))

    relay_near(4)
    bring(4)
    for part in range(2):
        arrived(w_all, 3 * W_PART, w_recv.at[part, 0])
        for step in range(1, 4):
            for other in range(4):
                w_copy(line(part, other), part, 1, line(1 - part, step))
    relay_near(5)
    relay_far(STAGES + 3)
    relay_far(4)
    bring(5)
    for stage in range(STAGES):
        arrived(q_ref, len(units_of(stage, xtwin)) * HALF, rq_recv.at[stage])

    for block in range(MOVED):

        @pl.when(heavy & (block < moved))
        def _(block=block):
            send(
                q_ref.at[pl.ds(block * BLK, BLK), :],
                q_ref.at[pl.ds(TOK + block * BLK, BLK), :],
                m_send.at[block],
                m_recv.at[block],
                mate,
            )

    relay_near(STAGES + 4)
    relay_far(5)
    relay_near(STAGES + 5)
    relay_far(STAGES + 4)
    relay_far(STAGES + 5)
    for index in range(2 * STAGES):
        arrived(kv_all, 4 * HALF * len(batch(index)), s_recv.at[index])

    def w_to_partner():
        for part in range(2):
            arrived(w_all, 12 * W_PART, w_recv.at[part, 1])

        def one(step, carry):
            rows = rows_of(((head + step) % HEADS) * HD + core * W_HALF, W_HALF)
            send(w_all.at[rows, :], w_all.at[rows, :], wp_send, wp_recv, partner)
            return carry

        lax.fori_loop(1, HEADS, one, 0)

    def copies_of(turn, own, phase):
        base = own % BLOCKS * BLK
        copies = []
        offset, index = 0, 0
        while offset < BLK:
            inside = (phase * BLK + offset) % PIECE
            size = min(PIECE - inside, BLK - offset)
            target = (base + offset) // PIECE
            source = o_ref.at[rows_of(turn * BLK + offset, size), :]
            into = mix.at[head, pl.ds(inside, size), :]
            here = (own // BLOCKS == section) & (target == head)
            copy = pltpu.make_async_remote_copy(
                src_ref=source,
                dst_ref=into,
                send_sem=a_send.at[turn, index],
                recv_sem=a_recv,
                device_id={"section": own // BLOCKS, "head": target},
                device_id_type=MESH,
            )
            copies.append((source, into, here, copy))
            offset, index = offset + size, index + 1
        return copies

    def deliver(turn, own):
        for phase in range(3):

            @pl.when(own % 3 == phase)
            def _(phase=phase):
                for source, into, here, copy in copies_of(turn, own, phase):

                    @pl.when(here)
                    def _(source=source, into=into):
                        pltpu.make_async_copy(source, into, a_recv).start()

                    @pl.when(jnp.logical_not(here))
                    def _(copy=copy):
                        copy.start()

    def delivered(turn, own):
        for phase in range(3):

            @pl.when(own % 3 == phase)
            def _(phase=phase):
                for _, _, here, copy in copies_of(turn, own, phase):

                    @pl.when(jnp.logical_not(here))
                    def _(copy=copy):
                        copy.wait_send()

    own_lists.wait()
    arrived_lists = pltpu.make_async_copy(lists.at[1], lists.at[1], l_recv)
    arrived_lists.wait()
    taken = jnp.where(heavy, 0, moved)
    given = moved - taken
    turns = BLOCKS + taken - given

    for block in range(MOVED):

        @pl.when(block < taken)
        def _(block=block):
            arrived(q_ref, BLK, m_recv.at[block])

    def block_of(turn):
        away = turn < taken
        here = turn - taken + given
        row = jnp.where(away, turn, here)
        side = jnp.where(away, 1, 0)
        own = jnp.where(away, mate_section, section) * BLOCKS + row
        return own, side, row, row * BLK + side * TOK

    ones = jnp.ones((BLK, HD), jnp.bfloat16)

    def one_block(turn, carry):
        own, side, block, base = block_of(turn)
        base = pl.multiple_of(base, BLK)
        landing = pl.multiple_of(turn * BLK, BLK)
        others = (own * (KSEL - 1)) // (NBLK - 1)
        spare = others % GROUP

        def tiles(first, slots):
            sources = [lists[side, block, slot] for slot in slots]
            pairs = [
                (
                    kv_all[pl.ds(source * BLK, BLK), :HD],
                    jnp.concatenate([kv_all[pl.ds(source * BLK, BLK), HD:], ones], axis=1),
                )
                for source in sources
            ]
            for part in range(BLK // ROWS):
                rows = pl.ds(part * ROWS, ROWS)
                query = q_ref[pl.ds(pl.multiple_of(base + part * ROWS, ROWS), ROWS), :]
                keyed = list(pairs)
                if first:
                    seen = (part + 1) * ROWS
                    here = kv_all[pl.ds(own * BLK, seen), :]
                    keyed.append(
                        (here[:, :HD], jnp.concatenate([here[:, HD:], ones[:seen]], axis=1))
                    )
                scores = [
                    lax.dot_general(
                        query, keys, (((1,), (1,)), ((), ())), preferred_element_type=jnp.float32
                    )
                    for keys, _ in keyed
                ]
                if first:
                    row = lax.broadcasted_iota(jnp.int32, (ROWS, seen), 0) + part * ROWS
                    col = lax.broadcasted_iota(jnp.int32, (ROWS, seen), 1)
                    scores[-1] = jnp.where(col <= row, scores[-1], -jnp.inf)
                lanes = [
                    one[:, start : start + HD]
                    for one in scores
                    for start in range(0, one.shape[1], HD)
                ]
                peak = jnp.max(functools.reduce(jnp.maximum, lanes), axis=1, keepdims=True)
                if not first:
                    old = m_ref[rows, :1]
                    peak = jnp.maximum(peak, old)
                update = None
                for one, (_, values) in zip(scores, keyed):
                    weights = jnp.exp2(one - peak).astype(jnp.bfloat16)
                    term = jnp.dot(weights, values, preferred_element_type=jnp.float32)
                    update = term if update is None else update + term
                if first:
                    acc_ref[rows, :] = update
                else:
                    acc_ref[rows, :] = acc_ref[rows, :] * jnp.exp2(old - peak) + update
                m_ref[rows, :] = jnp.broadcast_to(peak, (ROWS, HD))

        for extra in range(GROUP):

            @pl.when(spare == extra)
            def _(extra=extra):
                tiles(True, [1 + slot for slot in range(extra)])

        def one_group(group, inner):
            first_slot = 1 + spare + group * GROUP
            tiles(False, [first_slot + slot for slot in range(GROUP)])
            return inner

        lax.fori_loop(0, others // GROUP, one_group, 0)
        for part in range(BLK // ROWS):
            rows = pl.ds(part * ROWS, ROWS)
            o_ref[pl.ds(pl.multiple_of(landing + part * ROWS, ROWS), ROWS), :] = (
                acc_ref[rows, :HD] / acc_ref[rows, HD:]
            ).astype(jnp.bfloat16)
        deliver(turn, own)
        return carry

    lax.fori_loop(0, turns, one_block, 0)
    w_to_partner()
    arrived(w_all, (HEADS - 1) * W_HALF, wp_recv)
    pltpu.make_async_copy(mix, mix, a_recv).wait()

    mixed = jnp.concatenate([mix[source] for source in range(HEADS)], axis=1)

    def one_tile(tile, carry):
        columns = pl.ds(pl.multiple_of(tile * OUT_TILE, OUT_TILE), OUT_TILE)
        summed = jnp.dot(mixed, w_all[:, columns], preferred_element_type=jnp.float32)
        out_ref[:, columns] = summed
        return carry

    lax.fori_loop(0, D // OUT_TILE, one_tile, 0)

    arrived(w_all, 30 * W_PART, w_send)
    arrived(w_all, (HEADS - 1) * W_HALF, wp_send)

    def sent(turn, carry):
        delivered(turn, block_of(turn)[0])
        return carry

    lax.fori_loop(0, turns, sent, 0)
    pltpu.make_async_copy(lists.at[1], lists.at[1], l_send).wait()
    for block in range(MOVED):

        @pl.when(heavy & (block < moved))
        def _(block=block):
            arrived(q_ref, BLK, m_send.at[block])

    arrived(x_all, 7 * PIECE, x_send)
    half_two = w_two.at[:, pl.ds(0, depth), :]
    pltpu.make_async_copy(half_two, half_two, v_send).wait()
    pltpu.make_async_copy(half_two, half_two, vp_send).wait()
    arrived(kv_all, TOK // 2, rk_send)
    arrived(q_ref, TOK // 2, rq_send)
    arrived(kv_all, 3 * TOK, z_send)
    arrived(kv_all, 4 * TOK, s_send)


def layer(lists, hidden, gain, weight, shard, tables):
    vmem = pl.BlockSpec(memory_space=pltpu.VMEM)
    here = pl.BlockSpec(memory_space=pl.ANY)
    dma = pltpu.SemaphoreType.DMA
    return pl.pallas_call(
        layer_kernel,
        out_shape=jax.ShapeDtypeStruct((PIECE, D), jnp.float32),
        in_specs=[pl.BlockSpec(memory_space=pltpu.SMEM), here, vmem, here, here] + [vmem] * 4,
        out_specs=vmem,
        scratch_shapes=[
            pltpu.VMEM((PIECE, D), jnp.bfloat16),
            pltpu.VMEM((PIECE, D), jnp.bfloat16),
            pltpu.VMEM((3, D, HD), jnp.bfloat16),
            dma((2,)),
            pltpu.VMEM((TOK // 2, D), jnp.bfloat16),
            pltpu.VMEM((SECTIONS * TOK, 2 * HD), jnp.bfloat16),
            pltpu.VMEM((TOK + MOVED * BLK, HD), jnp.bfloat16),
            pltpu.VMEM((BLK, HD), jnp.float32),
            pltpu.VMEM((BLK, 2 * HD), jnp.float32),
            pltpu.VMEM((TOK + MOVED * BLK, HD), jnp.bfloat16),
            pltpu.VMEM((D, D), jnp.bfloat16),
            pltpu.VMEM((HEADS, PIECE, HD), jnp.bfloat16),
            pltpu.VMEM((3, D, HD), jnp.bfloat16),
            pltpu.VMEM((TOK // 2, HD), jnp.bfloat16),
            pltpu.VMEM((TOK // 2, 2 * HD), jnp.bfloat16),
            dma((2, 2)),
            dma((2,)),
            dma((2, 2)),
            dma((2, 2)),
            dma,
            dma,
            dma((3,)),
            dma,
            dma((3,)),
            dma,
            dma,
            dma((STAGES,)),
            dma((STAGES,)),
            dma,
            dma((4, 2 * STAGES)),
            dma,
            dma((2 * STAGES,)),
            dma,
            dma((2, 2)),
            dma,
            dma,
            dma,
            dma((BLOCKS + MOVED, 4)),
            dma,
            pltpu.SMEM((2, BLOCKS, KSEL), jnp.int32),
            dma,
            dma,
            dma,
            dma((MOVED,)),
            dma((MOVED,)),
        ],
        compiler_params=pltpu.CompilerParams(
            collective_id=0, has_side_effects=True, vmem_limit_bytes=60 << 20
        ),
        name="layer",
    )(lists, hidden, gain, weight, shard, *tables)


def rotary_tables(positions):
    frequency = THETA ** (-2.0 * np.arange(HD // 2) / HD)
    angle = positions[:, None] * frequency[None, :]
    cosine, sine = np.cos(angle), np.sin(angle)
    return (
        np.concatenate([cosine, cosine], axis=1).astype(np.float32),
        np.concatenate([-sine, sine], axis=1).astype(np.float32),
    )


def local(hidden_in, norm_gain, w_qkv, w_out, block_lists):
    weight = jnp.transpose(w_qkv, (1, 0, 2))
    bases = rotary_tables(np.arange(SECTIONS * HEADS) * PIECE)
    steps = rotary_tables(np.arange(PIECE))
    gain = norm_gain.reshape(1, D)
    summed = layer(block_lists, hidden_in, gain, weight, w_out, bases + steps)
    return (hidden_in.astype(jnp.float32) + summed).astype(jnp.bfloat16)


def solution(mesh):
    placed = (
        P(("section", "head"), None),
        P(),
        P(None, None, "head"),
        P("head", None),
        P("section", None),
    )
    return jax.shard_map(
        local, mesh=mesh, in_specs=placed, out_specs=P(("section", "head"), None), check_vma=False
    )
```

```python
import functools
import math

import jax
import jax.numpy as jnp
import numpy as np
from jax import lax
from jax.experimental import pallas as pl
from jax.experimental.pallas import tpu as pltpu
from jax.sharding import PartitionSpec as P

D = 2048
HD = 128
BLK = 512
KSEL = 12
NBLK = 48
SECTIONS = 8
HEADS = 16

EPS = 1e-05
THETA = 10000.0
QSCALE = math.log2(math.e) / math.sqrt(HD)
ROWS = 128
GROUP = 4

PIECE = 192
HALF = PIECE // 2
UNIT = HALF // 2
TOK = PIECE * HEADS
STAGES = 6
W_HALF = HD // 2
W_PART = W_HALF // 2
BLOCKS = TOK // BLK
MOVED = 3
OUT_TILE = 256
MESH = pl.DeviceIdType.MESH


def layer_kernel(
    lists_here, hidden_in, gain, w_in, shard, cos_b, sin_b, cos_r, sin_r, out_ref,
    hidden, xn, w_ref, in_sems,
    x_all, kv_all, q_ref, m_ref, acc_ref, o_ref, w_all, mix, w_two, q_two, kv_two,
    near_recv, far_recv, side_recv, copy_recv, x_send, v_send, v_recv, vp_send, vp_recv,
    rq_send, rk_send, rq_recv, rk_recv, z_send, z_recv, s_send, s_recv,
    w_send, w_recv, wp_send, wp_recv, w_own, a_send, a_recv,
    lists, l_send, l_recv, l_own, m_send, m_recv,
):
    section = lax.axis_index("section")
    head = lax.axis_index("head")
    ypos, xpos = head // 4, head % 4

    def at(across, along):
        return {"section": section, "head": (ypos + across) % 4 * 4 + along}

    xside = xpos + 1 - 2 * (xpos % 2)
    xtwin = (xpos + 3 + 2 * (xpos % 2)) % 4
    up, down, beside, twin = at(1, xpos), at(3, xpos), at(0, xside), at(0, xtwin)
    z_up = {"section": (section + 2) % SECTIONS, "head": head}
    z_down = {"section": (section + SECTIONS - 2) % SECTIONS, "head": head}
    partner = {"section": section + 1 - 2 * (section % 2), "head": head}
    mate_section = SECTIONS - 1 - section
    mate = {"section": mate_section, "head": head}
    heavy = section >= SECTIONS // 2
    moved = (jnp.maximum(section, mate_section) - 1) // 2

    barrier = pltpu.get_barrier_semaphore()
    for device in (z_up, z_down, partner):
        pl.semaphore_signal(barrier, inc=1, device_id=device, device_id_type=MESH)

    def greet(step, carry):
        peer = {"section": section, "head": (head + step) % HEADS}
        pl.semaphore_signal(barrier, inc=1, device_id=peer, device_id_type=MESH)
        return carry

    lax.fori_loop(1, HEADS, greet, 0)

    def greet_mates(step, carry):
        peer = {"section": mate_section, "head": (head + step) % HEADS}
        pl.semaphore_signal(barrier, inc=1, device_id=peer, device_id_type=MESH)
        return carry

    lax.fori_loop(0, HEADS, greet_mates, 0)
    own_hidden = pltpu.make_async_copy(hidden_in, hidden, in_sems.at[0])
    own_weight = pltpu.make_async_copy(w_in, w_ref, in_sems.at[1])
    own_hidden.start()
    own_weight.start()
    own_hidden.wait()
    resid = hidden[...].astype(jnp.float32)
    spread = jnp.mean(resid * resid, axis=1, keepdims=True)
    xn[...] = (resid * lax.rsqrt(spread + EPS) * gain[...]).astype(jnp.bfloat16)
    pl.semaphore_wait(barrier, 2 * HEADS + 2)

    def rows_of(start, size):
        return pl.ds(pl.multiple_of(start, 16), size)

    def send(source, target, send_sem, recv_sem, device):
        pltpu.make_async_remote_copy(
            src_ref=source,
            dst_ref=target,
            send_sem=send_sem,
            recv_sem=recv_sem,
            device_id=device,
            device_id_type=MESH,
        ).start()

    def arrived(ref, rows, sem):
        view = ref.at[pl.ds(0, rows), :]
        pltpu.make_async_copy(view, view, sem).wait()

    def units_of(stage, along):
        beyond = along + 1 - 2 * (along % 2)
        if stage == 0:
            places = ((0, along, 0), (0, along, 1))
        elif stage == 1:
            places = ((3, along, 0), (1, along, 1), (0, beyond, 0))
        elif stage == 2:
            places = ((3, along, 1), (1, along, 0), (0, beyond, 1))
        elif stage == 3:
            places = ((2, along, 0), (2, along, 1))
        else:
            part = stage - 4
            places = ((3, beyond, part), (1, beyond, part), (2, beyond, part))
        return [((ypos + across) % 4, column, part) for across, column, part in places]

    def slot_rows(unit):
        row, column, part = unit
        return rows_of((row * 2 + column % 2) * PIECE + part * HALF, HALF)

    def token_start(unit):
        row, column, part = unit
        return (row * 4 + column) * PIECE + part * HALF

    def tokens_of(stage):
        if stage == 0:
            return [xn[...]]
        return [x_all[slot_rows(unit), :] for unit in units_of(stage, xpos)]

    def forward(unit, recv_sem, device, own=False):
        rows = slot_rows(unit)
        part = unit[2]
        source = xn.at[pl.ds(part * HALF, HALF), :] if own else x_all.at[rows, :]
        send(source, x_all.at[rows, :], x_send, recv_sem, device)

    def project(stages, mine, wanted=(0, 1, 2)):
        tokens = [piece for stage in stages for piece in tokens_of(stage)]
        tokens = tokens[0] if len(tokens) == 1 else jnp.concatenate(tokens, axis=0)
        source = w_ref if mine else w_two
        weight = [source[part] for part in wanted]
        weight = weight[0] if len(weight) == 1 else jnp.concatenate(weight, axis=1)
        result = jnp.dot(tokens, weight, preferred_element_type=jnp.float32)
        units = [unit for stage in stages for unit in units_of(stage, xpos)]
        for index, unit in enumerate(units):
            row, column, half = unit
            part = result[index * HALF : (index + 1) * HALF]
            parts = {
                name: part[:, place * HD : (place + 1) * HD] for place, name in enumerate(wanted)
            }
            place = section * HEADS + row * 4 + column
            base_cos, base_sin = cos_b[pl.ds(place, 1), :], sin_b[pl.ds(place, 1), :]
            row_cos = cos_r[half * HALF : (half + 1) * HALF, :]
            row_sin = sin_r[half * HALF : (half + 1) * HALF, :]
            cosine = base_cos * row_cos - base_sin * row_sin
            sine = base_sin * row_cos + base_cos * row_sin
            start = token_start(unit)
            if mine:
                q_to, q_rows = q_ref, rows_of(start, HALF)
                kv_to, kv_rows = kv_all, rows_of(section * TOK + start, HALF)
            else:
                q_to, kv_to = q_two, kv_two
                q_rows = kv_rows = slot_rows(unit)
            if 0 in parts:
                query = parts[0]
                query = (query * cosine + pltpu.roll(query, HD // 2, 1) * sine) * QSCALE
                q_to[q_rows, :] = query.astype(jnp.bfloat16)
            if 1 in parts:
                key = parts[1]
                key = key * cosine + pltpu.roll(key, HD // 2, 1) * sine
                kv_to[kv_rows, :HD] = key.astype(jnp.bfloat16)
                kv_to[kv_rows, HD:] = parts[2].astype(jnp.bfloat16)

    def keys_home(stage):
        for unit in units_of(stage, xpos):
            rows = rows_of(section * TOK + token_start(unit), HALF)
            send(
                kv_two.at[slot_rows(unit), :], kv_all.at[rows, :], rk_send, rk_recv.at[stage], twin
            )

    def queries_home(stage):
        for unit in units_of(stage, xpos):
            rows = rows_of(token_start(unit), HALF)
            send(q_two.at[slot_rows(unit), :], q_ref.at[rows, :], rq_send, rq_recv.at[stage], twin)

    def came_home(stage):
        count = len(units_of(stage, xtwin)) * HALF
        arrived(kv_all, count, rk_recv.at[stage])

    def batch(index):
        return units_of(index % STAGES, xpos if index < STAGES else xtwin)

    def kv_copy(region, start, size, send_sem, recv_sem, device):
        rows = rows_of(region * TOK + start, size)
        send(kv_all.at[rows, :], kv_all.at[rows, :], send_sem, recv_sem, device)

    def share(index):
        for unit in batch(index):
            start = token_start(unit)
            kv_copy(section, start, HALF, z_send, z_recv.at[0, index], z_up)
            kv_copy(section, start, HALF, z_send, z_recv.at[1, index], z_down)
            kv_copy(section, start, HALF, s_send, s_recv.at[index], partner)

    def relay_near(index):
        below, above = (section + SECTIONS - 2) % SECTIONS, (section + 2) % SECTIONS
        units = batch(index)
        arrived(kv_all, len(units) * HALF, z_recv.at[0, index])
        for unit in units:
            start = token_start(unit)
            kv_copy(below, start, UNIT, z_send, z_recv.at[2, index], z_up)
            kv_copy(below, start, HALF, s_send, s_recv.at[index], partner)
        arrived(kv_all, len(units) * HALF, z_recv.at[1, index])
        for unit in units:
            start = token_start(unit)
            kv_copy(above, start + UNIT, UNIT, z_send, z_recv.at[3, index], z_down)
            kv_copy(above, start, HALF, s_send, s_recv.at[index], partner)

    def relay_far(index):
        across = (section + 4) % SECTIONS
        units = batch(index)
        arrived(kv_all, len(units) * UNIT, z_recv.at[2, index])
        arrived(kv_all, len(units) * UNIT, z_recv.at[3, index])
        for unit in units:
            kv_copy(across, token_start(unit), HALF, s_send, s_recv.at[index], partner)

    core = section % 2
    depth = D // 2

    def twin_rows(part):
        return w_two.at[part, rows_of(core * depth, depth), :]

    for order in range(2):
        forward((ypos, xpos, order), near_recv.at[0, order], up, True)
        forward((ypos, xpos, 1 - order), near_recv.at[1, 1 - order], down, True)
        forward((ypos, xpos, order), side_recv.at[0, order], beside, True)
    own_weight.wait()
    for part in (1, 2, 0):
        send(
            w_ref.at[part, rows_of(core * depth, depth), :],
            twin_rows(part),
            v_send,
            v_recv.at[part],
            twin,
        )
    send(lists_here, lists.at[1], l_send, l_recv, mate)
    own_lists = pltpu.make_async_copy(lists_here, lists.at[0], l_own)
    own_lists.start()
    own_rows = pltpu.make_async_copy(
        shard, w_all.at[rows_of(head * HD, HD), :], w_own
    )
    own_rows.start()

    def weight_on(part):
        pltpu.make_async_copy(twin_rows(part), twin_rows(part), v_recv.at[part]).wait()
        send(twin_rows(part), twin_rows(part), vp_send, vp_recv.at[part], partner)

    def weight_in(part):
        pltpu.make_async_copy(twin_rows(part), twin_rows(part), vp_recv.at[part]).wait()

    def first_stage(stage):
        below, above, across = units_of(stage, xpos)
        arrived(x_all, HALF, near_recv.at[0, below[2]])
        if stage == 1:
            forward(below, far_recv.at[0], up)
        arrived(x_all, HALF, near_recv.at[1, above[2]])
        if stage == 1:
            forward(above, far_recv.at[1], down)
        arrived(x_all, HALF, side_recv.at[0, across[2]])
        forward(across, copy_recv.at[0, across[2]], up)
        forward(across, copy_recv.at[1, across[2]], down)
        project([stage], True)
        share(stage)

    def w_rows(source, part):
        return rows_of(source * HD + core * W_HALF + part * W_PART, W_PART)

    def line(part, step):
        if part == 0:
            return ypos * 4 + (xpos + step) % 4
        return ((ypos + step) % 4) * 4 + xpos

    def w_copy(source, part, stage, target):
        view = w_all.at[w_rows(source, part), :]
        send(
            view,
            w_all.at[w_rows(source, part), :],
            w_send,
            w_recv.at[part, stage],
            {"section": section, "head": target},
        )

    def w_near():
        own_rows.wait()
        for part in range(2):
            for step in range(1, 4):
                w_copy(head, part, 0, line(part, step))

    def last_stage(stage):
        for way in range(2):
            arrived(x_all, HALF, copy_recv.at[way, stage - 4])
        arrived(x_all, HALF, side_recv.at[1, stage - 4])
        if stage == 5:
            w_near()
        project([stage], True)
        share(stage)
        project([stage], False, (1, 2))
        keys_home(stage)

    def bring(stage):
        came_home(stage)
        share(STAGES + stage)

    project([0], True)
    share(0)
    first_stage(1)
    relay_near(0)
    for part in (1, 2):
        weight_on(part)
    for part in (1, 2):
        weight_in(part)
    project([0, 1], False, (1, 2))
    keys_home(0)
    keys_home(1)
    relay_far(0)
    first_stage(2)
    project([2], False, (1, 2))
    keys_home(2)
    weight_on(0)
    relay_near(1)
    bring(0)
    bring(1)
    for part, unit in enumerate(units_of(3, xpos)):
        arrived(x_all, HALF, far_recv.at[part])
        forward(unit, side_recv.at[1, part], beside)
    project([3], True)
    share(3)
    project([3], False, (1, 2))
    keys_home(3)
    bring(2)
    relay_near(2)
    relay_near(STAGES)
    relay_far(1)
    relay_near(STAGES + 1)
    weight_in(0)
    project([0, 1, 2, 3], False, (0,))
    for stage in range(4):
        queries_home(stage)
    relay_near(3)
    relay_near(STAGES + 2)
    bring(3)
    relay_far(2)
    relay_far(STAGES)
    last_stage(4)
    relay_far(STAGES + 1)
    relay_near(STAGES + 3)
    relay_far(3)
    relay_far(STAGES + 2)
    last_stage(5)
    project([4, 5], False, (0,))
    queries_home(4)
    queries_home(5)
    relay_near(4)
    bring(4)
    for part in range(2):
        arrived(w_all, 3 * W_PART, w_recv.at[part, 0])
        for step in range(1, 4):
            for other in range(4):
                w_copy(line(part, other), part, step, line(1 - part, step))
    relay_near(5)
    relay_far(STAGES + 3)
    relay_far(4)
    bring(5)
    for stage in range(STAGES):
        arrived(q_ref, len(units_of(stage, xtwin)) * HALF, rq_recv.at[stage])

    for block in range(MOVED):

        @pl.when(heavy & (block < moved))
        def _(block=block):
            send(
                q_ref.at[pl.ds(block * BLK, BLK), :],
                q_ref.at[pl.ds(TOK + block * BLK, BLK), :],
                m_send.at[block],
                m_recv.at[block],
                mate,
            )

    relay_near(STAGES + 4)
    relay_far(5)
    relay_near(STAGES + 5)
    relay_far(STAGES + 4)
    relay_far(STAGES + 5)
    for index in range(2 * STAGES):
        arrived(kv_all, 4 * HALF * len(batch(index)), s_recv.at[index])

    def w_to_partner(source, part):
        rows = w_rows(source, part)
        send(w_all.at[rows, :], w_all.at[rows, :], wp_send, wp_recv, partner)

    def w_near_to_partner():
        for part in range(2):
            for step in range(1, 4):
                w_to_partner(line(part, step), part)

    def w_far_to_partner(step):
        for part in range(2):
            arrived(w_all, 4 * W_PART, w_recv.at[part, step])
            for other in range(4):
                if part == 0:
                    source = (ypos + 4 - step) % 4 * 4 + other
                else:
                    source = other * 4 + (xpos + 4 - step) % 4
                w_to_partner(source, part)

    def copies_of(turn, own, phase):
        base = own % BLOCKS * BLK
        copies = []
        offset, index = 0, 0
        while offset < BLK:
            inside = (phase * BLK + offset) % PIECE
            size = min(PIECE - inside, BLK - offset)
            target = (base + offset) // PIECE
            source = o_ref.at[rows_of(turn * BLK + offset, size), :]
            into = mix.at[head, pl.ds(inside, size), :]
            here = (own // BLOCKS == section) & (target == head)
            copy = pltpu.make_async_remote_copy(
                src_ref=source,
                dst_ref=into,
                send_sem=a_send.at[turn, index],
                recv_sem=a_recv,
                device_id={"section": own // BLOCKS, "head": target},
                device_id_type=MESH,
            )
            copies.append((source, into, here, copy))
            offset, index = offset + size, index + 1
        return copies

    def deliver(turn, own):
        for phase in range(3):

            @pl.when(own % 3 == phase)
            def _(phase=phase):
                for source, into, here, copy in copies_of(turn, own, phase):

                    @pl.when(here)
                    def _(source=source, into=into):
                        pltpu.make_async_copy(source, into, a_recv).start()

                    @pl.when(jnp.logical_not(here))
                    def _(copy=copy):
                        copy.start()

    def delivered(turn, own):
        for phase in range(3):

            @pl.when(own % 3 == phase)
            def _(phase=phase):
                for _, _, here, copy in copies_of(turn, own, phase):

                    @pl.when(jnp.logical_not(here))
                    def _(copy=copy):
                        copy.wait_send()

    own_lists.wait()
    arrived_lists = pltpu.make_async_copy(lists.at[1], lists.at[1], l_recv)
    arrived_lists.wait()
    taken = jnp.where(heavy, 0, moved)
    given = moved - taken
    turns = BLOCKS + taken - given

    kept = BLOCKS - given

    def block_of(turn):
        away = turn >= kept
        here = given + (turn + head) % kept
        there = (jnp.maximum(turn - kept, 0) + head) % jnp.maximum(taken, 1)
        row = jnp.where(away, there, here)
        side = jnp.where(away, 1, 0)
        own = jnp.where(away, mate_section, section) * BLOCKS + row
        return own, side, row, row * BLK + side * TOK

    ones = jnp.ones((BLK, HD), jnp.bfloat16)

    def one_block(turn, carry):
        own, side, block, base = block_of(turn)
        base = pl.multiple_of(base, BLK)
        landing = pl.multiple_of(turn * BLK, BLK)

        @pl.when(turn >= kept)
        def _():
            arrived(q_ref, BLK, m_recv.at[block])

        others = (own * (KSEL - 1)) // (NBLK - 1)
        spare = others % GROUP

        def tiles(first, slots):
            sources = [lists[side, block, slot] for slot in slots]
            pairs = [
                (
                    kv_all[pl.ds(source * BLK, BLK), :HD],
                    jnp.concatenate([kv_all[pl.ds(source * BLK, BLK), HD:], ones], axis=1),
                )
                for source in sources
            ]
            for part in range(BLK // ROWS):
                rows = pl.ds(part * ROWS, ROWS)
                query = q_ref[pl.ds(pl.multiple_of(base + part * ROWS, ROWS), ROWS), :]
                keyed = list(pairs)
                if first:
                    seen = (part + 1) * ROWS
                    here = kv_all[pl.ds(own * BLK, seen), :]
                    keyed.append(
                        (here[:, :HD], jnp.concatenate([here[:, HD:], ones[:seen]], axis=1))
                    )
                scores = [
                    lax.dot_general(
                        query, keys, (((1,), (1,)), ((), ())), preferred_element_type=jnp.float32
                    )
                    for keys, _ in keyed
                ]
                if first:
                    row = lax.broadcasted_iota(jnp.int32, (ROWS, seen), 0) + part * ROWS
                    col = lax.broadcasted_iota(jnp.int32, (ROWS, seen), 1)
                    scores[-1] = jnp.where(col <= row, scores[-1], -jnp.inf)
                lanes = [
                    one[:, start : start + HD]
                    for one in scores
                    for start in range(0, one.shape[1], HD)
                ]
                peak = jnp.max(functools.reduce(jnp.maximum, lanes), axis=1, keepdims=True)
                if not first:
                    old = m_ref[rows, :1]
                    peak = jnp.maximum(peak, old)
                update = None
                for one, (_, values) in zip(scores, keyed):
                    weights = jnp.exp2(one - peak).astype(jnp.bfloat16)
                    term = jnp.dot(weights, values, preferred_element_type=jnp.float32)
                    update = term if update is None else update + term
                if first:
                    acc_ref[rows, :] = update
                else:
                    acc_ref[rows, :] = acc_ref[rows, :] * jnp.exp2(old - peak) + update
                m_ref[rows, :] = jnp.broadcast_to(peak, (ROWS, HD))

        for extra in range(GROUP):

            @pl.when(spare == extra)
            def _(extra=extra):
                tiles(True, [1 + slot for slot in range(extra)])

        def one_group(group, inner):
            first_slot = 1 + spare + group * GROUP
            tiles(False, [first_slot + slot for slot in range(GROUP)])
            return inner

        lax.fori_loop(0, others // GROUP, one_group, 0)
        for part in range(BLK // ROWS):
            rows = pl.ds(part * ROWS, ROWS)
            o_ref[pl.ds(pl.multiple_of(landing + part * ROWS, ROWS), ROWS), :] = (
                acc_ref[rows, :HD] / acc_ref[rows, HD:]
            ).astype(jnp.bfloat16)
        deliver(turn, own)

        @pl.when(turn == turns - 3)
        def _():
            w_near_to_partner()

        @pl.when(turn == turns - 2)
        def _():
            w_far_to_partner(1)
            w_far_to_partner(3)

        return carry

    lax.fori_loop(0, turns, one_block, 0)
    w_far_to_partner(2)
    arrived(w_all, (HEADS - 1) * W_HALF, wp_recv)
    pltpu.make_async_copy(mix, mix, a_recv).wait()

    mixed = jnp.concatenate([mix[source] for source in range(HEADS)], axis=1)

    def one_tile(tile, carry):
        columns = pl.ds(pl.multiple_of(tile * OUT_TILE, OUT_TILE), OUT_TILE)
        summed = jnp.dot(mixed, w_all[:, columns], preferred_element_type=jnp.float32)
        out_ref[:, columns] = (hidden[:, columns].astype(jnp.float32) + summed).astype(
            jnp.bfloat16
        )
        return carry

    lax.fori_loop(0, D // OUT_TILE, one_tile, 0)

    arrived(w_all, 30 * W_PART, w_send)
    arrived(w_all, (HEADS - 1) * W_HALF, wp_send)

    def sent(turn, carry):
        delivered(turn, block_of(turn)[0])
        return carry

    lax.fori_loop(0, turns, sent, 0)
    pltpu.make_async_copy(lists.at[1], lists.at[1], l_send).wait()
    for block in range(MOVED):

        @pl.when(heavy & (block < moved))
        def _(block=block):
            arrived(q_ref, BLK, m_send.at[block])

    arrived(x_all, 7 * PIECE, x_send)
    half_two = w_two.at[:, pl.ds(0, depth), :]
    pltpu.make_async_copy(half_two, half_two, v_send).wait()
    pltpu.make_async_copy(half_two, half_two, vp_send).wait()
    arrived(kv_all, TOK // 2, rk_send)
    arrived(q_ref, TOK // 2, rq_send)
    arrived(kv_all, 3 * TOK, z_send)
    arrived(kv_all, 4 * TOK, s_send)


def layer(lists, hidden, gain, weight, shard, tables):
    vmem = pl.BlockSpec(memory_space=pltpu.VMEM)
    here = pl.BlockSpec(memory_space=pl.ANY)
    dma = pltpu.SemaphoreType.DMA
    return pl.pallas_call(
        layer_kernel,
        out_shape=jax.ShapeDtypeStruct((PIECE, D), jnp.bfloat16),
        in_specs=[pl.BlockSpec(memory_space=pltpu.SMEM), here, vmem, here, here] + [vmem] * 4,
        out_specs=vmem,
        scratch_shapes=[
            pltpu.VMEM((PIECE, D), jnp.bfloat16),
            pltpu.VMEM((PIECE, D), jnp.bfloat16),
            pltpu.VMEM((3, D, HD), jnp.bfloat16),
            dma((2,)),
            pltpu.VMEM((TOK // 2, D), jnp.bfloat16),
            pltpu.VMEM((SECTIONS * TOK, 2 * HD), jnp.bfloat16),
            pltpu.VMEM((TOK + MOVED * BLK, HD), jnp.bfloat16),
            pltpu.VMEM((BLK, HD), jnp.float32),
            pltpu.VMEM((BLK, 2 * HD), jnp.float32),
            pltpu.VMEM((TOK + MOVED * BLK, HD), jnp.bfloat16),
            pltpu.VMEM((D, D), jnp.bfloat16),
            pltpu.VMEM((HEADS, PIECE, HD), jnp.bfloat16),
            pltpu.VMEM((3, D, HD), jnp.bfloat16),
            pltpu.VMEM((TOK // 2, HD), jnp.bfloat16),
            pltpu.VMEM((TOK // 2, 2 * HD), jnp.bfloat16),
            dma((2, 2)),
            dma((2,)),
            dma((2, 2)),
            dma((2, 2)),
            dma,
            dma,
            dma((3,)),
            dma,
            dma((3,)),
            dma,
            dma,
            dma((STAGES,)),
            dma((STAGES,)),
            dma,
            dma((4, 2 * STAGES)),
            dma,
            dma((2 * STAGES,)),
            dma,
            dma((2, 4)),
            dma,
            dma,
            dma,
            dma((BLOCKS + MOVED, 4)),
            dma,
            pltpu.SMEM((2, BLOCKS, KSEL), jnp.int32),
            dma,
            dma,
            dma,
            dma((MOVED,)),
            dma((MOVED,)),
        ],
        compiler_params=pltpu.CompilerParams(
            collective_id=0, has_side_effects=True, vmem_limit_bytes=60 << 20
        ),
        name="layer",
    )(lists, hidden, gain, weight, shard, *tables)


def rotary_tables(positions):
    frequency = THETA ** (-2.0 * np.arange(HD // 2) / HD)
    angle = positions[:, None] * frequency[None, :]
    cosine, sine = np.cos(angle), np.sin(angle)
    return (
        np.concatenate([cosine, cosine], axis=1).astype(np.float32),
        np.concatenate([-sine, sine], axis=1).astype(np.float32),
    )


def local(hidden_in, norm_gain, w_qkv, w_out, block_lists):
    weight = jnp.transpose(w_qkv, (1, 0, 2))
    bases = rotary_tables(np.arange(SECTIONS * HEADS) * PIECE)
    steps = rotary_tables(np.arange(PIECE))
    gain = norm_gain.reshape(1, D)
    return layer(block_lists, hidden_in, gain, weight, w_out, bases + steps)


def solution(mesh):
    placed = (
        P(("section", "head"), None),
        P(),
        P(None, None, "head"),
        P("head", None),
        P("section", None),
    )
    return jax.shard_map(
        local, mesh=mesh, in_specs=placed, out_specs=P(("section", "head"), None), check_vma=False
    )
```

```python
import functools
import math

import jax
import jax.numpy as jnp
import numpy as np
from jax import lax
from jax.experimental import pallas as pl
from jax.experimental.pallas import tpu as pltpu
from jax.sharding import PartitionSpec as P

D = 2048
HD = 128
BLK = 512
KSEL = 12
NBLK = 48
SECTIONS = 8
HEADS = 16

EPS = 1e-05
THETA = 10000.0
QSCALE = math.log2(math.e) / math.sqrt(HD)
ROWS = 128
GROUP = 4

PIECE = 192
HALF = PIECE // 2
UNIT = HALF // 2
TOK = PIECE * HEADS
STAGES = 6
W_HALF = HD // 2
W_PART = W_HALF // 4
BLOCKS = TOK // BLK
MOVED = 3
OUT_TILE = 256
MESH = pl.DeviceIdType.MESH


def layer_kernel(
    lists_here, hidden_in, gain, w_in, shard, cos_b, sin_b, cos_r, sin_r, out_ref,
    hidden, xn, w_ref, in_sems,
    x_all, kv_all, q_ref, m_ref, acc_ref, o_ref, w_all, mix, w_two, q_two, kv_two,
    near_recv, far_recv, side_recv, copy_recv, x_send, v_send, v_recv, vp_send, vp_recv,
    rq_send, rk_send, rq_recv, rk_recv, z_send, z_recv, s_send, s_recv,
    w_send, w_recv, wz_recv, wp_send, wp_recv, w_own, a_send, a_recv,
    lists, l_send, l_recv, l_own, m_send, m_recv,
):
    section = lax.axis_index("section")
    head = lax.axis_index("head")
    ypos, xpos = head // 4, head % 4

    def at(across, along):
        return {"section": section, "head": (ypos + across) % 4 * 4 + along}

    xside = xpos + 1 - 2 * (xpos % 2)
    xtwin = (xpos + 3 + 2 * (xpos % 2)) % 4
    up, down, beside, twin = at(1, xpos), at(3, xpos), at(0, xside), at(0, xtwin)
    z_up = {"section": (section + 2) % SECTIONS, "head": head}
    z_down = {"section": (section + SECTIONS - 2) % SECTIONS, "head": head}
    partner = {"section": section + 1 - 2 * (section % 2), "head": head}
    mate_section = SECTIONS - 1 - section
    mate = {"section": mate_section, "head": head}
    heavy = section >= SECTIONS // 2
    moved = (jnp.maximum(section, mate_section) - 1) // 2

    own_hidden = pltpu.make_async_copy(hidden_in, hidden, in_sems.at[0])
    own_weight = pltpu.make_async_copy(w_in, w_ref, in_sems.at[1])
    own_hidden.start()
    own_weight.start()

    barrier = pltpu.get_barrier_semaphore()
    for device in (z_up, z_down, partner):
        pl.semaphore_signal(barrier, inc=1, device_id=device, device_id_type=MESH)

    def greet(step, carry):
        peer = {"section": section, "head": (head + step) % HEADS}
        pl.semaphore_signal(barrier, inc=1, device_id=peer, device_id_type=MESH)
        return carry

    lax.fori_loop(1, HEADS, greet, 0)

    def greet_mates(step, carry):
        peer = {"section": mate_section, "head": (head + step) % HEADS}
        pl.semaphore_signal(barrier, inc=1, device_id=peer, device_id_type=MESH)
        return carry

    lax.fori_loop(0, HEADS, greet_mates, 0)
    own_hidden.wait()
    resid = hidden[...].astype(jnp.float32)
    spread = jnp.mean(resid * resid, axis=1, keepdims=True)
    xn[...] = (resid * lax.rsqrt(spread + EPS) * gain[...]).astype(jnp.bfloat16)
    pl.semaphore_wait(barrier, 2 * HEADS + 2)

    def rows_of(start, size):
        return pl.ds(pl.multiple_of(start, 16), size)

    def send(source, target, send_sem, recv_sem, device):
        pltpu.make_async_remote_copy(
            src_ref=source,
            dst_ref=target,
            send_sem=send_sem,
            recv_sem=recv_sem,
            device_id=device,
            device_id_type=MESH,
        ).start()

    def arrived(ref, rows, sem):
        view = ref.at[pl.ds(0, rows), :]
        pltpu.make_async_copy(view, view, sem).wait()

    def units_of(stage, along):
        beyond = along + 1 - 2 * (along % 2)
        if stage == 0:
            places = ((0, along, 0), (0, along, 1))
        elif stage == 1:
            places = ((3, along, 0), (1, along, 1), (0, beyond, 0))
        elif stage == 2:
            places = ((3, along, 1), (1, along, 0), (0, beyond, 1))
        elif stage == 3:
            places = ((2, along, 0), (2, along, 1))
        else:
            part = stage - 4
            places = ((3, beyond, part), (1, beyond, part), (2, beyond, part))
        return [((ypos + across) % 4, column, part) for across, column, part in places]

    def slot_rows(unit):
        row, column, part = unit
        return rows_of((row * 2 + column % 2) * PIECE + part * HALF, HALF)

    def token_start(unit):
        row, column, part = unit
        return (row * 4 + column) * PIECE + part * HALF

    def tokens_of(stage):
        if stage == 0:
            return [xn[...]]
        return [x_all[slot_rows(unit), :] for unit in units_of(stage, xpos)]

    def forward(unit, recv_sem, device, own=False):
        rows = slot_rows(unit)
        part = unit[2]
        source = xn.at[pl.ds(part * HALF, HALF), :] if own else x_all.at[rows, :]
        send(source, x_all.at[rows, :], x_send, recv_sem, device)

    def project(stages, mine, wanted=(0, 1, 2)):
        tokens = [piece for stage in stages for piece in tokens_of(stage)]
        tokens = tokens[0] if len(tokens) == 1 else jnp.concatenate(tokens, axis=0)
        source = w_ref if mine else w_two
        weight = [source[part] for part in wanted]
        weight = weight[0] if len(weight) == 1 else jnp.concatenate(weight, axis=1)
        result = jnp.dot(tokens, weight, preferred_element_type=jnp.float32)
        units = [unit for stage in stages for unit in units_of(stage, xpos)]
        for index, unit in enumerate(units):
            row, column, half = unit
            part = result[index * HALF : (index + 1) * HALF]
            parts = {
                name: part[:, place * HD : (place + 1) * HD] for place, name in enumerate(wanted)
            }
            place = section * HEADS + row * 4 + column
            base_cos, base_sin = cos_b[pl.ds(place, 1), :], sin_b[pl.ds(place, 1), :]
            row_cos = cos_r[half * HALF : (half + 1) * HALF, :]
            row_sin = sin_r[half * HALF : (half + 1) * HALF, :]
            cosine = base_cos * row_cos - base_sin * row_sin
            sine = base_sin * row_cos + base_cos * row_sin
            start = token_start(unit)
            if mine:
                q_to, q_rows = q_ref, rows_of(start, HALF)
                kv_to, kv_rows = kv_all, rows_of(section * TOK + start, HALF)
            else:
                q_to, kv_to = q_two, kv_two
                q_rows = kv_rows = slot_rows(unit)
            if 0 in parts:
                query = parts[0]
                query = (query * cosine + pltpu.roll(query, HD // 2, 1) * sine) * QSCALE
                q_to[q_rows, :] = query.astype(jnp.bfloat16)
            if 1 in parts:
                key = parts[1]
                key = key * cosine + pltpu.roll(key, HD // 2, 1) * sine
                kv_to[kv_rows, :HD] = key.astype(jnp.bfloat16)
                kv_to[kv_rows, HD:] = parts[2].astype(jnp.bfloat16)

    def keys_home(stage):
        for unit in units_of(stage, xpos):
            rows = rows_of(section * TOK + token_start(unit), HALF)
            send(
                kv_two.at[slot_rows(unit), :], kv_all.at[rows, :], rk_send, rk_recv.at[stage], twin
            )

    def queries_home(stage):
        for unit in units_of(stage, xpos):
            rows = rows_of(token_start(unit), HALF)
            send(q_two.at[slot_rows(unit), :], q_ref.at[rows, :], rq_send, rq_recv.at[stage], twin)

    def came_home(stage):
        count = len(units_of(stage, xtwin)) * HALF
        arrived(kv_all, count, rk_recv.at[stage])

    def batch(index):
        return units_of(index % STAGES, xpos if index < STAGES else xtwin)

    def kv_copy(region, start, size, send_sem, recv_sem, device):
        rows = rows_of(region * TOK + start, size)
        send(kv_all.at[rows, :], kv_all.at[rows, :], send_sem, recv_sem, device)

    def share(index):
        for unit in batch(index):
            start = token_start(unit)
            kv_copy(section, start, HALF, z_send, z_recv.at[0, index], z_up)
            kv_copy(section, start, HALF, z_send, z_recv.at[1, index], z_down)
            kv_copy(section, start, HALF, s_send, s_recv.at[index], partner)

    def relay_near(index):
        below, above = (section + SECTIONS - 2) % SECTIONS, (section + 2) % SECTIONS
        units = batch(index)
        arrived(kv_all, len(units) * HALF, z_recv.at[0, index])
        for unit in units:
            start = token_start(unit)
            kv_copy(below, start, UNIT, z_send, z_recv.at[2, index], z_up)
            kv_copy(below, start, HALF, s_send, s_recv.at[index], partner)
        arrived(kv_all, len(units) * HALF, z_recv.at[1, index])
        for unit in units:
            start = token_start(unit)
            kv_copy(above, start + UNIT, UNIT, z_send, z_recv.at[3, index], z_down)
            kv_copy(above, start, HALF, s_send, s_recv.at[index], partner)

    def relay_far(index):
        across = (section + 4) % SECTIONS
        units = batch(index)
        arrived(kv_all, len(units) * UNIT, z_recv.at[2, index])
        arrived(kv_all, len(units) * UNIT, z_recv.at[3, index])
        for unit in units:
            kv_copy(across, token_start(unit), HALF, s_send, s_recv.at[index], partner)

    core = section % 2
    depth = D // 2

    def twin_rows(part):
        return w_two.at[part, rows_of(core * depth, depth), :]

    for order in range(2):
        forward((ypos, xpos, order), near_recv.at[0, order], up, True)
        forward((ypos, xpos, 1 - order), near_recv.at[1, 1 - order], down, True)
        forward((ypos, xpos, order), side_recv.at[0, order], beside, True)
    own_weight.wait()
    for part in (1, 2, 0):
        send(
            w_ref.at[part, rows_of(core * depth, depth), :],
            twin_rows(part),
            v_send,
            v_recv.at[part],
            twin,
        )
    send(lists_here, lists.at[1], l_send, l_recv, mate)
    own_lists = pltpu.make_async_copy(lists_here, lists.at[0], l_own)
    own_lists.start()
    own_rows = pltpu.make_async_copy(
        shard, w_all.at[rows_of(head * HD, HD), :], w_own
    )
    own_rows.start()

    def weight_on(part):
        pltpu.make_async_copy(twin_rows(part), twin_rows(part), v_recv.at[part]).wait()
        send(twin_rows(part), twin_rows(part), vp_send, vp_recv.at[part], partner)

    def weight_in(part):
        pltpu.make_async_copy(twin_rows(part), twin_rows(part), vp_recv.at[part]).wait()

    def first_stage(stage):
        below, above, across = units_of(stage, xpos)
        arrived(x_all, HALF, near_recv.at[0, below[2]])
        if stage == 1:
            forward(below, far_recv.at[0], up)
        arrived(x_all, HALF, near_recv.at[1, above[2]])
        if stage == 1:
            forward(above, far_recv.at[1], down)
        arrived(x_all, HALF, side_recv.at[0, across[2]])
        forward(across, copy_recv.at[0, across[2]], up)
        forward(across, copy_recv.at[1, across[2]], down)
        project([stage], True)
        share(stage)

    parity = section // 2 % 2

    def w_rows(source, part, side):
        return rows_of(source * HD + core * W_HALF + side * 2 * W_PART + part * W_PART, W_PART)

    def line(part, step):
        if part == 0:
            return ypos * 4 + (xpos + step) % 4
        return ((ypos + step) % 4) * 4 + xpos

    def w_copy(source, part, stage, target):
        view = w_all.at[w_rows(source, part, parity), :]
        send(
            view,
            view,
            w_send,
            w_recv.at[part, stage],
            {"section": section, "head": target},
        )

    def w_near():
        own_rows.wait()
        for part in range(2):
            for step in range(1, 4):
                w_copy(head, part, 0, line(part, step))

    def last_stage(stage):
        for way in range(2):
            arrived(x_all, HALF, copy_recv.at[way, stage - 4])
        arrived(x_all, HALF, side_recv.at[1, stage - 4])
        if stage == 5:
            w_near()
        project([stage], True)
        share(stage)
        project([stage], False, (1, 2))
        keys_home(stage)

    def bring(stage):
        came_home(stage)
        share(STAGES + stage)

    project([0], True)
    share(0)
    first_stage(1)
    relay_near(0)
    for part in (1, 2):
        weight_on(part)
    for part in (1, 2):
        weight_in(part)
    project([0, 1], False, (1, 2))
    keys_home(0)
    keys_home(1)
    relay_far(0)
    first_stage(2)
    project([2], False, (1, 2))
    keys_home(2)
    weight_on(0)
    relay_near(1)
    bring(0)
    bring(1)
    for part, unit in enumerate(units_of(3, xpos)):
        arrived(x_all, HALF, far_recv.at[part])
        forward(unit, side_recv.at[1, part], beside)
    project([3], True)
    share(3)
    project([3], False, (1, 2))
    keys_home(3)
    bring(2)
    relay_near(2)
    relay_near(STAGES)
    relay_far(1)
    relay_near(STAGES + 1)
    weight_in(0)
    project([0, 1, 2, 3], False, (0,))
    for stage in range(4):
        queries_home(stage)
    relay_near(3)
    relay_near(STAGES + 2)
    bring(3)
    relay_far(2)
    relay_far(STAGES)
    last_stage(4)
    relay_far(STAGES + 1)
    relay_near(STAGES + 3)
    relay_far(3)
    relay_far(STAGES + 2)
    last_stage(5)
    project([4, 5], False, (0,))
    queries_home(4)
    queries_home(5)
    relay_near(4)
    bring(4)
    for part in range(2):
        arrived(w_all, 3 * W_PART, w_recv.at[part, 0])
        for step in range(1, 4):
            for other in range(4):
                w_copy(line(part, other), part, step, line(1 - part, step))
    relay_near(5)
    relay_far(STAGES + 3)
    relay_far(4)
    bring(5)
    for stage in range(STAGES):
        arrived(q_ref, len(units_of(stage, xtwin)) * HALF, rq_recv.at[stage])

    for block in range(MOVED):

        @pl.when(heavy & (block < moved))
        def _(block=block):
            send(
                q_ref.at[pl.ds(block * BLK, BLK), :],
                q_ref.at[pl.ds(TOK + block * BLK, BLK), :],
                m_send.at[block],
                m_recv.at[block],
                mate,
            )

    relay_near(STAGES + 4)
    relay_far(5)
    relay_near(STAGES + 5)
    relay_far(STAGES + 4)
    relay_far(STAGES + 5)
    for index in range(2 * STAGES):
        arrived(kv_all, 4 * HALF * len(batch(index)), s_recv.at[index])

    def w_group(part, step):
        if step == 0:
            return [line(part, other) for other in range(1, 4)]
        if part == 0:
            return [(ypos + 4 - step) % 4 * 4 + other for other in range(4)]
        return [other * 4 + (xpos + 4 - step) % 4 for other in range(4)]

    def w_to_partner(source, part, side):
        view = w_all.at[w_rows(source, part, side), :]
        send(view, view, wp_send, wp_recv, partner)

    def w_spread(step):
        for part in range(2):
            if step > 0:
                arrived(w_all, 4 * W_PART, w_recv.at[part, step])
            for source in w_group(part, step):
                view = w_all.at[w_rows(source, part, parity), :]
                send(view, view, w_send, wz_recv.at[part, step], z_down if part else z_up)
                w_to_partner(source, part, parity)

    def w_finish(step):
        for part in range(2):
            sources = w_group(part, step)
            arrived(w_all, len(sources) * W_PART, wz_recv.at[part, step])
            for source in sources:
                w_to_partner(source, part, 1 - parity)

    def copies_of(turn, own, phase):
        base = own % BLOCKS * BLK
        copies = []
        offset, index = 0, 0
        while offset < BLK:
            inside = (phase * BLK + offset) % PIECE
            size = min(PIECE - inside, BLK - offset)
            target = (base + offset) // PIECE
            source = o_ref.at[rows_of(turn * BLK + offset, size), :]
            into = mix.at[head, pl.ds(inside, size), :]
            here = (own // BLOCKS == section) & (target == head)
            copy = pltpu.make_async_remote_copy(
                src_ref=source,
                dst_ref=into,
                send_sem=a_send.at[turn, index],
                recv_sem=a_recv,
                device_id={"section": own // BLOCKS, "head": target},
                device_id_type=MESH,
            )
            copies.append((source, into, here, copy))
            offset, index = offset + size, index + 1
        return copies

    def deliver(turn, own):
        for phase in range(3):

            @pl.when(own % 3 == phase)
            def _(phase=phase):
                for source, into, here, copy in copies_of(turn, own, phase):

                    @pl.when(here)
                    def _(source=source, into=into):
                        pltpu.make_async_copy(source, into, a_recv).start()

                    @pl.when(jnp.logical_not(here))
                    def _(copy=copy):
                        copy.start()

    def delivered(turn, own):
        for phase in range(3):

            @pl.when(own % 3 == phase)
            def _(phase=phase):
                for _, _, here, copy in copies_of(turn, own, phase):

                    @pl.when(jnp.logical_not(here))
                    def _(copy=copy):
                        copy.wait_send()

    own_lists.wait()
    arrived_lists = pltpu.make_async_copy(lists.at[1], lists.at[1], l_recv)
    arrived_lists.wait()
    taken = jnp.where(heavy, 0, moved)
    given = moved - taken
    turns = BLOCKS + taken - given

    kept = BLOCKS - given

    def block_of(turn):
        away = turn >= kept
        here = given + (turn + head) % kept
        there = (jnp.maximum(turn - kept, 0) + head) % jnp.maximum(taken, 1)
        row = jnp.where(away, there, here)
        side = jnp.where(away, 1, 0)
        own = jnp.where(away, mate_section, section) * BLOCKS + row
        return own, side, row, row * BLK + side * TOK

    ones = jnp.ones((BLK, HD), jnp.bfloat16)

    def one_block(turn, carry):
        own, side, block, base = block_of(turn)
        base = pl.multiple_of(base, BLK)
        landing = pl.multiple_of(turn * BLK, BLK)

        @pl.when(turn >= kept)
        def _():
            arrived(q_ref, BLK, m_recv.at[block])

        others = (own * (KSEL - 1)) // (NBLK - 1)
        spare = others % GROUP

        def tiles(first, slots):
            sources = [lists[side, block, slot] for slot in slots]
            pairs = [
                (
                    kv_all[pl.ds(source * BLK, BLK), :HD],
                    jnp.concatenate([kv_all[pl.ds(source * BLK, BLK), HD:], ones], axis=1),
                )
                for source in sources
            ]
            for part in range(BLK // ROWS):
                rows = pl.ds(part * ROWS, ROWS)
                query = q_ref[pl.ds(pl.multiple_of(base + part * ROWS, ROWS), ROWS), :]
                keyed = list(pairs)
                if first:
                    seen = (part + 1) * ROWS
                    here = kv_all[pl.ds(own * BLK, seen), :]
                    keyed.append(
                        (here[:, :HD], jnp.concatenate([here[:, HD:], ones[:seen]], axis=1))
                    )
                scores = [
                    lax.dot_general(
                        query, keys, (((1,), (1,)), ((), ())), preferred_element_type=jnp.float32
                    )
                    for keys, _ in keyed
                ]
                if first:
                    row = lax.broadcasted_iota(jnp.int32, (ROWS, seen), 0) + part * ROWS
                    col = lax.broadcasted_iota(jnp.int32, (ROWS, seen), 1)
                    scores[-1] = jnp.where(col <= row, scores[-1], -jnp.inf)
                lanes = [
                    one[:, start : start + HD]
                    for one in scores
                    for start in range(0, one.shape[1], HD)
                ]
                peak = jnp.max(functools.reduce(jnp.maximum, lanes), axis=1, keepdims=True)
                if not first:
                    old = m_ref[rows, :1]
                    peak = jnp.maximum(peak, old)
                update = None
                for one, (_, values) in zip(scores, keyed):
                    weights = jnp.exp2(one - peak).astype(jnp.bfloat16)
                    term = jnp.dot(weights, values, preferred_element_type=jnp.float32)
                    update = term if update is None else update + term
                if first:
                    acc_ref[rows, :] = update
                else:
                    acc_ref[rows, :] = acc_ref[rows, :] * jnp.exp2(old - peak) + update
                m_ref[rows, :] = jnp.broadcast_to(peak, (ROWS, HD))

        for extra in range(GROUP):

            @pl.when(spare == extra)
            def _(extra=extra):
                tiles(True, [1 + slot for slot in range(extra)])

        def one_group(group, inner):
            first_slot = 1 + spare + group * GROUP
            tiles(False, [first_slot + slot for slot in range(GROUP)])
            return inner

        lax.fori_loop(0, others // GROUP, one_group, 0)
        for part in range(BLK // ROWS):
            rows = pl.ds(part * ROWS, ROWS)
            o_ref[pl.ds(pl.multiple_of(landing + part * ROWS, ROWS), ROWS), :] = (
                acc_ref[rows, :HD] / acc_ref[rows, HD:]
            ).astype(jnp.bfloat16)
        deliver(turn, own)

        @pl.when(turn == 0)
        def _():
            w_spread(1)
            w_spread(3)

        @pl.when(turn == (turns - 1) // 3)
        def _():
            w_spread(2)

        @pl.when(turn == turns - 2)
        def _():
            w_finish(0)

        return carry

    w_spread(0)
    lax.fori_loop(0, turns, one_block, 0)
    w_finish(1)
    w_finish(3)
    w_finish(2)
    arrived(w_all, (HEADS - 1) * W_HALF, wp_recv)
    pltpu.make_async_copy(mix, mix, a_recv).wait()

    mixed = jnp.concatenate([mix[source] for source in range(HEADS)], axis=1)

    def one_tile(tile, carry):
        columns = pl.ds(pl.multiple_of(tile * OUT_TILE, OUT_TILE), OUT_TILE)
        summed = jnp.dot(mixed, w_all[:, columns], preferred_element_type=jnp.float32)
        out_ref[:, columns] = (hidden[:, columns].astype(jnp.float32) + summed).astype(
            jnp.bfloat16
        )
        return carry

    lax.fori_loop(0, D // OUT_TILE, one_tile, 0)

    arrived(w_all, 60 * W_PART, w_send)
    arrived(w_all, (HEADS - 1) * W_HALF, wp_send)

    def sent(turn, carry):
        delivered(turn, block_of(turn)[0])
        return carry

    lax.fori_loop(0, turns, sent, 0)
    pltpu.make_async_copy(lists.at[1], lists.at[1], l_send).wait()
    for block in range(MOVED):

        @pl.when(heavy & (block < moved))
        def _(block=block):
            arrived(q_ref, BLK, m_send.at[block])

    arrived(x_all, 7 * PIECE, x_send)
    half_two = w_two.at[:, pl.ds(0, depth), :]
    pltpu.make_async_copy(half_two, half_two, v_send).wait()
    pltpu.make_async_copy(half_two, half_two, vp_send).wait()
    arrived(kv_all, TOK // 2, rk_send)
    arrived(q_ref, TOK // 2, rq_send)
    arrived(kv_all, 3 * TOK, z_send)
    arrived(kv_all, 4 * TOK, s_send)


def layer(lists, hidden, gain, weight, shard, tables):
    vmem = pl.BlockSpec(memory_space=pltpu.VMEM)
    here = pl.BlockSpec(memory_space=pl.ANY)
    dma = pltpu.SemaphoreType.DMA
    return pl.pallas_call(
        layer_kernel,
        out_shape=jax.ShapeDtypeStruct((PIECE, D), jnp.bfloat16),
        in_specs=[pl.BlockSpec(memory_space=pltpu.SMEM), here, vmem, here, here] + [vmem] * 4,
        out_specs=vmem,
        scratch_shapes=[
            pltpu.VMEM((PIECE, D), jnp.bfloat16),
            pltpu.VMEM((PIECE, D), jnp.bfloat16),
            pltpu.VMEM((3, D, HD), jnp.bfloat16),
            dma((2,)),
            pltpu.VMEM((TOK // 2, D), jnp.bfloat16),
            pltpu.VMEM((SECTIONS * TOK, 2 * HD), jnp.bfloat16),
            pltpu.VMEM((TOK + MOVED * BLK, HD), jnp.bfloat16),
            pltpu.VMEM((BLK, HD), jnp.float32),
            pltpu.VMEM((BLK, 2 * HD), jnp.float32),
            pltpu.VMEM((TOK + MOVED * BLK, HD), jnp.bfloat16),
            pltpu.VMEM((D, D), jnp.bfloat16),
            pltpu.VMEM((HEADS, PIECE, HD), jnp.bfloat16),
            pltpu.VMEM((3, D, HD), jnp.bfloat16),
            pltpu.VMEM((TOK // 2, HD), jnp.bfloat16),
            pltpu.VMEM((TOK // 2, 2 * HD), jnp.bfloat16),
            dma((2, 2)),
            dma((2,)),
            dma((2, 2)),
            dma((2, 2)),
            dma,
            dma,
            dma((3,)),
            dma,
            dma((3,)),
            dma,
            dma,
            dma((STAGES,)),
            dma((STAGES,)),
            dma,
            dma((4, 2 * STAGES)),
            dma,
            dma((2 * STAGES,)),
            dma,
            dma((2, 4)),
            dma((2, 4)),
            dma,
            dma,
            dma,
            dma((BLOCKS + MOVED, 4)),
            dma,
            pltpu.SMEM((2, BLOCKS, KSEL), jnp.int32),
            dma,
            dma,
            dma,
            dma((MOVED,)),
            dma((MOVED,)),
        ],
        compiler_params=pltpu.CompilerParams(
            collective_id=0, has_side_effects=True, vmem_limit_bytes=60 << 20
        ),
        name="layer",
    )(lists, hidden, gain, weight, shard, *tables)


def rotary_tables(positions):
    frequency = THETA ** (-2.0 * np.arange(HD // 2) / HD)
    angle = positions[:, None] * frequency[None, :]
    cosine, sine = np.cos(angle), np.sin(angle)
    return (
        np.concatenate([cosine, cosine], axis=1).astype(np.float32),
        np.concatenate([-sine, sine], axis=1).astype(np.float32),
    )


def local(hidden_in, norm_gain, w_qkv, w_out, block_lists):
    weight = jnp.transpose(w_qkv, (1, 0, 2))
    bases = rotary_tables(np.arange(SECTIONS * HEADS) * PIECE)
    steps = rotary_tables(np.arange(PIECE))
    gain = norm_gain.reshape(1, D)
    return layer(block_lists, hidden_in, gain, weight, w_out, bases + steps)


def solution(mesh):
    placed = (
        P(("section", "head"), None),
        P(),
        P(None, None, "head"),
        P("head", None),
        P("section", None),
    )
    return jax.shard_map(
        local, mesh=mesh, in_specs=placed, out_specs=P(("section", "head"), None), check_vma=False
    )
```

```python
import functools
import math

import jax
import jax.numpy as jnp
import numpy as np
from jax import lax
from jax.experimental import pallas as pl
from jax.experimental.pallas import tpu as pltpu
from jax.sharding import PartitionSpec as P

D = 2048
HD = 128
BLK = 512
KSEL = 12
NBLK = 48
SECTIONS = 8
HEADS = 16

EPS = 1e-05
THETA = 10000.0
QSCALE = math.log2(math.e) / math.sqrt(HD)
ROWS = 128
GROUP = 4

PIECE = 192
HALF = PIECE // 2
UNIT = HALF // 2
TOK = PIECE * HEADS
STAGES = 6
W_HALF = HD // 2
W_PART = W_HALF // 2
BLOCKS = TOK // BLK
MOVED = 3
OUT_TILE = 256
MESH = pl.DeviceIdType.MESH


def layer_kernel(
    lists_here, hidden_in, gain, w_in, shard, cos_b, sin_b, cos_r, sin_r, out_ref,
    hidden, xn, w_ref, in_sems,
    x_all, kv_all, q_ref, m_ref, acc_ref, o_ref, w_all, mix, w_two, q_two, kv_two,
    near_recv, far_recv, side_recv, copy_recv, x_send, v_send, v_recv, vp_send, vp_recv,
    rq_send, rk_send, rq_recv, rk_recv, z_send, z_recv, s_send, s_recv,
    w_send, w_recv, w_far, wp_send, wp_recv, w_own, a_send, a_recv,
    lists, l_send, l_recv, l_own, m_send, m_recv,
):
    section = lax.axis_index("section")
    head = lax.axis_index("head")
    ypos, xpos = head // 4, head % 4

    def at(across, along):
        return {"section": section, "head": (ypos + across) % 4 * 4 + along}

    xside = xpos + 1 - 2 * (xpos % 2)
    xtwin = (xpos + 3 + 2 * (xpos % 2)) % 4
    up, down, beside, twin = at(1, xpos), at(3, xpos), at(0, xside), at(0, xtwin)
    z_up = {"section": (section + 2) % SECTIONS, "head": head}
    z_down = {"section": (section + SECTIONS - 2) % SECTIONS, "head": head}
    partner = {"section": section + 1 - 2 * (section % 2), "head": head}
    mate_section = SECTIONS - 1 - section
    mate = {"section": mate_section, "head": head}
    heavy = section >= SECTIONS // 2
    moved = (jnp.maximum(section, mate_section) - 1) // 2

    own_hidden = pltpu.make_async_copy(hidden_in, hidden, in_sems.at[0])
    own_weight = pltpu.make_async_copy(w_in, w_ref, in_sems.at[1])
    own_hidden.start()
    own_weight.start()

    barrier = pltpu.get_barrier_semaphore()
    for device in (z_up, z_down, partner):
        pl.semaphore_signal(barrier, inc=1, device_id=device, device_id_type=MESH)

    def greet(step, carry):
        peer = {"section": section, "head": (head + step) % HEADS}
        pl.semaphore_signal(barrier, inc=1, device_id=peer, device_id_type=MESH)
        return carry

    lax.fori_loop(1, HEADS, greet, 0)

    def greet_mates(step, carry):
        peer = {"section": mate_section, "head": (head + step) % HEADS}
        pl.semaphore_signal(barrier, inc=1, device_id=peer, device_id_type=MESH)
        return carry

    lax.fori_loop(0, HEADS, greet_mates, 0)
    own_hidden.wait()
    resid = hidden[...].astype(jnp.float32)
    spread = jnp.mean(resid * resid, axis=1, keepdims=True)
    xn[...] = (resid * lax.rsqrt(spread + EPS) * gain[...]).astype(jnp.bfloat16)
    pl.semaphore_wait(barrier, 2 * HEADS + 2)

    def rows_of(start, size):
        return pl.ds(pl.multiple_of(start, 16), size)

    def send(source, target, send_sem, recv_sem, device):
        pltpu.make_async_remote_copy(
            src_ref=source,
            dst_ref=target,
            send_sem=send_sem,
            recv_sem=recv_sem,
            device_id=device,
            device_id_type=MESH,
        ).start()

    def arrived(ref, rows, sem):
        view = ref.at[pl.ds(0, rows), :]
        pltpu.make_async_copy(view, view, sem).wait()

    def units_of(stage, along):
        beyond = along + 1 - 2 * (along % 2)
        if stage == 0:
            places = ((0, along, 0), (0, along, 1))
        elif stage == 1:
            places = ((3, along, 0), (1, along, 1), (0, beyond, 0))
        elif stage == 2:
            places = ((3, along, 1), (1, along, 0), (0, beyond, 1))
        elif stage == 3:
            places = ((2, along, 0), (2, along, 1))
        else:
            part = stage - 4
            places = ((3, beyond, part), (1, beyond, part), (2, beyond, part))
        return [((ypos + across) % 4, column, part) for across, column, part in places]

    def slot_rows(unit):
        row, column, part = unit
        return rows_of((row * 2 + column % 2) * PIECE + part * HALF, HALF)

    def token_start(unit):
        row, column, part = unit
        return (row * 4 + column) * PIECE + part * HALF

    def tokens_of(stage):
        if stage == 0:
            return [xn[...]]
        return [x_all[slot_rows(unit), :] for unit in units_of(stage, xpos)]

    def forward(unit, recv_sem, device, own=False):
        rows = slot_rows(unit)
        part = unit[2]
        source = xn.at[pl.ds(part * HALF, HALF), :] if own else x_all.at[rows, :]
        send(source, x_all.at[rows, :], x_send, recv_sem, device)

    def project(stages, mine, wanted=(0, 1, 2)):
        tokens = [piece for stage in stages for piece in tokens_of(stage)]
        tokens = tokens[0] if len(tokens) == 1 else jnp.concatenate(tokens, axis=0)
        source = w_ref if mine else w_two
        weight = [source[part] for part in wanted]
        weight = weight[0] if len(weight) == 1 else jnp.concatenate(weight, axis=1)
        result = jnp.dot(tokens, weight, preferred_element_type=jnp.float32)
        units = [unit for stage in stages for unit in units_of(stage, xpos)]
        for index, unit in enumerate(units):
            row, column, half = unit
            part = result[index * HALF : (index + 1) * HALF]
            parts = {
                name: part[:, place * HD : (place + 1) * HD] for place, name in enumerate(wanted)
            }
            place = section * HEADS + row * 4 + column
            base_cos, base_sin = cos_b[pl.ds(place, 1), :], sin_b[pl.ds(place, 1), :]
            row_cos = cos_r[half * HALF : (half + 1) * HALF, :]
            row_sin = sin_r[half * HALF : (half + 1) * HALF, :]
            cosine = base_cos * row_cos - base_sin * row_sin
            sine = base_sin * row_cos + base_cos * row_sin
            start = token_start(unit)
            if mine:
                q_to, q_rows = q_ref, rows_of(start, HALF)
                kv_to, kv_rows = kv_all, rows_of(section * TOK + start, HALF)
            else:
                q_to, kv_to = q_two, kv_two
                q_rows = kv_rows = slot_rows(unit)
            if 0 in parts:
                query = parts[0]
                query = (query * cosine + pltpu.roll(query, HD // 2, 1) * sine) * QSCALE
                q_to[q_rows, :] = query.astype(jnp.bfloat16)
            if 1 in parts:
                key = parts[1]
                key = key * cosine + pltpu.roll(key, HD // 2, 1) * sine
                kv_to[kv_rows, :HD] = key.astype(jnp.bfloat16)
                kv_to[kv_rows, HD:] = parts[2].astype(jnp.bfloat16)

    def keys_home(stage):
        for unit in units_of(stage, xpos):
            rows = rows_of(section * TOK + token_start(unit), HALF)
            send(
                kv_two.at[slot_rows(unit), :], kv_all.at[rows, :], rk_send, rk_recv.at[stage], twin
            )

    def queries_home(stage):
        for unit in units_of(stage, xpos):
            rows = rows_of(token_start(unit), HALF)
            send(q_two.at[slot_rows(unit), :], q_ref.at[rows, :], rq_send, rq_recv.at[stage], twin)

    def came_home(stage):
        count = len(units_of(stage, xtwin)) * HALF
        arrived(kv_all, count, rk_recv.at[stage])

    def batch(index):
        return units_of(index % STAGES, xpos if index < STAGES else xtwin)

    def kv_copy(region, start, size, send_sem, recv_sem, device):
        rows = rows_of(region * TOK + start, size)
        send(kv_all.at[rows, :], kv_all.at[rows, :], send_sem, recv_sem, device)

    def share(index):
        for unit in batch(index):
            start = token_start(unit)
            kv_copy(section, start, HALF, z_send, z_recv.at[0, index], z_up)
            kv_copy(section, start, HALF, z_send, z_recv.at[1, index], z_down)
            kv_copy(section, start, HALF, s_send, s_recv.at[index], partner)

    def relay_near(index):
        below, above = (section + SECTIONS - 2) % SECTIONS, (section + 2) % SECTIONS
        units = batch(index)
        arrived(kv_all, len(units) * HALF, z_recv.at[0, index])
        for unit in units:
            start = token_start(unit)
            kv_copy(below, start, UNIT, z_send, z_recv.at[2, index], z_up)
            kv_copy(below, start, HALF, s_send, s_recv.at[index], partner)
        arrived(kv_all, len(units) * HALF, z_recv.at[1, index])
        for unit in units:
            start = token_start(unit)
            kv_copy(above, start + UNIT, UNIT, z_send, z_recv.at[3, index], z_down)
            kv_copy(above, start, HALF, s_send, s_recv.at[index], partner)

    def relay_far(index):
        across = (section + 4) % SECTIONS
        units = batch(index)
        arrived(kv_all, len(units) * UNIT, z_recv.at[2, index])
        arrived(kv_all, len(units) * UNIT, z_recv.at[3, index])
        for unit in units:
            kv_copy(across, token_start(unit), HALF, s_send, s_recv.at[index], partner)

    core = section % 2
    depth = D // 2

    def twin_rows(part):
        return w_two.at[part, rows_of(core * depth, depth), :]

    for order in range(2):
        forward((ypos, xpos, order), near_recv.at[0, order], up, True)
        forward((ypos, xpos, 1 - order), near_recv.at[1, 1 - order], down, True)
        forward((ypos, xpos, order), side_recv.at[0, order], beside, True)
    own_weight.wait()
    for part in (1, 2, 0):
        send(
            w_ref.at[part, rows_of(core * depth, depth), :],
            twin_rows(part),
            v_send,
            v_recv.at[part],
            twin,
        )
    send(lists_here, lists.at[1], l_send, l_recv, mate)
    own_lists = pltpu.make_async_copy(lists_here, lists.at[0], l_own)
    own_lists.start()
    own_rows = pltpu.make_async_copy(
        shard, w_all.at[rows_of(head * HD, HD), :], w_own
    )
    own_rows.start()

    def weight_on(part):
        pltpu.make_async_copy(twin_rows(part), twin_rows(part), v_recv.at[part]).wait()
        send(twin_rows(part), twin_rows(part), vp_send, vp_recv.at[part], partner)

    def weight_in(part):
        pltpu.make_async_copy(twin_rows(part), twin_rows(part), vp_recv.at[part]).wait()

    def first_stage(stage):
        below, above, across = units_of(stage, xpos)
        arrived(x_all, HALF, near_recv.at[0, below[2]])
        if stage == 1:
            forward(below, far_recv.at[0], up)
        arrived(x_all, HALF, near_recv.at[1, above[2]])
        if stage == 1:
            forward(above, far_recv.at[1], down)
        arrived(x_all, HALF, side_recv.at[0, across[2]])
        forward(across, copy_recv.at[0, across[2]], up)
        forward(across, copy_recv.at[1, across[2]], down)
        project([stage], True)
        share(stage)

    def w_rows(source, part, first, size):
        return rows_of(source * HD + core * W_HALF + part * W_PART + first, size)

    def line(part, step):
        if part == 0:
            return ypos * 4 + (xpos + step) % 4
        return ((ypos + step) % 4) * 4 + xpos

    def w_copy(source, part, sems, stage, way, target, first=0, size=W_PART):
        view = w_all.at[w_rows(source, part, first, size), :]
        sem = sems.at[part, stage, way]
        send(view, view, w_send, sem, {"section": section, "head": target})

    def w_line(part, stage, step):
        if stage == 0:
            return [line(part, step)]
        if part == 0:
            return [(ypos + step) % 4 * 4 + other for other in range(4)]
        return [other * 4 + (xpos + step) % 4 for other in range(4)]

    def w_begin(stage):
        for part in range(2):
            along = part if stage == 0 else 1 - part
            for source in w_line(part, stage, 0):
                w_copy(source, part, w_recv, stage, 0, line(along, 1))
                w_copy(source, part, w_recv, stage, 1, line(along, 3))

    def w_relay(stage):
        count = 1 if stage == 0 else 4
        for part in range(2):
            along = part if stage == 0 else 1 - part
            for way in range(2):
                arrived(w_all, count * W_PART, w_recv.at[part, stage, way])
                for source in w_line(part, stage, 3 - 2 * way):
                    first = way * (W_PART // 2)
                    target = line(along, 1 + 2 * way)
                    w_copy(source, part, w_far, stage, way, target, first, W_PART // 2)

    def w_complete(stage):
        count = 1 if stage == 0 else 4
        for part in range(2):
            for way in range(2):
                arrived(w_all, count * (W_PART // 2), w_far.at[part, stage, way])

    def w_to_partner(stage, steps):
        for part in range(2):
            for step in steps:
                for source in w_line(part, stage, step):
                    view = w_all.at[w_rows(source, part, 0, W_PART), :]
                    send(view, view, wp_send, wp_recv, partner)

    def last_stage(stage):
        for way in range(2):
            arrived(x_all, HALF, copy_recv.at[way, stage - 4])
        arrived(x_all, HALF, side_recv.at[1, stage - 4])
        if stage == 5:
            own_rows.wait()
            w_begin(0)
        project([stage], True)
        share(stage)
        project([stage], False, (1, 2))
        keys_home(stage)

    def bring(stage):
        came_home(stage)
        share(STAGES + stage)

    project([0], True)
    share(0)
    first_stage(1)
    relay_near(0)
    for part in (1, 2):
        weight_on(part)
    for part in (1, 2):
        weight_in(part)
    project([0, 1], False, (1, 2))
    keys_home(0)
    keys_home(1)
    relay_far(0)
    first_stage(2)
    project([2], False, (1, 2))
    keys_home(2)
    weight_on(0)
    relay_near(1)
    bring(0)
    bring(1)
    for part, unit in enumerate(units_of(3, xpos)):
        arrived(x_all, HALF, far_recv.at[part])
        forward(unit, side_recv.at[1, part], beside)
    project([3], True)
    share(3)
    project([3], False, (1, 2))
    keys_home(3)
    bring(2)
    relay_near(2)
    relay_near(STAGES)
    relay_far(1)
    relay_near(STAGES + 1)
    weight_in(0)
    project([0, 1, 2, 3], False, (0,))
    for stage in range(4):
        queries_home(stage)
    relay_near(3)
    relay_near(STAGES + 2)
    bring(3)
    relay_far(2)
    relay_far(STAGES)
    last_stage(4)
    relay_far(STAGES + 1)
    relay_near(STAGES + 3)
    relay_far(3)
    relay_far(STAGES + 2)
    last_stage(5)
    project([4, 5], False, (0,))
    queries_home(4)
    queries_home(5)
    w_relay(0)
    relay_near(4)
    bring(4)
    w_complete(0)
    w_begin(1)
    relay_near(5)
    relay_far(STAGES + 3)
    relay_far(4)
    bring(5)
    for stage in range(STAGES):
        arrived(q_ref, len(units_of(stage, xtwin)) * HALF, rq_recv.at[stage])

    for block in range(MOVED):

        @pl.when(heavy & (block < moved))
        def _(block=block):
            send(
                q_ref.at[pl.ds(block * BLK, BLK), :],
                q_ref.at[pl.ds(TOK + block * BLK, BLK), :],
                m_send.at[block],
                m_recv.at[block],
                mate,
            )

    relay_near(STAGES + 4)
    relay_far(5)
    relay_near(STAGES + 5)
    relay_far(STAGES + 4)
    relay_far(STAGES + 5)
    for index in range(2 * STAGES):
        arrived(kv_all, 4 * HALF * len(batch(index)), s_recv.at[index])

    def copies_of(turn, own, phase):
        base = own % BLOCKS * BLK
        copies = []
        offset, index = 0, 0
        while offset < BLK:
            inside = (phase * BLK + offset) % PIECE
            size = min(PIECE - inside, BLK - offset)
            target = (base + offset) // PIECE
            source = o_ref.at[rows_of(turn * BLK + offset, size), :]
            into = mix.at[head, pl.ds(inside, size), :]
            here = (own // BLOCKS == section) & (target == head)
            copy = pltpu.make_async_remote_copy(
                src_ref=source,
                dst_ref=into,
                send_sem=a_send.at[turn, index],
                recv_sem=a_recv,
                device_id={"section": own // BLOCKS, "head": target},
                device_id_type=MESH,
            )
            copies.append((source, into, here, copy))
            offset, index = offset + size, index + 1
        return copies

    def deliver(turn, own):
        for phase in range(3):

            @pl.when(own % 3 == phase)
            def _(phase=phase):
                for source, into, here, copy in copies_of(turn, own, phase):

                    @pl.when(here)
                    def _(source=source, into=into):
                        pltpu.make_async_copy(source, into, a_recv).start()

                    @pl.when(jnp.logical_not(here))
                    def _(copy=copy):
                        copy.start()

    def delivered(turn, own):
        for phase in range(3):

            @pl.when(own % 3 == phase)
            def _(phase=phase):
                for _, _, here, copy in copies_of(turn, own, phase):

                    @pl.when(jnp.logical_not(here))
                    def _(copy=copy):
                        copy.wait_send()

    own_lists.wait()
    arrived_lists = pltpu.make_async_copy(lists.at[1], lists.at[1], l_recv)
    arrived_lists.wait()
    taken = jnp.where(heavy, 0, moved)
    given = moved - taken
    turns = BLOCKS + taken - given

    kept = BLOCKS - given

    def block_of(turn):
        away = turn >= kept
        here = given + (turn + head) % kept
        there = (jnp.maximum(turn - kept, 0) + head) % jnp.maximum(taken, 1)
        row = jnp.where(away, there, here)
        side = jnp.where(away, 1, 0)
        own = jnp.where(away, mate_section, section) * BLOCKS + row
        return own, side, row, row * BLK + side * TOK

    ones = jnp.ones((BLK, HD), jnp.bfloat16)

    def one_block(turn, carry):
        own, side, block, base = block_of(turn)
        base = pl.multiple_of(base, BLK)
        landing = pl.multiple_of(turn * BLK, BLK)

        @pl.when(turn >= kept)
        def _():
            arrived(q_ref, BLK, m_recv.at[block])

        others = (own * (KSEL - 1)) // (NBLK - 1)
        spare = others % GROUP

        def tiles(first, slots):
            sources = [lists[side, block, slot] for slot in slots]
            pairs = [
                (
                    kv_all[pl.ds(source * BLK, BLK), :HD],
                    jnp.concatenate([kv_all[pl.ds(source * BLK, BLK), HD:], ones], axis=1),
                )
                for source in sources
            ]
            for part in range(BLK // ROWS):
                rows = pl.ds(part * ROWS, ROWS)
                query = q_ref[pl.ds(pl.multiple_of(base + part * ROWS, ROWS), ROWS), :]
                keyed = list(pairs)
                if first:
                    seen = (part + 1) * ROWS
                    here = kv_all[pl.ds(own * BLK, seen), :]
                    keyed.append(
                        (here[:, :HD], jnp.concatenate([here[:, HD:], ones[:seen]], axis=1))
                    )
                scores = [
                    lax.dot_general(
                        query, keys, (((1,), (1,)), ((), ())), preferred_element_type=jnp.float32
                    )
                    for keys, _ in keyed
                ]
                if first:
                    row = lax.broadcasted_iota(jnp.int32, (ROWS, seen), 0) + part * ROWS
                    col = lax.broadcasted_iota(jnp.int32, (ROWS, seen), 1)
                    scores[-1] = jnp.where(col <= row, scores[-1], -jnp.inf)
                lanes = [
                    one[:, start : start + HD]
                    for one in scores
                    for start in range(0, one.shape[1], HD)
                ]
                peak = jnp.max(functools.reduce(jnp.maximum, lanes), axis=1, keepdims=True)
                if not first:
                    old = m_ref[rows, :1]
                    peak = jnp.maximum(peak, old)
                update = None
                for one, (_, values) in zip(scores, keyed):
                    weights = jnp.exp2(one - peak).astype(jnp.bfloat16)
                    term = jnp.dot(weights, values, preferred_element_type=jnp.float32)
                    update = term if update is None else update + term
                if first:
                    acc_ref[rows, :] = update
                else:
                    acc_ref[rows, :] = acc_ref[rows, :] * jnp.exp2(old - peak) + update
                m_ref[rows, :] = jnp.broadcast_to(peak, (ROWS, HD))

        for extra in range(GROUP):

            @pl.when(spare == extra)
            def _(extra=extra):
                tiles(True, [1 + slot for slot in range(extra)])

        def one_group(group, inner):
            first_slot = 1 + spare + group * GROUP
            tiles(False, [first_slot + slot for slot in range(GROUP)])
            return inner

        lax.fori_loop(0, others // GROUP, one_group, 0)
        for part in range(BLK // ROWS):
            rows = pl.ds(part * ROWS, ROWS)
            o_ref[pl.ds(pl.multiple_of(landing + part * ROWS, ROWS), ROWS), :] = (
                acc_ref[rows, :HD] / acc_ref[rows, HD:]
            ).astype(jnp.bfloat16)
        deliver(turn, own)

        @pl.when(turn == (turns - 1) // 3)
        def _():
            w_relay(1)
            w_to_partner(0, (1, 2, 3))
            w_to_partner(1, (1, 3))

        @pl.when(turn == turns - 2)
        def _():
            w_complete(1)
            w_to_partner(1, (2,))

        return carry

    lax.fori_loop(0, turns, one_block, 0)
    arrived(w_all, (HEADS - 1) * W_HALF, wp_recv)
    pltpu.make_async_copy(mix, mix, a_recv).wait()

    mixed = jnp.concatenate([mix[source] for source in range(HEADS)], axis=1)

    def one_tile(tile, carry):
        columns = pl.ds(pl.multiple_of(tile * OUT_TILE, OUT_TILE), OUT_TILE)
        summed = jnp.dot(mixed, w_all[:, columns], preferred_element_type=jnp.float32)
        out_ref[:, columns] = (hidden[:, columns].astype(jnp.float32) + summed).astype(
            jnp.bfloat16
        )
        return carry

    lax.fori_loop(0, D // OUT_TILE, one_tile, 0)

    arrived(w_all, 30 * W_PART, w_send)
    arrived(w_all, (HEADS - 1) * W_HALF, wp_send)

    def sent(turn, carry):
        delivered(turn, block_of(turn)[0])
        return carry

    lax.fori_loop(0, turns, sent, 0)
    pltpu.make_async_copy(lists.at[1], lists.at[1], l_send).wait()
    for block in range(MOVED):

        @pl.when(heavy & (block < moved))
        def _(block=block):
            arrived(q_ref, BLK, m_send.at[block])

    arrived(x_all, 7 * PIECE, x_send)
    half_two = w_two.at[:, pl.ds(0, depth), :]
    pltpu.make_async_copy(half_two, half_two, v_send).wait()
    pltpu.make_async_copy(half_two, half_two, vp_send).wait()
    arrived(kv_all, TOK // 2, rk_send)
    arrived(q_ref, TOK // 2, rq_send)
    arrived(kv_all, 3 * TOK, z_send)
    arrived(kv_all, 4 * TOK, s_send)


def layer(lists, hidden, gain, weight, shard, tables):
    vmem = pl.BlockSpec(memory_space=pltpu.VMEM)
    here = pl.BlockSpec(memory_space=pl.ANY)
    dma = pltpu.SemaphoreType.DMA
    return pl.pallas_call(
        layer_kernel,
        out_shape=jax.ShapeDtypeStruct((PIECE, D), jnp.bfloat16),
        in_specs=[pl.BlockSpec(memory_space=pltpu.SMEM), here, vmem, here, here] + [vmem] * 4,
        out_specs=vmem,
        scratch_shapes=[
            pltpu.VMEM((PIECE, D), jnp.bfloat16),
            pltpu.VMEM((PIECE, D), jnp.bfloat16),
            pltpu.VMEM((3, D, HD), jnp.bfloat16),
            dma((2,)),
            pltpu.VMEM((TOK // 2, D), jnp.bfloat16),
            pltpu.VMEM((SECTIONS * TOK, 2 * HD), jnp.bfloat16),
            pltpu.VMEM((TOK + MOVED * BLK, HD), jnp.bfloat16),
            pltpu.VMEM((BLK, HD), jnp.float32),
            pltpu.VMEM((BLK, 2 * HD), jnp.float32),
            pltpu.VMEM((TOK + MOVED * BLK, HD), jnp.bfloat16),
            pltpu.VMEM((D, D), jnp.bfloat16),
            pltpu.VMEM((HEADS, PIECE, HD), jnp.bfloat16),
            pltpu.VMEM((3, D, HD), jnp.bfloat16),
            pltpu.VMEM((TOK // 2, HD), jnp.bfloat16),
            pltpu.VMEM((TOK // 2, 2 * HD), jnp.bfloat16),
            dma((2, 2)),
            dma((2,)),
            dma((2, 2)),
            dma((2, 2)),
            dma,
            dma,
            dma((3,)),
            dma,
            dma((3,)),
            dma,
            dma,
            dma((STAGES,)),
            dma((STAGES,)),
            dma,
            dma((4, 2 * STAGES)),
            dma,
            dma((2 * STAGES,)),
            dma,
            dma((2, 2, 2)),
            dma((2, 2, 2)),
            dma,
            dma,
            dma,
            dma((BLOCKS + MOVED, 4)),
            dma,
            pltpu.SMEM((2, BLOCKS, KSEL), jnp.int32),
            dma,
            dma,
            dma,
            dma((MOVED,)),
            dma((MOVED,)),
        ],
        compiler_params=pltpu.CompilerParams(
            collective_id=0, has_side_effects=True, vmem_limit_bytes=60 << 20
        ),
        name="layer",
    )(lists, hidden, gain, weight, shard, *tables)


def rotary_tables(positions):
    frequency = THETA ** (-2.0 * np.arange(HD // 2) / HD)
    angle = positions[:, None] * frequency[None, :]
    cosine, sine = np.cos(angle), np.sin(angle)
    return (
        np.concatenate([cosine, cosine], axis=1).astype(np.float32),
        np.concatenate([-sine, sine], axis=1).astype(np.float32),
    )


def local(hidden_in, norm_gain, w_qkv, w_out, block_lists):
    weight = jnp.transpose(w_qkv, (1, 0, 2))
    bases = rotary_tables(np.arange(SECTIONS * HEADS) * PIECE)
    steps = rotary_tables(np.arange(PIECE))
    gain = norm_gain.reshape(1, D)
    return layer(block_lists, hidden_in, gain, weight, w_out, bases + steps)


def solution(mesh):
    placed = (
        P(("section", "head"), None),
        P(),
        P(None, None, "head"),
        P("head", None),
        P("section", None),
    )
    return jax.shard_map(
        local, mesh=mesh, in_specs=placed, out_specs=P(("section", "head"), None), check_vma=False
    )
```

```python
import functools
import math

import jax
import jax.numpy as jnp
import numpy as np
from jax import lax
from jax.experimental import pallas as pl
from jax.experimental.pallas import tpu as pltpu
from jax.sharding import PartitionSpec as P

D = 2048
HD = 128
BLK = 512
KSEL = 12
NBLK = 48
SECTIONS = 8
HEADS = 16

EPS = 1e-05
THETA = 10000.0
QSCALE = math.log2(math.e) / math.sqrt(HD)
ROWS = 128
GROUP = 4

PIECE = 192
HALF = PIECE // 2
UNIT = HALF // 2
TOK = PIECE * HEADS
STAGES = 6
W_HALF = HD // 2
W_PART = W_HALF // 2
BLOCKS = TOK // BLK
MOVED = 3
AHEAD = 3
OUT_TILE = 256
MESH = pl.DeviceIdType.MESH


def layer_kernel(
    lists_here, hidden_in, gain, w_in, shard, cos_b, sin_b, cos_r, sin_r, out_ref,
    hidden, xn, w_ref, in_sems,
    x_all, kv_all, q_ref, m_ref, acc_ref, o_ref, w_all, mix, w_two, q_two, kv_two,
    near_recv, far_recv, side_recv, copy_recv, x_send, v_send, v_recv, vp_send, vp_recv,
    rq_send, rk_send, rq_recv, rk_recv, z_send, z_recv, s_send, s_recv,
    w_send, w_recv, w_far, wp_send, wp_recv, w_own, a_send, a_recv,
    lists, l_send, l_recv, l_own, m_send, m_recv,
):
    section = lax.axis_index("section")
    head = lax.axis_index("head")
    ypos, xpos = head // 4, head % 4

    def at(across, along):
        return {"section": section, "head": (ypos + across) % 4 * 4 + along}

    xside = xpos + 1 - 2 * (xpos % 2)
    xtwin = (xpos + 3 + 2 * (xpos % 2)) % 4
    up, down, beside, twin = at(1, xpos), at(3, xpos), at(0, xside), at(0, xtwin)
    z_up = {"section": (section + 2) % SECTIONS, "head": head}
    z_down = {"section": (section + SECTIONS - 2) % SECTIONS, "head": head}
    partner = {"section": section + 1 - 2 * (section % 2), "head": head}
    mate_section = SECTIONS - 1 - section
    mate = {"section": mate_section, "head": head}
    heavy = section >= SECTIONS // 2
    moved = (jnp.maximum(section, mate_section) - 1) // 2
    shift = 1 - jnp.maximum(section, mate_section) % 2


    own_hidden = pltpu.make_async_copy(hidden_in, hidden, in_sems.at[0])
    own_weight = pltpu.make_async_copy(w_in, w_ref, in_sems.at[1])
    own_hidden.start()
    own_weight.start()

    barrier = pltpu.get_barrier_semaphore()
    for device in (z_up, z_down, partner):
        pl.semaphore_signal(barrier, inc=1, device_id=device, device_id_type=MESH)

    def greet(step, carry):
        peer = {"section": section, "head": (head + step) % HEADS}
        pl.semaphore_signal(barrier, inc=1, device_id=peer, device_id_type=MESH)
        return carry

    lax.fori_loop(1, HEADS, greet, 0)

    def greet_mates(step, carry):
        peer = {"section": mate_section, "head": (head + step) % HEADS}
        pl.semaphore_signal(barrier, inc=1, device_id=peer, device_id_type=MESH)
        return carry

    lax.fori_loop(0, HEADS, greet_mates, 0)
    own_hidden.wait()
    resid = hidden[...].astype(jnp.float32)
    spread = jnp.mean(resid * resid, axis=1, keepdims=True)
    xn[...] = (resid * lax.rsqrt(spread + EPS) * gain[...]).astype(jnp.bfloat16)
    pl.semaphore_wait(barrier, 2 * HEADS + 2)

    def rows_of(start, size):
        return pl.ds(pl.multiple_of(start, 16), size)

    def send(source, target, send_sem, recv_sem, device):
        pltpu.make_async_remote_copy(
            src_ref=source,
            dst_ref=target,
            send_sem=send_sem,
            recv_sem=recv_sem,
            device_id=device,
            device_id_type=MESH,
        ).start()

    def arrived(ref, rows, sem):
        view = ref.at[pl.ds(0, rows), :]
        pltpu.make_async_copy(view, view, sem).wait()

    def units_of(stage, along):
        beyond = along + 1 - 2 * (along % 2)
        if stage == 0:
            places = ((0, along, 0), (0, along, 1))
        elif stage == 1:
            places = ((3, along, 0), (1, along, 1), (0, beyond, 0))
        elif stage == 2:
            places = ((3, along, 1), (1, along, 0), (0, beyond, 1))
        elif stage == 3:
            places = ((2, along, 0), (2, along, 1))
        else:
            part = stage - 4
            places = ((3, beyond, part), (1, beyond, part), (2, beyond, part))
        return [((ypos + across) % 4, column, part) for across, column, part in places]

    def slot_rows(unit):
        row, column, part = unit
        return rows_of((row * 2 + column % 2) * PIECE + part * HALF, HALF)

    def token_start(unit):
        row, column, part = unit
        return (row * 4 + column) * PIECE + part * HALF

    def tokens_of(stage):
        if stage == 0:
            return [xn[...]]
        return [x_all[slot_rows(unit), :] for unit in units_of(stage, xpos)]

    def forward(unit, recv_sem, device, own=False):
        rows = slot_rows(unit)
        part = unit[2]
        source = xn.at[pl.ds(part * HALF, HALF), :] if own else x_all.at[rows, :]
        send(source, x_all.at[rows, :], x_send, recv_sem, device)

    def project(stages, mine, wanted=(0, 1, 2)):
        tokens = [piece for stage in stages for piece in tokens_of(stage)]
        tokens = tokens[0] if len(tokens) == 1 else jnp.concatenate(tokens, axis=0)
        source = w_ref if mine else w_two
        weight = [source[part] for part in wanted]
        weight = weight[0] if len(weight) == 1 else jnp.concatenate(weight, axis=1)
        result = jnp.dot(tokens, weight, preferred_element_type=jnp.float32)
        units = [unit for stage in stages for unit in units_of(stage, xpos)]
        for index, unit in enumerate(units):
            row, column, half = unit
            part = result[index * HALF : (index + 1) * HALF]
            parts = {
                name: part[:, place * HD : (place + 1) * HD] for place, name in enumerate(wanted)
            }
            place = section * HEADS + row * 4 + column
            base_cos, base_sin = cos_b[pl.ds(place, 1), :], sin_b[pl.ds(place, 1), :]
            row_cos = cos_r[half * HALF : (half + 1) * HALF, :]
            row_sin = sin_r[half * HALF : (half + 1) * HALF, :]
            cosine = base_cos * row_cos - base_sin * row_sin
            sine = base_sin * row_cos + base_cos * row_sin
            start = token_start(unit)
            if mine:
                q_to, q_rows = q_ref, rows_of(start, HALF)
                kv_to, kv_rows = kv_all, rows_of(section * TOK + start, HALF)
            else:
                q_to, kv_to = q_two, kv_two
                q_rows = kv_rows = slot_rows(unit)
            if 0 in parts:
                query = parts[0]
                query = (query * cosine + pltpu.roll(query, HD // 2, 1) * sine) * QSCALE
                q_to[q_rows, :] = query.astype(jnp.bfloat16)
            if 1 in parts:
                key = parts[1]
                key = key * cosine + pltpu.roll(key, HD // 2, 1) * sine
                kv_to[kv_rows, :HD] = key.astype(jnp.bfloat16)
                kv_to[kv_rows, HD:] = parts[2].astype(jnp.bfloat16)

    def keys_home(stage):
        for unit in units_of(stage, xpos):
            rows = rows_of(section * TOK + token_start(unit), HALF)
            send(
                kv_two.at[slot_rows(unit), :], kv_all.at[rows, :], rk_send, rk_recv.at[stage], twin
            )

    def queries_home(stage):
        for unit in units_of(stage, xpos):
            rows = rows_of(token_start(unit), HALF)
            send(q_two.at[slot_rows(unit), :], q_ref.at[rows, :], rq_send, rq_recv.at[stage], twin)

    def came_home(stage):
        count = len(units_of(stage, xtwin)) * HALF
        arrived(kv_all, count, rk_recv.at[stage])

    def batch(index):
        return units_of(index % STAGES, xpos if index < STAGES else xtwin)

    def kv_copy(region, start, size, send_sem, recv_sem, device):
        rows = rows_of(region * TOK + start, size)
        send(kv_all.at[rows, :], kv_all.at[rows, :], send_sem, recv_sem, device)

    def share(index):
        for unit in batch(index):
            start = token_start(unit)
            kv_copy(section, start, HALF, z_send, z_recv.at[0, index], z_up)
            kv_copy(section, start, HALF, z_send, z_recv.at[1, index], z_down)
            kv_copy(section, start, HALF, s_send, s_recv.at[index], partner)

    def relay_near(index):
        below, above = (section + SECTIONS - 2) % SECTIONS, (section + 2) % SECTIONS
        units = batch(index)
        arrived(kv_all, len(units) * HALF, z_recv.at[0, index])
        for unit in units:
            start = token_start(unit)
            kv_copy(below, start, UNIT, z_send, z_recv.at[2, index], z_up)
            kv_copy(below, start, HALF, s_send, s_recv.at[index], partner)
        arrived(kv_all, len(units) * HALF, z_recv.at[1, index])
        for unit in units:
            start = token_start(unit)
            kv_copy(above, start + UNIT, UNIT, z_send, z_recv.at[3, index], z_down)
            kv_copy(above, start, HALF, s_send, s_recv.at[index], partner)

    def relay_far(index):
        across = (section + 4) % SECTIONS
        units = batch(index)
        arrived(kv_all, len(units) * UNIT, z_recv.at[2, index])
        arrived(kv_all, len(units) * UNIT, z_recv.at[3, index])
        for unit in units:
            kv_copy(across, token_start(unit), HALF, s_send, s_recv.at[index], partner)

    core = section % 2
    depth = D // 2

    def twin_rows(part):
        return w_two.at[part, rows_of(core * depth, depth), :]

    for order in range(2):
        forward((ypos, xpos, order), near_recv.at[0, order], up, True)
        forward((ypos, xpos, 1 - order), near_recv.at[1, 1 - order], down, True)
        forward((ypos, xpos, order), side_recv.at[0, order], beside, True)
    own_weight.wait()
    for part in (1, 2, 0):
        send(
            w_ref.at[part, rows_of(core * depth, depth), :],
            twin_rows(part),
            v_send,
            v_recv.at[part],
            twin,
        )
    send(lists_here, lists.at[1], l_send, l_recv, mate)
    own_lists = pltpu.make_async_copy(lists_here, lists.at[0], l_own)
    own_lists.start()
    own_rows = pltpu.make_async_copy(
        shard, w_all.at[rows_of(head * HD, HD), :], w_own
    )
    own_rows.start()

    def weight_on(part):
        pltpu.make_async_copy(twin_rows(part), twin_rows(part), v_recv.at[part]).wait()
        send(twin_rows(part), twin_rows(part), vp_send, vp_recv.at[part], partner)

    def weight_in(part):
        pltpu.make_async_copy(twin_rows(part), twin_rows(part), vp_recv.at[part]).wait()

    def first_stage(stage):
        below, above, across = units_of(stage, xpos)
        arrived(x_all, HALF, near_recv.at[0, below[2]])
        if stage == 1:
            forward(below, far_recv.at[0], up)
        arrived(x_all, HALF, near_recv.at[1, above[2]])
        if stage == 1:
            forward(above, far_recv.at[1], down)
        arrived(x_all, HALF, side_recv.at[0, across[2]])
        forward(across, copy_recv.at[0, across[2]], up)
        forward(across, copy_recv.at[1, across[2]], down)
        project([stage], True)
        share(stage)

    def w_rows(source, part, first, size):
        return rows_of(source * HD + core * W_HALF + part * W_PART + first, size)

    def line(part, step):
        if part == 0:
            return ypos * 4 + (xpos + step) % 4
        return ((ypos + step) % 4) * 4 + xpos

    def w_copy(source, part, sems, stage, way, target, first=0, size=W_PART):
        view = w_all.at[w_rows(source, part, first, size), :]
        sem = sems.at[part, stage, way]
        send(view, view, w_send, sem, {"section": section, "head": target})

    def w_line(part, stage, step):
        if stage == 0:
            return [line(part, step)]
        if part == 0:
            return [(ypos + step) % 4 * 4 + other for other in range(4)]
        return [other * 4 + (xpos + step) % 4 for other in range(4)]

    def w_begin(stage):
        for part in range(2):
            along = part if stage == 0 else 1 - part
            for source in w_line(part, stage, 0):
                w_copy(source, part, w_recv, stage, 0, line(along, 1))
                w_copy(source, part, w_recv, stage, 1, line(along, 3))

    def w_relay(stage):
        count = 1 if stage == 0 else 4
        for part in range(2):
            along = part if stage == 0 else 1 - part
            for way in range(2):
                arrived(w_all, count * W_PART, w_recv.at[part, stage, way])
                for source in w_line(part, stage, 3 - 2 * way):
                    first = way * (W_PART // 2)
                    target = line(along, 1 + 2 * way)
                    w_copy(source, part, w_far, stage, way, target, first, W_PART // 2)

    def w_complete(stage):
        count = 1 if stage == 0 else 4
        for part in range(2):
            for way in range(2):
                arrived(w_all, count * (W_PART // 2), w_far.at[part, stage, way])

    def w_to_partner(stage, steps):
        for part in range(2):
            for step in steps:
                for source in w_line(part, stage, step):
                    view = w_all.at[w_rows(source, part, 0, W_PART), :]
                    send(view, view, wp_send, wp_recv, partner)

    def last_stage(stage):
        for way in range(2):
            arrived(x_all, HALF, copy_recv.at[way, stage - 4])
        arrived(x_all, HALF, side_recv.at[1, stage - 4])
        if stage == 5:
            own_rows.wait()
            w_begin(0)
        project([stage], True)
        share(stage)
        project([stage], False, (1, 2))
        keys_home(stage)

    def bring(stage):
        came_home(stage)
        share(STAGES + stage)

    project([0], True)
    share(0)
    first_stage(1)
    relay_near(0)
    for part in (1, 2):
        weight_on(part)
    for part in (1, 2):
        weight_in(part)
    project([0, 1], False, (1, 2))
    keys_home(0)
    keys_home(1)
    relay_far(0)
    first_stage(2)
    project([2], False, (1, 2))
    keys_home(2)
    weight_on(0)
    relay_near(1)
    bring(0)
    bring(1)
    for part, unit in enumerate(units_of(3, xpos)):
        arrived(x_all, HALF, far_recv.at[part])
        forward(unit, side_recv.at[1, part], beside)
    project([3], True)
    share(3)
    project([3], False, (1, 2))
    keys_home(3)
    bring(2)
    relay_near(2)
    relay_near(STAGES)
    relay_far(1)
    relay_near(STAGES + 1)
    weight_in(0)
    project([0, 1, 2, 3], False, (0,))
    for stage in range(4):
        queries_home(stage)
    relay_near(3)
    relay_near(STAGES + 2)
    bring(3)
    relay_far(2)
    relay_far(STAGES)
    last_stage(4)
    relay_far(STAGES + 1)
    relay_near(STAGES + 3)
    relay_far(3)
    relay_far(STAGES + 2)
    last_stage(5)
    project([4, 5], False, (0,))
    queries_home(4)
    queries_home(5)
    w_relay(0)
    relay_near(4)
    bring(4)
    w_complete(0)
    w_begin(1)
    relay_near(5)
    relay_far(STAGES + 3)
    relay_far(4)
    bring(5)
    for stage in range(STAGES):
        arrived(q_ref, len(units_of(stage, xtwin)) * HALF, rq_recv.at[stage])

    for block in range(MOVED):

        @pl.when(heavy & (block < moved))
        def _(block=block):
            send(
                q_ref.at[rows_of((2 * block + shift) * BLK, BLK), :],
                q_ref.at[pl.ds(TOK + block * BLK, BLK), :],
                m_send.at[block],
                m_recv.at[block],
                mate,
            )

    relay_near(STAGES + 4)
    relay_far(5)
    relay_near(STAGES + 5)
    relay_far(STAGES + 4)
    relay_far(STAGES + 5)
    for index in range(2 * STAGES):
        arrived(kv_all, 4 * HALF * len(batch(index)), s_recv.at[index])

    def copies_of(turn, own, phase):
        base = own % BLOCKS * BLK
        copies = []
        offset, index = 0, 0
        while offset < BLK:
            inside = (phase * BLK + offset) % PIECE
            size = min(PIECE - inside, BLK - offset)
            target = (base + offset) // PIECE
            source = o_ref.at[rows_of(turn * BLK + offset, size), :]
            into = mix.at[head, pl.ds(inside, size), :]
            here = (own // BLOCKS == section) & (target == head)
            copy = pltpu.make_async_remote_copy(
                src_ref=source,
                dst_ref=into,
                send_sem=a_send.at[turn, index],
                recv_sem=a_recv,
                device_id={"section": own // BLOCKS, "head": target},
                device_id_type=MESH,
            )
            copies.append((source, into, here, copy))
            offset, index = offset + size, index + 1
        return copies

    def deliver(turn, own):
        for phase in range(3):

            @pl.when(own % 3 == phase)
            def _(phase=phase):
                for source, into, here, copy in copies_of(turn, own, phase):

                    @pl.when(here)
                    def _(source=source, into=into):
                        pltpu.make_async_copy(source, into, a_recv).start()

                    @pl.when(jnp.logical_not(here))
                    def _(copy=copy):
                        copy.start()

    def delivered(turn, own):
        for phase in range(3):

            @pl.when(own % 3 == phase)
            def _(phase=phase):
                for _, _, here, copy in copies_of(turn, own, phase):

                    @pl.when(jnp.logical_not(here))
                    def _(copy=copy):
                        copy.wait_send()

    own_lists.wait()
    arrived_lists = pltpu.make_async_copy(lists.at[1], lists.at[1], l_recv)
    arrived_lists.wait()
    taken = jnp.where(heavy, 0, moved)
    given = moved - taken
    turns = BLOCKS + taken - given

    kept = BLOCKS - given

    def block_of(turn):
        away = (turn >= AHEAD) & (turn < AHEAD + taken)
        place = jnp.where(turn < AHEAD, turn, turn - taken)
        place = (place + head) % kept
        here = jnp.where(place < given, 2 * place + 1 - shift, place + given)
        there = (jnp.maximum(turn - AHEAD, 0) + head) % jnp.maximum(taken, 1)
        row = jnp.where(away, 2 * there + shift, here)
        side = jnp.where(away, 1, 0)
        own = jnp.where(away, mate_section, section) * BLOCKS + row
        base = jnp.where(away, TOK + there * BLK, row * BLK)
        return own, side, row, base, away, there

    ones = jnp.ones((BLK, HD), jnp.bfloat16)

    def one_block(turn, carry):
        own, side, block, base, away, there = block_of(turn)
        base = pl.multiple_of(base, BLK)
        landing = pl.multiple_of(turn * BLK, BLK)

        @pl.when(away)
        def _():
            arrived(q_ref, BLK, m_recv.at[there])

        others = (own * (KSEL - 1)) // (NBLK - 1)
        spare = others % GROUP

        def tiles(first, slots):
            sources = [lists[side, block, slot] for slot in slots]
            pairs = [
                (
                    kv_all[pl.ds(source * BLK, BLK), :HD],
                    jnp.concatenate([kv_all[pl.ds(source * BLK, BLK), HD:], ones], axis=1),
                )
                for source in sources
            ]
            for part in range(BLK // ROWS):
                rows = pl.ds(part * ROWS, ROWS)
                query = q_ref[pl.ds(pl.multiple_of(base + part * ROWS, ROWS), ROWS), :]
                keyed = list(pairs)
                if first:
                    seen = (part + 1) * ROWS
                    here = kv_all[pl.ds(own * BLK, seen), :]
                    keyed.append(
                        (here[:, :HD], jnp.concatenate([here[:, HD:], ones[:seen]], axis=1))
                    )
                scores = [
                    lax.dot_general(
                        query, keys, (((1,), (1,)), ((), ())), preferred_element_type=jnp.float32
                    )
                    for keys, _ in keyed
                ]
                if first:
                    row = lax.broadcasted_iota(jnp.int32, (ROWS, seen), 0) + part * ROWS
                    col = lax.broadcasted_iota(jnp.int32, (ROWS, seen), 1)
                    scores[-1] = jnp.where(col <= row, scores[-1], -jnp.inf)
                lanes = [
                    one[:, start : start + HD]
                    for one in scores
                    for start in range(0, one.shape[1], HD)
                ]
                peak = jnp.max(functools.reduce(jnp.maximum, lanes), axis=1, keepdims=True)
                if not first:
                    old = m_ref[rows, :1]
                    peak = jnp.maximum(peak, old)
                update = None
                for one, (_, values) in zip(scores, keyed):
                    weights = jnp.exp2(one - peak).astype(jnp.bfloat16)
                    term = jnp.dot(weights, values, preferred_element_type=jnp.float32)
                    update = term if update is None else update + term
                if first:
                    acc_ref[rows, :] = update
                else:
                    acc_ref[rows, :] = acc_ref[rows, :] * jnp.exp2(old - peak) + update
                m_ref[rows, :] = jnp.broadcast_to(peak, (ROWS, HD))

        for extra in range(GROUP):

            @pl.when(spare == extra)
            def _(extra=extra):
                tiles(True, [1 + slot for slot in range(extra)])

        def one_group(group, inner):
            first_slot = 1 + spare + group * GROUP
            tiles(False, [first_slot + slot for slot in range(GROUP)])
            return inner

        lax.fori_loop(0, others // GROUP, one_group, 0)
        for part in range(BLK // ROWS):
            rows = pl.ds(part * ROWS, ROWS)
            o_ref[pl.ds(pl.multiple_of(landing + part * ROWS, ROWS), ROWS), :] = (
                acc_ref[rows, :HD] / acc_ref[rows, HD:]
            ).astype(jnp.bfloat16)
        deliver(turn, own)

        @pl.when(turn == (turns - 1) // 3)
        def _():
            w_relay(1)
            w_to_partner(0, (1, 2, 3))
            w_to_partner(1, (1, 3))

        @pl.when(turn == turns - 2)
        def _():
            w_complete(1)
            w_to_partner(1, (2,))

        return carry

    lax.fori_loop(0, turns, one_block, 0)
    arrived(w_all, (HEADS - 1) * W_HALF, wp_recv)
    pltpu.make_async_copy(mix, mix, a_recv).wait()

    mixed = jnp.concatenate([mix[source] for source in range(HEADS)], axis=1)

    def one_tile(tile, carry):
        columns = pl.ds(pl.multiple_of(tile * OUT_TILE, OUT_TILE), OUT_TILE)
        summed = jnp.dot(mixed, w_all[:, columns], preferred_element_type=jnp.float32)
        out_ref[:, columns] = (hidden[:, columns].astype(jnp.float32) + summed).astype(
            jnp.bfloat16
        )
        return carry

    lax.fori_loop(0, D // OUT_TILE, one_tile, 0)

    arrived(w_all, 30 * W_PART, w_send)
    arrived(w_all, (HEADS - 1) * W_HALF, wp_send)

    def sent(turn, carry):
        delivered(turn, block_of(turn)[0])
        return carry

    lax.fori_loop(0, turns, sent, 0)
    pltpu.make_async_copy(lists.at[1], lists.at[1], l_send).wait()
    for block in range(MOVED):

        @pl.when(heavy & (block < moved))
        def _(block=block):
            arrived(q_ref, BLK, m_send.at[block])

    arrived(x_all, 7 * PIECE, x_send)
    half_two = w_two.at[:, pl.ds(0, depth), :]
    pltpu.make_async_copy(half_two, half_two, v_send).wait()
    pltpu.make_async_copy(half_two, half_two, vp_send).wait()
    arrived(kv_all, TOK // 2, rk_send)
    arrived(q_ref, TOK // 2, rq_send)
    arrived(kv_all, 3 * TOK, z_send)
    arrived(kv_all, 4 * TOK, s_send)


def layer(lists, hidden, gain, weight, shard, tables):
    vmem = pl.BlockSpec(memory_space=pltpu.VMEM)
    here = pl.BlockSpec(memory_space=pl.ANY)
    dma = pltpu.SemaphoreType.DMA
    return pl.pallas_call(
        layer_kernel,
        out_shape=jax.ShapeDtypeStruct((PIECE, D), jnp.bfloat16),
        in_specs=[pl.BlockSpec(memory_space=pltpu.SMEM), here, vmem, here, here] + [vmem] * 4,
        out_specs=vmem,
        scratch_shapes=[
            pltpu.VMEM((PIECE, D), jnp.bfloat16),
            pltpu.VMEM((PIECE, D), jnp.bfloat16),
            pltpu.VMEM((3, D, HD), jnp.bfloat16),
            dma((2,)),
            pltpu.VMEM((TOK // 2, D), jnp.bfloat16),
            pltpu.VMEM((SECTIONS * TOK, 2 * HD), jnp.bfloat16),
            pltpu.VMEM((TOK + MOVED * BLK, HD), jnp.bfloat16),
            pltpu.VMEM((BLK, HD), jnp.float32),
            pltpu.VMEM((BLK, 2 * HD), jnp.float32),
            pltpu.VMEM((TOK + MOVED * BLK, HD), jnp.bfloat16),
            pltpu.VMEM((D, D), jnp.bfloat16),
            pltpu.VMEM((HEADS, PIECE, HD), jnp.bfloat16),
            pltpu.VMEM((3, D, HD), jnp.bfloat16),
            pltpu.VMEM((TOK // 2, HD), jnp.bfloat16),
            pltpu.VMEM((TOK // 2, 2 * HD), jnp.bfloat16),
            dma((2, 2)),
            dma((2,)),
            dma((2, 2)),
            dma((2, 2)),
            dma,
            dma,
            dma((3,)),
            dma,
            dma((3,)),
            dma,
            dma,
            dma((STAGES,)),
            dma((STAGES,)),
            dma,
            dma((4, 2 * STAGES)),
            dma,
            dma((2 * STAGES,)),
            dma,
            dma((2, 2, 2)),
            dma((2, 2, 2)),
            dma,
            dma,
            dma,
            dma((BLOCKS + MOVED, 4)),
            dma,
            pltpu.SMEM((2, BLOCKS, KSEL), jnp.int32),
            dma,
            dma,
            dma,
            dma((MOVED,)),
            dma((MOVED,)),
        ],
        compiler_params=pltpu.CompilerParams(
            collective_id=0, has_side_effects=True, vmem_limit_bytes=60 << 20
        ),
        name="layer",
    )(lists, hidden, gain, weight, shard, *tables)


def rotary_tables(positions):
    frequency = THETA ** (-2.0 * np.arange(HD // 2) / HD)
    angle = positions[:, None] * frequency[None, :]
    cosine, sine = np.cos(angle), np.sin(angle)
    return (
        np.concatenate([cosine, cosine], axis=1).astype(np.float32),
        np.concatenate([-sine, sine], axis=1).astype(np.float32),
    )


def local(hidden_in, norm_gain, w_qkv, w_out, block_lists):
    weight = jnp.transpose(w_qkv, (1, 0, 2))
    bases = rotary_tables(np.arange(SECTIONS * HEADS) * PIECE)
    steps = rotary_tables(np.arange(PIECE))
    gain = norm_gain.reshape(1, D)
    return layer(block_lists, hidden_in, gain, weight, w_out, bases + steps)


def solution(mesh):
    placed = (
        P(("section", "head"), None),
        P(),
        P(None, None, "head"),
        P("head", None),
        P("section", None),
    )
    return jax.shard_map(
        local, mesh=mesh, in_specs=placed, out_specs=P(("section", "head"), None), check_vma=False
    )
```

```python
import functools
import math

import jax
import jax.numpy as jnp
import numpy as np
from jax import lax
from jax.experimental import pallas as pl
from jax.experimental.pallas import tpu as pltpu
from jax.sharding import PartitionSpec as P

D = 2048
HD = 128
BLK = 512
KSEL = 12
NBLK = 48
SECTIONS = 8
HEADS = 16

EPS = 1e-05
THETA = 10000.0
QSCALE = math.log2(math.e) / math.sqrt(HD)
ROWS = 128
GROUP = 4

PIECE = 192
HALF = PIECE // 2
UNIT = HALF // 2
TOK = PIECE * HEADS
STAGES = 6
W_HALF = HD // 2
W_PART = W_HALF // 2
BLOCKS = TOK // BLK
MOVED = 3
AHEAD = 3
OUT_TILE = 512
MESH = pl.DeviceIdType.MESH


def layer_kernel(
    lists_here, hidden_in, gain, w_in, shard, cos_b, sin_b, cos_r, sin_r, out_ref,
    hidden, xn, w_ref, in_sems,
    x_all, kv_all, q_ref, m_ref, acc_ref, o_ref, w_all, mix, w_two, q_two, kv_two,
    near_recv, far_recv, side_recv, copy_recv, x_send, v_send, v_recv, vp_send, vp_recv,
    rq_send, rk_send, rq_recv, rk_recv, z_send, z_recv, s_send, s_recv,
    w_send, w_recv, w_far, wp_send, wp_recv, w_own, a_send, a_recv,
    lists, l_send, l_recv, l_own, m_send, m_recv,
):
    section = lax.axis_index("section")
    head = lax.axis_index("head")
    ypos, xpos = head // 4, head % 4

    def at(across, along):
        return {"section": section, "head": (ypos + across) % 4 * 4 + along}

    xside = xpos + 1 - 2 * (xpos % 2)
    xtwin = (xpos + 3 + 2 * (xpos % 2)) % 4
    up, down, beside, twin = at(1, xpos), at(3, xpos), at(0, xside), at(0, xtwin)
    z_up = {"section": (section + 2) % SECTIONS, "head": head}
    z_down = {"section": (section + SECTIONS - 2) % SECTIONS, "head": head}
    partner = {"section": section + 1 - 2 * (section % 2), "head": head}
    mate_section = SECTIONS - 1 - section
    mate = {"section": mate_section, "head": head}
    heavy = section >= SECTIONS // 2
    moved = (jnp.maximum(section, mate_section) - 2) // 2
    shift = 1 - jnp.maximum(section, mate_section) % 2


    own_hidden = pltpu.make_async_copy(hidden_in, hidden, in_sems.at[0])
    own_weight = pltpu.make_async_copy(w_in, w_ref, in_sems.at[1])
    own_hidden.start()
    own_weight.start()

    barrier = pltpu.get_barrier_semaphore()
    for device in (z_up, z_down, partner):
        pl.semaphore_signal(barrier, inc=1, device_id=device, device_id_type=MESH)

    def greet(step, carry):
        peer = {"section": section, "head": (head + step) % HEADS}
        pl.semaphore_signal(barrier, inc=1, device_id=peer, device_id_type=MESH)
        return carry

    lax.fori_loop(1, HEADS, greet, 0)

    def greet_mates(step, carry):
        peer = {"section": mate_section, "head": (head + step) % HEADS}
        pl.semaphore_signal(barrier, inc=1, device_id=peer, device_id_type=MESH)
        return carry

    lax.fori_loop(0, HEADS, greet_mates, 0)
    own_hidden.wait()
    resid = hidden[...].astype(jnp.float32)
    spread = jnp.mean(resid * resid, axis=1, keepdims=True)
    xn[...] = (resid * lax.rsqrt(spread + EPS) * gain[...]).astype(jnp.bfloat16)
    pl.semaphore_wait(barrier, 2 * HEADS + 2)

    def rows_of(start, size):
        return pl.ds(pl.multiple_of(start, 16), size)

    def send(source, target, send_sem, recv_sem, device):
        pltpu.make_async_remote_copy(
            src_ref=source,
            dst_ref=target,
            send_sem=send_sem,
            recv_sem=recv_sem,
            device_id=device,
            device_id_type=MESH,
        ).start()

    def arrived(ref, rows, sem):
        view = ref.at[pl.ds(0, rows), :]
        pltpu.make_async_copy(view, view, sem).wait()

    def units_of(stage, along):
        beyond = along + 1 - 2 * (along % 2)
        if stage == 0:
            places = ((0, along, 0), (0, along, 1))
        elif stage == 1:
            places = ((3, along, 0), (1, along, 1), (0, beyond, 0))
        elif stage == 2:
            places = ((3, along, 1), (1, along, 0), (0, beyond, 1))
        elif stage == 3:
            places = ((2, along, 0), (2, along, 1))
        else:
            part = stage - 4
            places = ((3, beyond, part), (1, beyond, part), (2, beyond, part))
        return [((ypos + across) % 4, column, part) for across, column, part in places]

    def slot_rows(unit):
        row, column, part = unit
        return rows_of((row * 2 + column % 2) * PIECE + part * HALF, HALF)

    def token_start(unit):
        row, column, part = unit
        return (row * 4 + column) * PIECE + part * HALF

    def tokens_of(stage):
        if stage == 0:
            return [xn[...]]
        return [x_all[slot_rows(unit), :] for unit in units_of(stage, xpos)]

    def forward(unit, recv_sem, device, own=False):
        rows = slot_rows(unit)
        part = unit[2]
        source = xn.at[pl.ds(part * HALF, HALF), :] if own else x_all.at[rows, :]
        send(source, x_all.at[rows, :], x_send, recv_sem, device)

    def project(stages, mine, wanted=(0, 1, 2)):
        tokens = [piece for stage in stages for piece in tokens_of(stage)]
        tokens = tokens[0] if len(tokens) == 1 else jnp.concatenate(tokens, axis=0)
        source = w_ref if mine else w_two
        weight = [source[part] for part in wanted]
        weight = weight[0] if len(weight) == 1 else jnp.concatenate(weight, axis=1)
        result = jnp.dot(tokens, weight, preferred_element_type=jnp.float32)
        units = [unit for stage in stages for unit in units_of(stage, xpos)]
        for index, unit in enumerate(units):
            row, column, half = unit
            part = result[index * HALF : (index + 1) * HALF]
            parts = {
                name: part[:, place * HD : (place + 1) * HD] for place, name in enumerate(wanted)
            }
            place = section * HEADS + row * 4 + column
            base_cos, base_sin = cos_b[pl.ds(place, 1), :], sin_b[pl.ds(place, 1), :]
            row_cos = cos_r[half * HALF : (half + 1) * HALF, :]
            row_sin = sin_r[half * HALF : (half + 1) * HALF, :]
            cosine = base_cos * row_cos - base_sin * row_sin
            sine = base_sin * row_cos + base_cos * row_sin
            start = token_start(unit)
            if mine:
                q_to, q_rows = q_ref, rows_of(start, HALF)
                kv_to, kv_rows = kv_all, rows_of(section * TOK + start, HALF)
            else:
                q_to, kv_to = q_two, kv_two
                q_rows = kv_rows = slot_rows(unit)
            if 0 in parts:
                query = parts[0]
                query = (query * cosine + pltpu.roll(query, HD // 2, 1) * sine) * QSCALE
                q_to[q_rows, :] = query.astype(jnp.bfloat16)
            if 1 in parts:
                key = parts[1]
                key = key * cosine + pltpu.roll(key, HD // 2, 1) * sine
                kv_to[kv_rows, :HD] = key.astype(jnp.bfloat16)
                kv_to[kv_rows, HD:] = parts[2].astype(jnp.bfloat16)

    def keys_home(stage):
        for unit in units_of(stage, xpos):
            rows = rows_of(section * TOK + token_start(unit), HALF)
            send(
                kv_two.at[slot_rows(unit), :], kv_all.at[rows, :], rk_send, rk_recv.at[stage], twin
            )

    def queries_home(stage):
        for unit in units_of(stage, xpos):
            rows = rows_of(token_start(unit), HALF)
            send(q_two.at[slot_rows(unit), :], q_ref.at[rows, :], rq_send, rq_recv.at[stage], twin)

    def came_home(stage):
        count = len(units_of(stage, xtwin)) * HALF
        arrived(kv_all, count, rk_recv.at[stage])

    def batch(index):
        return units_of(index % STAGES, xpos if index < STAGES else xtwin)

    def kv_copy(region, start, size, send_sem, recv_sem, device):
        rows = rows_of(region * TOK + start, size)
        send(kv_all.at[rows, :], kv_all.at[rows, :], send_sem, recv_sem, device)

    def share(index):
        for unit in batch(index):
            start = token_start(unit)
            kv_copy(section, start, HALF, z_send, z_recv.at[0, index], z_up)
            kv_copy(section, start, HALF, z_send, z_recv.at[1, index], z_down)
            kv_copy(section, start, HALF, s_send, s_recv.at[index], partner)

    def relay_near(index):
        below, above = (section + SECTIONS - 2) % SECTIONS, (section + 2) % SECTIONS
        units = batch(index)
        arrived(kv_all, len(units) * HALF, z_recv.at[0, index])
        for unit in units:
            start = token_start(unit)
            kv_copy(below, start, UNIT, z_send, z_recv.at[2, index], z_up)
            kv_copy(below, start, HALF, s_send, s_recv.at[index], partner)
        arrived(kv_all, len(units) * HALF, z_recv.at[1, index])
        for unit in units:
            start = token_start(unit)
            kv_copy(above, start + UNIT, UNIT, z_send, z_recv.at[3, index], z_down)
            kv_copy(above, start, HALF, s_send, s_recv.at[index], partner)

    def relay_far(index):
        across = (section + 4) % SECTIONS
        units = batch(index)
        arrived(kv_all, len(units) * UNIT, z_recv.at[2, index])
        arrived(kv_all, len(units) * UNIT, z_recv.at[3, index])
        for unit in units:
            kv_copy(across, token_start(unit), HALF, s_send, s_recv.at[index], partner)

    core = section % 2
    depth = D // 2

    def twin_rows(part):
        return w_two.at[part, rows_of(core * depth, depth), :]

    for order in range(2):
        forward((ypos, xpos, order), near_recv.at[0, order], up, True)
        forward((ypos, xpos, 1 - order), near_recv.at[1, 1 - order], down, True)
        forward((ypos, xpos, order), side_recv.at[0, order], beside, True)
    own_weight.wait()
    for part in (1, 2, 0):
        send(
            w_ref.at[part, rows_of(core * depth, depth), :],
            twin_rows(part),
            v_send,
            v_recv.at[part],
            twin,
        )
    send(lists_here, lists.at[1], l_send, l_recv, mate)
    own_lists = pltpu.make_async_copy(lists_here, lists.at[0], l_own)
    own_lists.start()
    own_rows = pltpu.make_async_copy(
        shard, w_all.at[rows_of(head * HD, HD), :], w_own
    )
    own_rows.start()

    def weight_on(part):
        pltpu.make_async_copy(twin_rows(part), twin_rows(part), v_recv.at[part]).wait()
        send(twin_rows(part), twin_rows(part), vp_send, vp_recv.at[part], partner)

    def weight_in(part):
        pltpu.make_async_copy(twin_rows(part), twin_rows(part), vp_recv.at[part]).wait()

    def first_stage(stage):
        below, above, across = units_of(stage, xpos)
        arrived(x_all, HALF, near_recv.at[0, below[2]])
        if stage == 1:
            forward(below, far_recv.at[0], up)
        arrived(x_all, HALF, near_recv.at[1, above[2]])
        if stage == 1:
            forward(above, far_recv.at[1], down)
        arrived(x_all, HALF, side_recv.at[0, across[2]])
        forward(across, copy_recv.at[0, across[2]], up)
        forward(across, copy_recv.at[1, across[2]], down)
        project([stage], True)
        share(stage)

    def w_rows(source, part, first, size):
        return rows_of(source * HD + core * W_HALF + part * W_PART + first, size)

    def line(part, step):
        if part == 0:
            return ypos * 4 + (xpos + step) % 4
        return ((ypos + step) % 4) * 4 + xpos

    def w_copy(source, part, sems, stage, way, target, first=0, size=W_PART):
        view = w_all.at[w_rows(source, part, first, size), :]
        sem = sems.at[part, stage, way]
        send(view, view, w_send, sem, {"section": section, "head": target})

    def w_line(part, stage, step):
        if stage == 0:
            return [line(part, step)]
        if part == 0:
            return [(ypos + step) % 4 * 4 + other for other in range(4)]
        return [other * 4 + (xpos + step) % 4 for other in range(4)]

    def w_begin(stage):
        for part in range(2):
            along = part if stage == 0 else 1 - part
            for source in w_line(part, stage, 0):
                w_copy(source, part, w_recv, stage, 0, line(along, 1))
                w_copy(source, part, w_recv, stage, 1, line(along, 3))

    def w_relay(stage):
        count = 1 if stage == 0 else 4
        for part in range(2):
            along = part if stage == 0 else 1 - part
            for way in range(2):
                arrived(w_all, count * W_PART, w_recv.at[part, stage, way])
                for source in w_line(part, stage, 3 - 2 * way):
                    first = way * (W_PART // 2)
                    target = line(along, 1 + 2 * way)
                    w_copy(source, part, w_far, stage, way, target, first, W_PART // 2)

    def w_complete(stage):
        count = 1 if stage == 0 else 4
        for part in range(2):
            for way in range(2):
                arrived(w_all, count * (W_PART // 2), w_far.at[part, stage, way])

    def w_to_partner(stage, steps):
        for part in range(2):
            for step in steps:
                for source in w_line(part, stage, step):
                    view = w_all.at[w_rows(source, part, 0, W_PART), :]
                    send(view, view, wp_send, wp_recv, partner)

    def last_stage(stage):
        for way in range(2):
            arrived(x_all, HALF, copy_recv.at[way, stage - 4])
        arrived(x_all, HALF, side_recv.at[1, stage - 4])
        if stage == 5:
            own_rows.wait()
            w_begin(0)
        project([stage], True)
        share(stage)
        project([stage], False, (1, 2))
        keys_home(stage)

    def bring(stage):
        came_home(stage)
        share(STAGES + stage)

    project([0], True)
    share(0)
    first_stage(1)
    relay_near(0)
    for part in (1, 2):
        weight_on(part)
    for part in (1, 2):
        weight_in(part)
    project([0, 1], False, (1, 2))
    keys_home(0)
    keys_home(1)
    relay_far(0)
    first_stage(2)
    project([2], False, (1, 2))
    keys_home(2)
    weight_on(0)
    relay_near(1)
    bring(0)
    bring(1)
    for part, unit in enumerate(units_of(3, xpos)):
        arrived(x_all, HALF, far_recv.at[part])
        forward(unit, side_recv.at[1, part], beside)
    project([3], True)
    share(3)
    project([3], False, (1, 2))
    keys_home(3)
    bring(2)
    relay_near(2)
    relay_near(STAGES)
    relay_far(1)
    relay_near(STAGES + 1)
    weight_in(0)
    project([0, 1, 2, 3], False, (0,))
    for stage in range(4):
        queries_home(stage)
    relay_near(3)
    relay_near(STAGES + 2)
    bring(3)
    relay_far(2)
    relay_far(STAGES)
    last_stage(4)
    relay_far(STAGES + 1)
    relay_near(STAGES + 3)
    relay_far(3)
    relay_far(STAGES + 2)
    last_stage(5)
    project([4, 5], False, (0,))
    queries_home(4)
    queries_home(5)
    w_relay(0)
    relay_near(4)
    bring(4)
    w_complete(0)
    w_begin(1)
    relay_near(5)
    relay_far(STAGES + 3)
    relay_far(4)
    bring(5)
    for stage in range(STAGES):
        arrived(q_ref, len(units_of(stage, xtwin)) * HALF, rq_recv.at[stage])

    for block in range(MOVED):

        @pl.when(heavy & (block < moved))
        def _(block=block):
            send(
                q_ref.at[rows_of((2 * block + shift) * BLK, BLK), :],
                q_ref.at[pl.ds(TOK + block * BLK, BLK), :],
                m_send.at[block],
                m_recv.at[block],
                mate,
            )

    relay_near(STAGES + 4)
    relay_far(5)
    relay_near(STAGES + 5)
    relay_far(STAGES + 4)
    relay_far(STAGES + 5)
    for index in range(2 * STAGES):
        arrived(kv_all, 4 * HALF * len(batch(index)), s_recv.at[index])

    def copies_of(turn, own, phase):
        base = own % BLOCKS * BLK
        copies = []
        offset, index = 0, 0
        while offset < BLK:
            inside = (phase * BLK + offset) % PIECE
            size = min(PIECE - inside, BLK - offset)
            target = (base + offset) // PIECE
            source = o_ref.at[rows_of(turn * BLK + offset, size), :]
            into = mix.at[head, pl.ds(inside, size), :]
            here = (own // BLOCKS == section) & (target == head)
            copy = pltpu.make_async_remote_copy(
                src_ref=source,
                dst_ref=into,
                send_sem=a_send.at[turn, index],
                recv_sem=a_recv,
                device_id={"section": own // BLOCKS, "head": target},
                device_id_type=MESH,
            )
            copies.append((source, into, here, copy))
            offset, index = offset + size, index + 1
        return copies

    def deliver(turn, own):
        for phase in range(3):

            @pl.when(own % 3 == phase)
            def _(phase=phase):
                for source, into, here, copy in copies_of(turn, own, phase):

                    @pl.when(here)
                    def _(source=source, into=into):
                        pltpu.make_async_copy(source, into, a_recv).start()

                    @pl.when(jnp.logical_not(here))
                    def _(copy=copy):
                        copy.start()

    def delivered(turn, own):
        for phase in range(3):

            @pl.when(own % 3 == phase)
            def _(phase=phase):
                for _, _, here, copy in copies_of(turn, own, phase):

                    @pl.when(jnp.logical_not(here))
                    def _(copy=copy):
                        copy.wait_send()

    own_lists.wait()
    arrived_lists = pltpu.make_async_copy(lists.at[1], lists.at[1], l_recv)
    arrived_lists.wait()
    taken = jnp.where(heavy, 0, moved)
    given = moved - taken
    turns = BLOCKS + taken - given

    kept = BLOCKS - given

    def block_of(turn):
        away = (turn >= AHEAD) & (turn < AHEAD + taken)
        place = jnp.where(turn < AHEAD, turn, turn - taken)
        place = (place + head) % kept
        here = jnp.where(place < given, 2 * place + 1 - shift, place + given)
        there = (jnp.maximum(turn - AHEAD, 0) + head) % jnp.maximum(taken, 1)
        row = jnp.where(away, 2 * there + shift, here)
        side = jnp.where(away, 1, 0)
        own = jnp.where(away, mate_section, section) * BLOCKS + row
        base = jnp.where(away, TOK + there * BLK, row * BLK)
        return own, side, row, base, away, there

    ones = jnp.ones((BLK, HD), jnp.bfloat16)

    def one_block(turn, carry):
        own, side, block, base, away, there = block_of(turn)
        base = pl.multiple_of(base, BLK)
        landing = pl.multiple_of(turn * BLK, BLK)

        @pl.when(away)
        def _():
            arrived(q_ref, BLK, m_recv.at[there])

        others = (own * (KSEL - 1)) // (NBLK - 1)
        spare = others % GROUP

        def tiles(first, slots):
            sources = [lists[side, block, slot] for slot in slots]
            pairs = [
                (
                    kv_all[pl.ds(source * BLK, BLK), :HD],
                    jnp.concatenate([kv_all[pl.ds(source * BLK, BLK), HD:], ones], axis=1),
                )
                for source in sources
            ]
            for part in range(BLK // ROWS):
                rows = pl.ds(part * ROWS, ROWS)
                query = q_ref[pl.ds(pl.multiple_of(base + part * ROWS, ROWS), ROWS), :]
                keyed = list(pairs)
                if first:
                    seen = (part + 1) * ROWS
                    here = kv_all[pl.ds(own * BLK, seen), :]
                    keyed.append(
                        (here[:, :HD], jnp.concatenate([here[:, HD:], ones[:seen]], axis=1))
                    )
                scores = [
                    lax.dot_general(
                        query, keys, (((1,), (1,)), ((), ())), preferred_element_type=jnp.float32
                    )
                    for keys, _ in keyed
                ]
                if first:
                    row = lax.broadcasted_iota(jnp.int32, (ROWS, seen), 0) + part * ROWS
                    col = lax.broadcasted_iota(jnp.int32, (ROWS, seen), 1)
                    scores[-1] = jnp.where(col <= row, scores[-1], -jnp.inf)
                lanes = [
                    one[:, start : start + HD]
                    for one in scores
                    for start in range(0, one.shape[1], HD)
                ]
                peak = jnp.max(functools.reduce(jnp.maximum, lanes), axis=1, keepdims=True)
                if not first:
                    old = m_ref[rows, :1]
                    peak = jnp.maximum(peak, old)
                update = None
                for one, (_, values) in zip(scores, keyed):
                    weights = jnp.exp2(one - peak).astype(jnp.bfloat16)
                    term = jnp.dot(weights, values, preferred_element_type=jnp.float32)
                    update = term if update is None else update + term
                if first:
                    acc_ref[rows, :] = update
                else:
                    acc_ref[rows, :] = acc_ref[rows, :] * jnp.exp2(old - peak) + update
                m_ref[rows, :] = jnp.broadcast_to(peak, (ROWS, HD))

        for extra in range(GROUP):

            @pl.when(spare == extra)
            def _(extra=extra):
                tiles(True, [1 + slot for slot in range(extra)])

        def one_group(group, inner):
            first_slot = 1 + spare + group * GROUP
            tiles(False, [first_slot + slot for slot in range(GROUP)])
            return inner

        lax.fori_loop(0, others // GROUP, one_group, 0)
        for part in range(BLK // ROWS):
            rows = pl.ds(part * ROWS, ROWS)
            o_ref[pl.ds(pl.multiple_of(landing + part * ROWS, ROWS), ROWS), :] = (
                acc_ref[rows, :HD] / acc_ref[rows, HD:]
            ).astype(jnp.bfloat16)
        deliver(turn, own)

        @pl.when(turn == (turns - 1) // 3)
        def _():
            w_relay(1)
            w_to_partner(0, (1, 2, 3))
            w_to_partner(1, (1, 3))

        @pl.when(turn == turns - 2)
        def _():
            w_complete(1)
            w_to_partner(1, (2,))

        return carry

    lax.fori_loop(0, turns, one_block, 0)
    arrived(w_all, (HEADS - 1) * W_HALF, wp_recv)
    pltpu.make_async_copy(mix, mix, a_recv).wait()

    mixed = jnp.concatenate([mix[source] for source in range(HEADS)], axis=1)

    def one_tile(tile, carry):
        columns = pl.ds(pl.multiple_of(tile * OUT_TILE, OUT_TILE), OUT_TILE)
        summed = jnp.dot(mixed, w_all[:, columns], preferred_element_type=jnp.float32)
        out_ref[:, columns] = (hidden[:, columns].astype(jnp.float32) + summed).astype(
            jnp.bfloat16
        )
        return carry

    lax.fori_loop(0, D // OUT_TILE, one_tile, 0)

    arrived(w_all, 30 * W_PART, w_send)
    arrived(w_all, (HEADS - 1) * W_HALF, wp_send)

    def sent(turn, carry):
        delivered(turn, block_of(turn)[0])
        return carry

    lax.fori_loop(0, turns, sent, 0)
    pltpu.make_async_copy(lists.at[1], lists.at[1], l_send).wait()
    for block in range(MOVED):

        @pl.when(heavy & (block < moved))
        def _(block=block):
            arrived(q_ref, BLK, m_send.at[block])

    arrived(x_all, 7 * PIECE, x_send)
    half_two = w_two.at[:, pl.ds(0, depth), :]
    pltpu.make_async_copy(half_two, half_two, v_send).wait()
    pltpu.make_async_copy(half_two, half_two, vp_send).wait()
    arrived(kv_all, TOK // 2, rk_send)
    arrived(q_ref, TOK // 2, rq_send)
    arrived(kv_all, 3 * TOK, z_send)
    arrived(kv_all, 4 * TOK, s_send)


def layer(lists, hidden, gain, weight, shard, tables):
    vmem = pl.BlockSpec(memory_space=pltpu.VMEM)
    here = pl.BlockSpec(memory_space=pl.ANY)
    dma = pltpu.SemaphoreType.DMA
    return pl.pallas_call(
        layer_kernel,
        out_shape=jax.ShapeDtypeStruct((PIECE, D), jnp.bfloat16),
        in_specs=[pl.BlockSpec(memory_space=pltpu.SMEM), here, vmem, here, here] + [vmem] * 4,
        out_specs=vmem,
        scratch_shapes=[
            pltpu.VMEM((PIECE, D), jnp.bfloat16),
            pltpu.VMEM((PIECE, D), jnp.bfloat16),
            pltpu.VMEM((3, D, HD), jnp.bfloat16),
            dma((2,)),
            pltpu.VMEM((TOK // 2, D), jnp.bfloat16),
            pltpu.VMEM((SECTIONS * TOK, 2 * HD), jnp.bfloat16),
            pltpu.VMEM((TOK + MOVED * BLK, HD), jnp.bfloat16),
            pltpu.VMEM((BLK, HD), jnp.float32),
            pltpu.VMEM((BLK, 2 * HD), jnp.float32),
            pltpu.VMEM((TOK + MOVED * BLK, HD), jnp.bfloat16),
            pltpu.VMEM((D, D), jnp.bfloat16),
            pltpu.VMEM((HEADS, PIECE, HD), jnp.bfloat16),
            pltpu.VMEM((3, D, HD), jnp.bfloat16),
            pltpu.VMEM((TOK // 2, HD), jnp.bfloat16),
            pltpu.VMEM((TOK // 2, 2 * HD), jnp.bfloat16),
            dma((2, 2)),
            dma((2,)),
            dma((2, 2)),
            dma((2, 2)),
            dma,
            dma,
            dma((3,)),
            dma,
            dma((3,)),
            dma,
            dma,
            dma((STAGES,)),
            dma((STAGES,)),
            dma,
            dma((4, 2 * STAGES)),
            dma,
            dma((2 * STAGES,)),
            dma,
            dma((2, 2, 2)),
            dma((2, 2, 2)),
            dma,
            dma,
            dma,
            dma((BLOCKS + MOVED, 4)),
            dma,
            pltpu.SMEM((2, BLOCKS, KSEL), jnp.int32),
            dma,
            dma,
            dma,
            dma((MOVED,)),
            dma((MOVED,)),
        ],
        compiler_params=pltpu.CompilerParams(
            collective_id=0, has_side_effects=True, vmem_limit_bytes=60 << 20
        ),
        name="layer",
    )(lists, hidden, gain, weight, shard, *tables)


def rotary_tables(positions):
    frequency = THETA ** (-2.0 * np.arange(HD // 2) / HD)
    angle = positions[:, None] * frequency[None, :]
    cosine, sine = np.cos(angle), np.sin(angle)
    return (
        np.concatenate([cosine, cosine], axis=1).astype(np.float32),
        np.concatenate([-sine, sine], axis=1).astype(np.float32),
    )


def local(hidden_in, norm_gain, w_qkv, w_out, block_lists):
    weight = jnp.transpose(w_qkv, (1, 0, 2))
    bases = rotary_tables(np.arange(SECTIONS * HEADS) * PIECE)
    steps = rotary_tables(np.arange(PIECE))
    gain = norm_gain.reshape(1, D)
    return layer(block_lists, hidden_in, gain, weight, w_out, bases + steps)


def solution(mesh):
    placed = (
        P(("section", "head"), None),
        P(),
        P(None, None, "head"),
        P("head", None),
        P("section", None),
    )
    return jax.shard_map(
        local, mesh=mesh, in_specs=placed, out_specs=P(("section", "head"), None), check_vma=False
    )
```
